32 devices in a mesh: dp: 8 (over z, y), chan: 4 (over x, core).
Axes of the slice: x: 2, y: 2, z: 4, core: 2. Of those that a mesh axis runs over, the one named last changes fastest.
Arguments:
- block_input: bfloat16 [112, 6, 4, 128], P(None, None, None, 'dp'), may hold values from -8 to 8
- cotangent: bfloat16 [112, 6, 4, 128], P('chan', None, None, 'dp'), may hold values from -8 to 8
- expand_weight: float32 [672, 112], P('chan'), may hold values from -0.5 to 0.5
- expand_weight_first: float32 [672, 112], P('chan'), may hold values from -0.0024414062 to 0.0024414062
- expand_weight_second: float32 [672, 112], P('chan'), may hold values from 2.6e-09 to 1e-08
- expand_gains: float32 [2, 672], P(None, 'chan'), may hold values from 0.5 to 1.5
- expand_gains_first: float32 [2, 672], P(None, 'chan'), may hold values from -0.0024414062 to 0.0024414062
- expand_gains_second: float32 [2, 672], P(None, 'chan'), may hold values from 2.6e-09 to 1e-08
- depth_weight: float32 [25, 672], P(None, 'chan'), may hold values from -1.25 to 1.25
- depth_weight_first: float32 [25, 672], P(None, 'chan'), may hold values from -0.001953125 to 0.001953125
- depth_weight_second: float32 [25, 672], P(None, 'chan'), may hold values from 2e-09 to 7.8e-09
- depth_gains: float32 [2, 672], P(None, 'chan'), may hold values from 0.5 to 1.5
- depth_gains_first: float32 [2, 672], P(None, 'chan'), may hold values from -0.0024414062 to 0.0024414062
- depth_gains_second: float32 [2, 672], P(None, 'chan'), may hold values from 2.6e-09 to 1e-08
- squeeze_weight: float32 [28, 672], P(None, 'chan'), may hold values from -0.25 to 0.25
- squeeze_weight_first: float32 [28, 672], P(None, 'chan'), may hold values from -0.0007324219 to 0.0007324219
- squeeze_weight_second: float32 [28, 672], P(None, 'chan'), may hold values from 2.3e-10 to 9.2e-10
- squeeze_bias: float32 [28], replicated, may hold values from -3 to 3
- squeeze_bias_first: float32 [28], replicated, may hold values from -0.0024414062 to 0.0024414062
- squeeze_bias_second: float32 [28], replicated, may hold values from 2.6e-09 to 1e-08
- excite_weight: float32 [28, 672], P(None, 'chan'), may hold values from -1 to 1
- excite_weight_first: float32 [28, 672], P(None, 'chan'), may hold values from -0.00024414062 to 0.00024414062
- excite_weight_second: float32 [28, 672], P(None, 'chan'), may hold values from 2.6e-11 to 1e-10
- excite_bias: float32 [672], P('chan'), may hold values from -3 to 3
- excite_bias_first: float32 [672], P('chan'), may hold values from -0.0008544922 to 0.0008544922
- excite_bias_second: float32 [672], P('chan'), may hold values from 2.9e-10 to 1.2e-09
- project_weight: float32 [112, 672], P(None, 'chan'), may hold values from -0.25 to 0.25
- project_weight_first: float32 [112, 672], P(None, 'chan'), may hold values from -0.0048828125 to 0.0048828125
- project_weight_second: float32 [112, 672], P(None, 'chan'), may hold values from 1e-08 to 4.1e-08
- project_gains: float32 [2, 112], P(None, 'chan'), may hold values from 0.5 to 1.5
- project_gains_first: float32 [2, 112], P(None, 'chan'), may hold values from -0.0048828125 to 0.0048828125
- project_gains_second: float32 [2, 112], P(None, 'chan'), may hold values from 1e-08 to 4.1e-08
Outputs:
- block_output: bfloat16 [112, 6, 4, 128], P('chan', None, None, 'dp')
- input_grad: float32 [112, 6, 4, 128], P('chan', None, None, 'dp')
- expand_weight_new: float32 [672, 112], P('chan')
- expand_weight_first_new: float32 [672, 112], P('chan')
- expand_weight_second_new: float32 [672, 112], P('chan')
- expand_gains_new: float32 [2, 672], P(None, 'chan')
- expand_gains_first_new: float32 [2, 672], P(None, 'chan')
- expand_gains_second_new: float32 [2, 672], P(None, 'chan')
- depth_weight_new: float32 [25, 672], P(None, 'chan')
- depth_weight_first_new: float32 [25, 672], P(None, 'chan')
- depth_weight_second_new: float32 [25, 672], P(None, 'chan')
- depth_gains_new: float32 [2, 672], P(None, 'chan')
- depth_gains_first_new: float32 [2, 672], P(None, 'chan')
- depth_gains_second_new: float32 [2, 672], P(None, 'chan')
- squeeze_weight_new: float32 [28, 672], P(None, 'chan')
- squeeze_weight_first_new: float32 [28, 672], P(None, 'chan')
- squeeze_weight_second_new: float32 [28, 672], P(None, 'chan')
- squeeze_bias_new: float32 [28], replicated
- squeeze_bias_first_new: float32 [28], replicated
- squeeze_bias_second_new: float32 [28], replicated
- excite_weight_new: float32 [28, 672], P(None, 'chan')
- excite_weight_first_new: float32 [28, 672], P(None, 'chan')
- excite_weight_second_new: float32 [28, 672], P(None, 'chan')
- excite_bias_new: float32 [672], P('chan')
- excite_bias_first_new: float32 [672], P('chan')
- excite_bias_second_new: float32 [672], P('chan')
- project_weight_new: float32 [112, 672], P(None, 'chan')
- project_weight_first_new: float32 [112, 672], P(None, 'chan')
- project_weight_second_new: float32 [112, 672], P(None, 'chan')
- project_gains_new: float32 [2, 112], P(None, 'chan')
- project_gains_first_new: float32 [2, 112], P(None, 'chan')
- project_gains_second_new: float32 [2, 112], P(None, 'chan')
- grad_norm: float32 [], replicated
The draws below stay inside these ranges and needn't reach their ends.
All inputs are finite; a program needn't handle non-finite values.
Results may differ from the reference program's by a relative error of at most 0.0067.
Values may be sent and summed in bfloat16 or wider, within the bound.
No kernel may reach another device: no remote copies, remote signals or barrier semaphores. Data moves between devices by JAX's collectives and lax.ppermute only.
A program may use at most 64 MiB of HBM per device.

```python
import math
import jax
import jax.numpy as jnp
from jax import lax

C_IN = 112
EXP = 672
SE = 28
KS = 5
HT = 6
WD = 4
STEP = 10
SEGS = 128


def rising_field(key, channel_count):
    base_key = jax.random.fold_in(key, 0)
    field_shape = (channel_count, HT, WD, SEGS)
    fraction = jnp.arange(SEGS, dtype=jnp.float32) / max(SEGS - 1, 1)
    ramping = 0.5 + fraction
    values = jnp.clip(jax.random.normal(base_key, field_shape, jnp.float32), -4.0, 4.0)
    return values * ramping


def draw_block_input(key, part):
    return rising_field(jax.random.fold_in(key, 11), C_IN).astype(jnp.bfloat16)


def draw_cotangent(key, part):
    return rising_field(jax.random.fold_in(key, 23), C_IN).astype(jnp.bfloat16)


def shard_levels(own_key, shape, cuts, smallest, top_value):
    gain = 1.0
    for axis_at, shards_of in cuts:
        heights = jax.random.uniform(jax.random.fold_in(jax.random.fold_in(own_key, 6), axis_at), (shards_of,), jnp.float32, smallest / len(cuts), top_value / len(cuts))
        gain = gain * jnp.repeat(jnp.exp(heights), shape[axis_at] // shards_of).reshape((-1,) + (1,) * (len(shape) - 1 - axis_at))
    return gain


def normal_values(stream_key, shape, spread, bound, shards=(), held_as=jnp.bfloat16):
    level = shard_levels(stream_key, shape, shards, -0.22, 0.18) if shards else 1.0
    values = jax.random.normal(stream_key, shape, jnp.float32) * spread * level
    return jnp.minimum(jnp.maximum(values, -bound), bound).astype(held_as)


def setup_inputs(seed: int = 0) -> dict:
    streams_of = jax.random.split(jax.random.key(seed), 33)
    return {
        "block_input": draw_block_input(jax.random.fold_in(streams_of[32], 71), 0),
        "cotangent": draw_cotangent(jax.random.fold_in(streams_of[32], 71), 0),
        "expand_weight": normal_values(streams_of[2], (EXP, C_IN), C_IN ** -0.5, 0.5, ((0, 4),), jnp.float32),
        "expand_weight_first": normal_values(streams_of[3], (EXP, C_IN), (1.8e-4), 0.0024414062, ((0, 4),), jnp.float32),
        "expand_weight_second": jnp.clip(jnp.exp(math.log(9.99999993922529e-09) - 1.34707364 * jax.random.uniform(streams_of[4], (EXP, C_IN), jnp.float32) ** shard_levels(streams_of[4], (EXP, C_IN), ((0, 4),), -0.2, 0.2)), 2.5999999930803597e-09, 9.99999993922529e-09),
        "expand_gains": jnp.clip(0.5 + 1.0 * jax.random.uniform(streams_of[5], (2, EXP), jnp.float32) ** shard_levels(streams_of[5], (2, EXP), ((1, 4),), -0.2, 0.2), 0.5, 1.5),
        "expand_gains_first": normal_values(streams_of[6], (2, EXP), (1.8e-4), 0.0024414062, ((1, 4),), jnp.float32),
        "expand_gains_second": jnp.clip(jnp.exp(math.log(9.99999993922529e-09) - 1.34707364 * jax.random.uniform(streams_of[7], (2, EXP), jnp.float32) ** shard_levels(streams_of[7], (2, EXP), ((1, 4),), -0.2, 0.2)), 2.5999999930803597e-09, 9.99999993922529e-09),
        "depth_weight": normal_values(streams_of[8], (KS * KS, EXP), (KS * KS) ** -0.5, 1.25, ((1, 4),), jnp.float32),
        "depth_weight_first": normal_values(streams_of[9], (KS * KS, EXP), (1.5e-4), 0.001953125, ((1, 4),), jnp.float32),
        "depth_weight_second": jnp.clip(jnp.exp(math.log(7.799999757196474e-09) - 1.3609766 * jax.random.uniform(streams_of[10], (KS * KS, EXP), jnp.float32) ** shard_levels(streams_of[10], (KS * KS, EXP), ((1, 4),), -0.2, 0.2)), 1.999999943436137e-09, 7.799999757196474e-09),
        "depth_gains": jnp.clip(0.5 + 1.0 * jax.random.uniform(streams_of[11], (2, EXP), jnp.float32) ** shard_levels(streams_of[11], (2, EXP), ((1, 4),), -0.2, 0.2), 0.5, 1.5),
        "depth_gains_first": normal_values(streams_of[12], (2, EXP), (1.8e-4), 0.0024414062, ((1, 4),), jnp.float32),
        "depth_gains_second": jnp.clip(jnp.exp(math.log(9.99999993922529e-09) - 1.34707364 * jax.random.uniform(streams_of[13], (2, EXP), jnp.float32) ** shard_levels(streams_of[13], (2, EXP), ((1, 4),), -0.2, 0.2)), 2.5999999930803597e-09, 9.99999993922529e-09),
        "squeeze_weight": normal_values(streams_of[14], (SE, EXP), EXP ** -0.5, 0.25, ((1, 4),), jnp.float32),
        "squeeze_weight_first": normal_values(streams_of[15], (SE, EXP), (5.3e-5), 0.0007324219, ((1, 4),), jnp.float32),
        "squeeze_weight_second": jnp.clip(jnp.exp(math.log(9.200000206099901e-10) - 1.3862944 * jax.random.uniform(streams_of[16], (SE, EXP), jnp.float32) ** shard_levels(streams_of[16], (SE, EXP), ((1, 4),), -0.2, 0.2)), 2.3000000515249752e-10, 9.200000206099901e-10),
        "squeeze_bias": normal_values(streams_of[17], (SE,), 0.5, 3.0, (), jnp.float32),
        "squeeze_bias_first": normal_values(streams_of[18], (SE,), (1.8e-4), 0.0024414062, (), jnp.float32),
        "squeeze_bias_second": jnp.clip(jnp.exp(jax.random.uniform(streams_of[19], (SE,), jnp.float32, math.log(2.5999999930803597e-09), math.log(9.99999993922529e-09))), 2.5999999930803597e-09, 9.99999993922529e-09),
        "excite_weight": normal_values(streams_of[20], (SE, EXP), SE ** -0.5, 1.0, ((1, 4),), jnp.float32),
        "excite_weight_first": normal_values(streams_of[21], (SE, EXP), (1.8e-5), 0.00024414062, ((1, 4),), jnp.float32),
        "excite_weight_second": jnp.clip(jnp.exp(math.log(1.000000013351432e-10) - 1.34707363 * jax.random.uniform(streams_of[22], (SE, EXP), jnp.float32) ** shard_levels(streams_of[22], (SE, EXP), ((1, 4),), -0.2, 0.2)), 2.6000000763470865e-11, 1.000000013351432e-10),
        "excite_bias": normal_values(streams_of[23], (EXP,), 0.5, 3.0, ((0, 4),), jnp.float32),
        "excite_bias_first": normal_values(streams_of[24], (EXP,), (5.9e-5), 0.0008544922, ((0, 4),), jnp.float32),
        "excite_bias_second": jnp.clip(jnp.exp(math.log(1.1999999882661427e-09) - 1.4201959 * jax.random.uniform(streams_of[25], (EXP,), jnp.float32) ** shard_levels(streams_of[25], (EXP,), ((0, 4),), -0.2, 0.2)), 2.8999999623913197e-10, 1.1999999882661427e-09),
        "project_weight": normal_values(streams_of[26], (C_IN, EXP), EXP ** -0.5, 0.25, ((1, 4),), jnp.float32),
        "project_weight_first": normal_values(streams_of[27], (C_IN, EXP), (3.5e-4), 0.0048828125, ((1, 4),), jnp.float32),
        "project_weight_second": jnp.clip(jnp.exp(math.log(4.099999983964153e-08) - 1.410987 * jax.random.uniform(streams_of[28], (C_IN, EXP), jnp.float32) ** shard_levels(streams_of[28], (C_IN, EXP), ((1, 4),), -0.2, 0.2)), 9.99999993922529e-09, 4.099999983964153e-08),
        "project_gains": jnp.clip(0.5 + 1.0 * jax.random.uniform(streams_of[29], (2, C_IN), jnp.float32) ** shard_levels(streams_of[29], (2, C_IN), ((1, 4),), -0.2, 0.2), 0.5, 1.5),
        "project_gains_first": normal_values(streams_of[30], (2, C_IN), (3.5e-4), 0.0048828125, ((1, 4),), jnp.float32),
        "project_gains_second": jnp.clip(jnp.exp(math.log(4.099999983964153e-08) - 1.410987 * jax.random.uniform(streams_of[31], (2, C_IN), jnp.float32) ** shard_levels(streams_of[31], (2, C_IN), ((1, 4),), -0.2, 0.2)), 9.99999993922529e-09, 4.099999983964153e-08),
    }


@jax.custom_vjp
def low(v):
    return lax.optimization_barrier(v.astype(jnp.bfloat16)).astype(jnp.float32)

@jax.custom_vjp
def low_back(v):
    return v

def low_keep(v):
    return (low(v), None)

def low_pass(kept, grad):
    return (grad,)

def back_keep(v):
    return (v, None)

def back_low(kept, grad):
    return (low(grad),)
low.defvjp(low_keep, low_pass)
low_back.defvjp(back_keep, back_low)
norm_epsilon = 1e-05
beta_first = 0.9
beta_second = 0.999
adam_epsilon = 1e-08
decay_rate = 0.01
clip_limit = 1.0
step_rates = (0.3, 0.6, 0.6, 0.6, 0.12, 0.6, 0.6, 0.6, 0.12, 0.6)
decay_flags = (1.0, 0.0, 1.0, 0.0, 1.0, 0.0, 1.0, 0.0, 1.0, 0.0)

def product(left, right):
    return jnp.dot(left, right, precision=lax.Precision.HIGHEST, preferred_element_type=jnp.float32)

def batch_norm(values, gain_pair):
    average = lax.optimization_barrier(jnp.mean(values, axis=1, keepdims=True))
    squares = lax.optimization_barrier(jnp.mean(values * values, axis=1, keepdims=True))
    normal = (values - average) * lax.rsqrt(squares - average * average + norm_epsilon)
    return normal * gain_pair[0][:, None] + gain_pair[1][:, None]

def swish(values):
    return values * jax.nn.sigmoid(values)

def depthwise(activity, kernel):
    half = KS // 2
    return lax.conv_general_dilated(activity, kernel.reshape(KS, KS, 1, EXP), (1, 1), ((half, half), (half, half)), dimension_numbers=('CHWN', 'HWIO', 'CHWN'), feature_group_count=EXP, precision=lax.Precision.HIGHEST)

def forward(source, expand_weight, expand_gains, depth_weight, depth_gains, squeeze_weight, squeeze_bias, excite_weight, excite_bias, project_weight, project_gains):
    flattened = source.reshape(C_IN, -1)
    expanded = low_back(product(low(expand_weight), flattened))
    active_one = swish(batch_norm(expanded, expand_gains)).reshape(EXP, HT, WD, SEGS)
    depth_out = depthwise(active_one, depth_weight).reshape(EXP, -1)
    active_two = swish(batch_norm(depth_out, depth_gains)).reshape(EXP, HT, WD, SEGS)
    pooled = lax.optimization_barrier(jnp.mean(active_two, axis=(1, 2)))
    hidden = swish(product(squeeze_weight, pooled) + squeeze_bias[:, None])
    gating = jax.nn.sigmoid(product(excite_weight.T, hidden) + excite_bias[:, None])
    scaled = low(active_two * gating[:, None, None, :]).reshape(EXP, -1)
    projected = low_back(product(low(project_weight), scaled))
    return (flattened + batch_norm(projected, project_gains)).reshape(C_IN, HT, WD, SEGS)

def adam_step(weight, first_moment, second, gradient, step_rate, decay_flag):
    first_new = beta_first * first_moment + (1.0 - beta_first) * gradient
    second_new = beta_second * second + (1.0 - beta_second) * gradient * gradient
    first_hat = first_new / (1.0 - beta_first ** STEP)
    second_hat = second_new / (1.0 - beta_second ** STEP)
    weight_new = weight - step_rate * (first_hat / (jnp.sqrt(second_hat) + adam_epsilon) + decay_flag * decay_rate * weight)
    return (weight_new, first_new, second_new)

def reference(block_input, cotangent, expand_weight, expand_weight_first, expand_weight_second, expand_gains, expand_gains_first, expand_gains_second, depth_weight, depth_weight_first, depth_weight_second, depth_gains, depth_gains_first, depth_gains_second, squeeze_weight, squeeze_weight_first, squeeze_weight_second, squeeze_bias, squeeze_bias_first, squeeze_bias_second, excite_weight, excite_weight_first, excite_weight_second, excite_bias, excite_bias_first, excite_bias_second, project_weight, project_weight_first, project_weight_second, project_gains, project_gains_first, project_gains_second):
    weights = (expand_weight, expand_gains, depth_weight, depth_gains, squeeze_weight, squeeze_bias, excite_weight, excite_bias, project_weight, project_gains)
    firsts = (expand_weight_first, expand_gains_first, depth_weight_first, depth_gains_first, squeeze_weight_first, squeeze_bias_first, excite_weight_first, excite_bias_first, project_weight_first, project_gains_first)
    seconds = (expand_weight_second, expand_gains_second, depth_weight_second, depth_gains_second, squeeze_weight_second, squeeze_bias_second, excite_weight_second, excite_bias_second, project_weight_second, project_gains_second)
    source = block_input.astype(jnp.float32)
    output, pullback = jax.vjp(forward, source, *weights)
    gradients = pullback(cotangent.astype(jnp.float32))
    input_grad = gradients[0]
    weight_grads = gradients[1:]
    total_square = jnp.float32(0.0)
    for gradient in weight_grads:
        total_square = total_square + jnp.sum(gradient * gradient)
    grad_norm = jnp.sqrt(total_square)
    factor = clip_limit / jnp.maximum(grad_norm, clip_limit)
    updated = [adam_step(weights[entry], firsts[entry], seconds[entry], weight_grads[entry] * factor, step_rates[entry], decay_flags[entry]) for entry in range(10)]
    return (output.astype(jnp.bfloat16), input_grad, updated[0][0], updated[0][1], updated[0][2], updated[1][0], updated[1][1], updated[1][2], updated[2][0], updated[2][1], updated[2][2], updated[3][0], updated[3][1], updated[3][2], updated[4][0], updated[4][1], updated[4][2], updated[5][0], updated[5][1], updated[5][2], updated[6][0], updated[6][1], updated[6][2], updated[7][0], updated[7][1], updated[7][2], updated[8][0], updated[8][1], updated[8][2], updated[9][0], updated[9][1], updated[9][2], grad_norm)
```

```python
import functools

import jax
import jax.numpy as jnp
from jax import lax
from jax.experimental import pallas as pl
from jax.experimental.pallas import tpu as pltpu
from jax.sharding import PartitionSpec as P

C_IN = 112
KS = 5
HT = 6
WD = 4
STEP = 10


norm_epsilon = 1e-05
beta_first = 0.9
beta_second = 0.999
adam_epsilon = 1e-08
decay_rate = 0.01
clip_limit = 1.0
step_rates = (0.3, 0.6, 0.6, 0.6, 0.12, 0.6, 0.6, 0.6, 0.12, 0.6)
decay_flags = (1.0, 0.0, 1.0, 0.0, 1.0, 0.0, 1.0, 0.0, 1.0, 0.0)
contract_rows = (((0,), (0,)), ((), ()))
contract_cols = (((1,), (1,)), ((), ()))
contract_plain = (((1,), (0,)), ((), ()))


def swish(values):
    return values * jax.nn.sigmoid(values)


def swish_slope(values):
    logistic = jax.nn.sigmoid(values)
    return logistic * (1.0 + values * (1.0 - logistic))


def highest(left, right, numbers):
    return lax.dot_general(
        left, right, numbers, precision=lax.Precision.HIGHEST, preferred_element_type=jnp.float32
    )


def depthwise(activity, kernel):
    half = KS // 2
    padded = jnp.pad(activity, ((0, 0), (half, half), (half, half), (0, 0)))
    result = jnp.zeros_like(activity)
    for row_shift in range(KS):
        for col_shift in range(KS):
            window = padded[:, row_shift : row_shift + HT, col_shift : col_shift + WD, :]
            result = result + kernel[row_shift * KS + col_shift][:, None, None, None] * window
    return result


def depthwise_back(grad_field, activity, kernel):
    half = KS // 2
    padded = jnp.pad(activity, ((0, 0), (half, half), (half, half), (0, 0)))
    grad_padded = jnp.pad(grad_field, ((0, 0), (half, half), (half, half), (0, 0)))
    activity_grad = jnp.zeros_like(activity)
    kernel_rows = []
    for row_shift in range(KS):
        for col_shift in range(KS):
            window = padded[:, row_shift : row_shift + HT, col_shift : col_shift + WD, :]
            kernel_rows.append(jnp.sum(grad_field * window, axis=(1, 2, 3)))
            back_window = grad_padded[
                :,
                2 * half - row_shift : 2 * half - row_shift + HT,
                2 * half - col_shift : 2 * half - col_shift + WD,
                :,
            ]
            activity_grad = (
                activity_grad
                + kernel[row_shift * KS + col_shift][:, None, None, None] * back_window
            )
    return (activity_grad, jnp.stack(kernel_rows))


def adam_step(weight, first_moment, second, gradient, step_rate, decay_flag):
    first_new = beta_first * first_moment + (1.0 - beta_first) * gradient
    second_new = beta_second * second + (1.0 - beta_second) * gradient * gradient
    first_hat = first_new / (1.0 - beta_first**STEP)
    second_hat = second_new / (1.0 - beta_second**STEP)
    weight_new = weight - step_rate * (
        first_hat / (jnp.sqrt(second_hat) + adam_epsilon) + decay_flag * decay_rate * weight
    )
    return (weight_new, first_new, second_new)


def on_device(
    block_input,
    cotangent,
    expand_weight,
    expand_weight_first,
    expand_weight_second,
    expand_gains,
    expand_gains_first,
    expand_gains_second,
    depth_weight,
    depth_weight_first,
    depth_weight_second,
    depth_gains,
    depth_gains_first,
    depth_gains_second,
    squeeze_weight,
    squeeze_weight_first,
    squeeze_weight_second,
    squeeze_bias,
    squeeze_bias_first,
    squeeze_bias_second,
    excite_weight,
    excite_weight_first,
    excite_weight_second,
    excite_bias,
    excite_bias_first,
    excite_bias_second,
    project_weight,
    project_weight_first,
    project_weight_second,
    project_gains,
    project_gains_first,
    project_gains_second,
):
    shards = lax.axis_size("chan")
    position = lax.axis_index("chan")
    segments = block_input.shape[3]
    batch_rows = HT * WD * segments * lax.axis_size("dp")
    narrow = cotangent.shape[0]
    local_channels = expand_weight.shape[0]
    flattened = block_input.reshape(C_IN, -1)
    expand_low = expand_weight.astype(jnp.bfloat16)
    expanded = jnp.dot(expand_low, flattened, preferred_element_type=jnp.float32)
    one_sums, one_squares = lax.psum(
        (jnp.sum(expanded, axis=1), jnp.sum(expanded * expanded, axis=1)), "dp"
    )
    one_average = one_sums / batch_rows
    one_spread = lax.rsqrt(one_squares / batch_rows - one_average * one_average + norm_epsilon)
    one_normal = (expanded - one_average[:, None]) * one_spread[:, None]
    one_before = one_normal * expand_gains[0][:, None] + expand_gains[1][:, None]
    active_one = swish(one_before).reshape(local_channels, HT, WD, segments)
    depth_out = depthwise(active_one, depth_weight).reshape(local_channels, -1)
    two_sums, two_squares = lax.psum(
        (jnp.sum(depth_out, axis=1), jnp.sum(depth_out * depth_out, axis=1)), "dp"
    )
    two_average = two_sums / batch_rows
    two_spread = lax.rsqrt(two_squares / batch_rows - two_average * two_average + norm_epsilon)
    two_normal = (depth_out - two_average[:, None]) * two_spread[:, None]
    two_before = two_normal * depth_gains[0][:, None] + depth_gains[1][:, None]
    active_two = swish(two_before).reshape(local_channels, HT, WD, segments)
    pooled = jnp.mean(active_two, axis=(1, 2))
    squeeze_part = highest(squeeze_weight, pooled, contract_plain)
    squeeze_pre = lax.psum(squeeze_part, "chan") + squeeze_bias[:, None]
    hidden = swish(squeeze_pre)
    gating = jax.nn.sigmoid(highest(excite_weight, hidden, contract_rows) + excite_bias[:, None])
    scaled = (
        (active_two * gating[:, None, None, :]).astype(jnp.bfloat16).reshape(local_channels, -1)
    )
    project_low = project_weight.astype(jnp.bfloat16)
    projected = lax.psum_scatter(
        jnp.dot(project_low, scaled, preferred_element_type=jnp.float32),
        "chan",
        scatter_dimension=0,
        tiled=True,
    )
    three_sums, three_squares = lax.psum(
        (jnp.sum(projected, axis=1), jnp.sum(projected * projected, axis=1)), "dp"
    )
    three_average = three_sums / batch_rows
    three_spread = lax.rsqrt(
        three_squares / batch_rows - three_average * three_average + norm_epsilon
    )
    three_normal = (projected - three_average[:, None]) * three_spread[:, None]
    three_after = three_normal * project_gains[0][:, None] + project_gains[1][:, None]
    own_input = lax.dynamic_slice_in_dim(flattened, position * narrow, narrow, 0).astype(
        jnp.float32
    )
    block_output = (own_input + three_after).astype(jnp.bfloat16).reshape(narrow, HT, WD, segments)
    upstream = cotangent.astype(jnp.float32).reshape(narrow, -1)
    three_beta, three_gamma = lax.psum(
        (jnp.sum(upstream, axis=1), jnp.sum(upstream * three_normal, axis=1)), "dp"
    )
    project_gains_grad = jnp.stack([three_gamma, three_beta])
    three_delta = (project_gains[0] * three_spread)[:, None] * (
        upstream
        - (three_beta / batch_rows)[:, None]
        - three_normal * (three_gamma / batch_rows)[:, None]
    )
    delta_whole = lax.all_gather(three_delta.astype(jnp.bfloat16), "chan", axis=0, tiled=True)
    scaled_grad = lax.dot_general(
        project_low, delta_whole, contract_rows, preferred_element_type=jnp.float32
    )
    project_weight_grad = lax.dot_general(
        delta_whole, scaled, contract_cols, preferred_element_type=jnp.float32
    )
    scaled_four = scaled_grad.reshape(local_channels, HT, WD, segments)
    gating_grad = jnp.sum(scaled_four * active_two, axis=(1, 2))
    excite_delta = gating_grad * gating * (1.0 - gating)
    excite_bias_grad = jnp.sum(excite_delta, axis=1)
    excite_weight_grad = highest(hidden, excite_delta, contract_cols)
    hidden_part = highest(excite_weight, excite_delta, contract_plain)
    hidden_grad = lax.psum(hidden_part, "chan")
    squeeze_delta = hidden_grad * swish_slope(squeeze_pre)
    squeeze_bias_grad = jnp.sum(squeeze_delta, axis=1)
    squeeze_weight_grad = highest(squeeze_delta, pooled, contract_cols)
    pooled_grad = highest(squeeze_weight, squeeze_delta, contract_rows)
    active_grad = scaled_four * gating[:, None, None, :] + pooled_grad[:, None, None, :] / (HT * WD)
    two_delta = active_grad.reshape(local_channels, -1) * swish_slope(two_before)
    two_gamma, two_beta = lax.psum(
        (jnp.sum(two_delta * two_normal, axis=1), jnp.sum(two_delta, axis=1)), "dp"
    )
    depth_gains_grad = jnp.stack([two_gamma, two_beta])
    depth_grad = (depth_gains[0] * two_spread)[:, None] * (
        two_delta
        - (two_beta / batch_rows)[:, None]
        - two_normal * (two_gamma / batch_rows)[:, None]
    )
    active_one_grad, depth_weight_grad = depthwise_back(
        depth_grad.reshape(local_channels, HT, WD, segments), active_one, depth_weight
    )
    one_delta = active_one_grad.reshape(local_channels, -1) * swish_slope(one_before)
    one_gamma, one_beta = lax.psum(
        (jnp.sum(one_delta * one_normal, axis=1), jnp.sum(one_delta, axis=1)), "dp"
    )
    expand_gains_grad = jnp.stack([one_gamma, one_beta])
    expand_delta = (
        (expand_gains[0] * one_spread)[:, None]
        * (
            one_delta
            - (one_beta / batch_rows)[:, None]
            - one_normal * (one_gamma / batch_rows)[:, None]
        )
    ).astype(jnp.bfloat16)
    expand_weight_grad = lax.dot_general(
        expand_delta, flattened, contract_cols, preferred_element_type=jnp.float32
    )
    input_part = lax.psum_scatter(
        lax.dot_general(
            expand_low, expand_delta, contract_rows, preferred_element_type=jnp.float32
        ).astype(jnp.bfloat16),
        "chan",
        scatter_dimension=0,
        tiled=True,
    ).astype(jnp.float32)
    input_grad = (input_part + upstream).reshape(narrow, HT, WD, segments)
    partials = (
        expand_weight_grad,
        depth_weight_grad,
        squeeze_weight_grad,
        excite_weight_grad,
        excite_bias_grad,
        project_weight_grad,
        squeeze_bias_grad,
    )
    gains_square = (
        jnp.sum(expand_gains_grad * expand_gains_grad)
        + jnp.sum(depth_gains_grad * depth_gains_grad)
        + jnp.sum(project_gains_grad * project_gains_grad)
    )
    summed = lax.psum(
        (partials[0], partials[1], partials[2], partials[3], partials[4], partials[5], partials[6]),
        "dp",
    )
    local_square = gains_square + jnp.sum(summed[6] * summed[6]) / shards
    for member in summed[:6]:
        local_square = local_square + jnp.sum(member * member)
    total_square = lax.psum(local_square, "chan")
    grad_norm = jnp.sqrt(total_square)
    factor = clip_limit / jnp.maximum(grad_norm, clip_limit)
    weights = (
        expand_weight,
        expand_gains,
        depth_weight,
        depth_gains,
        squeeze_weight,
        squeeze_bias,
        excite_weight,
        excite_bias,
        project_weight,
        project_gains,
    )
    firsts = (
        expand_weight_first,
        expand_gains_first,
        depth_weight_first,
        depth_gains_first,
        squeeze_weight_first,
        squeeze_bias_first,
        excite_weight_first,
        excite_bias_first,
        project_weight_first,
        project_gains_first,
    )
    seconds = (
        expand_weight_second,
        expand_gains_second,
        depth_weight_second,
        depth_gains_second,
        squeeze_weight_second,
        squeeze_bias_second,
        excite_weight_second,
        excite_bias_second,
        project_weight_second,
        project_gains_second,
    )
    gradients = (
        summed[0],
        expand_gains_grad,
        summed[1],
        depth_gains_grad,
        summed[2],
        summed[6],
        summed[3],
        summed[4],
        summed[5],
        project_gains_grad,
    )
    updated = [
        adam_step(
            weights[entry],
            firsts[entry],
            seconds[entry],
            gradients[entry] * factor,
            step_rates[entry],
            decay_flags[entry],
        )
        for entry in range(10)
    ]
    return (
        block_output,
        input_grad,
        updated[0][0],
        updated[0][1],
        updated[0][2],
        updated[1][0],
        updated[1][1],
        updated[1][2],
        updated[2][0],
        updated[2][1],
        updated[2][2],
        updated[3][0],
        updated[3][1],
        updated[3][2],
        updated[4][0],
        updated[4][1],
        updated[4][2],
        updated[5][0],
        updated[5][1],
        updated[5][2],
        updated[6][0],
        updated[6][1],
        updated[6][2],
        updated[7][0],
        updated[7][1],
        updated[7][2],
        updated[8][0],
        updated[8][1],
        updated[8][2],
        updated[9][0],
        updated[9][1],
        updated[9][2],
        grad_norm,
    )


POSITIONS = HT * WD
HALF_KS = KS // 2
PAIR_LANES = 384
HIDDEN_ROWS = 32
TAPS = KS * KS
ROW_SQUEEZE = 32
ROW_EXCITE = 64
ROW_EXCITE_BIAS = 96
ROW_EXPAND_GAINS = 97
ROW_DEPTH_GAINS = 99
ROW_PROJECT_GAINS = 101
STACK_ROWS = 104
PAIRED_ROWS_LIMIT = 3072
contract_lanes = (((1,), (1,)), ((), ()))
f32 = jnp.float32
bf16 = jnp.bfloat16


def paired_fits(mesh):
    return mesh.shape["chan"] == 4 and mesh.shape["dp"] * POSITIONS * 8 <= PAIRED_ROWS_LIMIT


def dot(left, right, numbers):
    return lax.dot_general(left, right, numbers, preferred_element_type=f32)


def rows_sum(values):
    return jnp.broadcast_to(jnp.sum(values, axis=0, keepdims=True), (8, values.shape[1]))


def lane_tile(index, start=0):
    return pl.ds(pl.multiple_of(start + index * 128, 128), 128)


def swish_of_half(half):
    return half * jnp.tanh(half) + half


def slope_of_half(half):
    bent = jnp.tanh(half)
    up = 1.0 + bent
    return 0.5 * up * (1.0 + half * (1.0 - bent))


def taps_of(row, col):
    found = []
    for i in range(KS):
        for j in range(KS):
            r, c = row + i - HALF_KS, col + j - HALF_KS
            if 0 <= r < HT and 0 <= c < WD:
                found.append((i * KS + j, r * WD + c))
    return found


def gram_kernel(x_ref, gram_ref):
    blocks = x_ref.shape[0]
    flat = x_ref[...].reshape(blocks * x_ref.shape[1], x_ref.shape[2])
    gram_ref[0:C_IN, :] = dot(flat, flat, contract_rows)
    ones = jnp.ones((8, flat.shape[0]), bf16)
    gram_ref[C_IN : C_IN + 8, :] = dot(ones, flat, contract_plain)


def expand_kernel(
    total_rows, gram_own, gram_other, x_ref, we_ref, stack_ref,
    depth_ref, sums_ref, norm_ref, expanded_scr, taps_scr,
):
    blocks = x_ref.shape[0]
    width = we_ref.shape[0]
    gram = gram_own[...] + gram_other[...]
    weights = we_ref[...].astype(f32)
    average = highest(gram[C_IN : C_IN + 8], weights, contract_lanes) / total_rows
    turned = highest(weights, gram[0:C_IN], contract_plain)
    squares = highest(jnp.ones((8, C_IN), f32), turned * weights, contract_lanes) / total_rows
    spread = lax.rsqrt(squares - average * average + norm_epsilon)
    gain = stack_ref[ROW_EXPAND_GAINS : ROW_EXPAND_GAINS + 1, :] * spread
    shift = stack_ref[ROW_EXPAND_GAINS + 1 : ROW_EXPAND_GAINS + 2, :] - average * gain
    norm_ref[0:8, :] = 0.5 * gain
    norm_ref[8:16, :] = 0.5 * shift
    norm_ref[16:24, :] = average
    norm_ref[24:32, :] = spread
    for tap in range(TAPS):
        taps_scr[tap] = jnp.broadcast_to(stack_ref[tap : tap + 1, :], (8, width))
    sums_ref[...] = jnp.zeros_like(sums_ref)

    def one_block(block, carry):
        expanded_scr[...] = dot(x_ref[block], we_ref[...], contract_lanes)

        def one_tile(tile, carry):
            lanes = lane_tile(tile)
            gain_half = norm_ref[0:8, lanes]
            shift_half = norm_ref[8:16, lanes]
            active = [
                swish_of_half(expanded_scr[8 * at : 8 * at + 8, lanes] * gain_half + shift_half)
                for at in range(POSITIONS)
            ]
            total = jnp.zeros((8, 128), f32)
            square = jnp.zeros((8, 128), f32)
            for row in range(HT):
                for col in range(WD):
                    at = row * WD + col
                    value = None
                    for tap, source in taps_of(row, col):
                        term = taps_scr[tap, :, lanes] * active[source]
                        value = term if value is None else value + term
                    depth_ref[block, 8 * at : 8 * at + 8, lanes] = value
                    total = total + value
                    square = square + value * value
            sums_ref[0:8, lanes] += total
            sums_ref[8:16, lanes] += square
            return carry

        return lax.fori_loop(0, width // 128, one_tile, carry)

    lax.fori_loop(0, blocks, one_block, 0)


def squeeze_kernel(
    total_rows, index_ref, depth_ref, sums_own, sums_other, stack_ref, wp_ref, cot_ref, bias_ref,
    projected_ref, scaled_ref, sums_ref, gate_ref, before_ref, pooled_ref, norm_ref,
    active_scr, scaled_scr,
):
    blocks = depth_ref.shape[0]
    width = depth_ref.shape[2]
    own = pl.multiple_of(index_ref[1] // 2 * PAIR_LANES, 128)
    average = rows_sum(sums_own[0:8] + sums_other[0:8]) / total_rows
    squares = rows_sum(sums_own[8:16] + sums_other[8:16]) / total_rows
    spread = lax.rsqrt(squares - average * average + norm_epsilon)
    gain = stack_ref[ROW_DEPTH_GAINS : ROW_DEPTH_GAINS + 1, :] * spread
    shift = stack_ref[ROW_DEPTH_GAINS + 1 : ROW_DEPTH_GAINS + 2, :] - average * gain
    norm_ref[0:8, :] = 0.5 * gain
    norm_ref[8:16, :] = 0.5 * shift
    norm_ref[16:24, :] = average
    norm_ref[24:32, :] = spread

    def pool_block(block, carry):
        def pool_tile(tile, carry):
            lanes = lane_tile(tile)
            gain_half = norm_ref[0:8, lanes]
            shift_half = norm_ref[8:16, lanes]
            total = jnp.zeros((8, 128), f32)
            for at in range(POSITIONS):
                value = swish_of_half(
                    depth_ref[block, 8 * at : 8 * at + 8, lanes] * gain_half + shift_half
                )
                active_scr[block, 8 * at : 8 * at + 8, lanes] = value
                total = total + value
            pooled_ref[pl.ds(pl.multiple_of(block * 8, 8), 8), lanes] = total / POSITIONS
            return carry

        return lax.fori_loop(0, width // 128, pool_tile, carry)

    lax.fori_loop(0, blocks, pool_block, 0)
    squeeze = stack_ref[ROW_SQUEEZE : ROW_SQUEEZE + HIDDEN_ROWS, :]
    excite = stack_ref[ROW_EXCITE : ROW_EXCITE + HIDDEN_ROWS, :]
    before = highest(pooled_ref[...], squeeze, contract_lanes) + bias_ref[...]
    before_ref[...] = before
    hidden = swish_of_half(0.5 * before)
    raised = highest(hidden, excite, contract_plain)
    raised = raised + stack_ref[ROW_EXCITE_BIAS : ROW_EXCITE_BIAS + 1, :]
    gate_ref[...] = 0.5 + 0.5 * jnp.tanh(0.5 * raised)
    sums_ref[...] = jnp.zeros_like(sums_ref)

    def scale_block(block, carry):
        for tile in range(width // 128):
            lanes = slice(tile * 128, tile * 128 + 128)
            gate = gate_ref[pl.ds(pl.multiple_of(block * 8, 8), 8), lanes]
            value = active_scr[block, :, lanes].reshape(POSITIONS, 8, 128) * gate[None]
            scaled_scr[:, lanes] = value.reshape(POSITIONS * 8, 128).astype(bf16)
        projected = dot(scaled_scr[...], wp_ref[...], contract_plain)
        projected_ref[block] = projected
        scaled_ref[block] = scaled_scr[:, pl.ds(own, PAIR_LANES)]
        shaped = projected.reshape(POSITIONS, 8, C_IN)
        upstream = cot_ref[block].astype(f32).reshape(POSITIONS, 8, C_IN)
        sums_ref[0:8, :] += jnp.sum(shaped, axis=0)
        sums_ref[8:16, :] += jnp.sum(shaped * shaped, axis=0)
        sums_ref[16:24, :] += jnp.sum(shaped * upstream, axis=0)
        sums_ref[24:32, :] += jnp.sum(upstream, axis=0)
        return carry

    lax.fori_loop(0, blocks, scale_block, 0)


def gate_back_kernel(
    total_rows, index_ref, projected_ref, cot_ref, sums_own, sums_other, gains_ref, depth_ref,
    norm_ref, stack_ref, wp_ref, gate_ref, before_ref, pooled_ref, scaled_ref, x_ref,
    two_ref, sums_ref, project_ref, lanes_ref, bias_ref, gains_grad_ref, output_ref,
    delta_scr, grad_scr, gate_grad_scr, pooled_scr,
):
    blocks = depth_ref.shape[0]
    width = depth_ref.shape[2]
    own = pl.multiple_of(index_ref[1] // 2 * PAIR_LANES, 128)
    own_lanes = pl.ds(own, PAIR_LANES)
    sums = [rows_sum(sums_own[8 * k : 8 * k + 8] + sums_other[8 * k : 8 * k + 8])[0:1] for k in range(4)]
    average = sums[0] / total_rows
    spread = lax.rsqrt(sums[1] / total_rows - average * average + norm_epsilon)
    beta = sums[3]
    gamma = spread * (sums[2] - average * beta)
    gains_grad_ref[0:1, :] = gamma
    gains_grad_ref[1:2, :] = beta
    gain = gains_ref[0:1, :]
    shift = gains_ref[1:2, :]
    mine = index_ref[0]
    output_ref[...] = (
        x_ref[mine].astype(f32) + (projected_ref[mine] - average) * spread * gain + shift
    ).astype(output_ref.dtype)
    outer = gain * spread

    def back_block(block, carry):
        normal = (projected_ref[block] - average) * spread
        delta = outer * (
            cot_ref[block].astype(f32) - beta / total_rows - normal * (gamma / total_rows)
        )
        delta_scr[block] = delta.astype(bf16)
        grad_scr[...] = dot(delta_scr[block], wp_ref[...], contract_lanes)
        two_ref[block] = grad_scr[:, own_lanes]

        def gate_tile(tile, carry):
            lanes = lane_tile(tile)
            gain_half = norm_ref[0:8, lanes]
            shift_half = norm_ref[8:16, lanes]
            total = jnp.zeros((8, 128), f32)
            for at in range(POSITIONS):
                active = swish_of_half(
                    depth_ref[block, 8 * at : 8 * at + 8, lanes] * gain_half + shift_half
                )
                total = total + active * grad_scr[8 * at : 8 * at + 8, lanes]
            gate_grad_scr[pl.ds(pl.multiple_of(block * 8, 8), 8), lanes] = total
            return carry

        return lax.fori_loop(0, width // 128, gate_tile, carry)

    lax.fori_loop(0, blocks, back_block, 0)
    excite = stack_ref[ROW_EXCITE : ROW_EXCITE + HIDDEN_ROWS, :]
    gate = gate_ref[...]
    gate_grad_scr[...] = gate_grad_scr[...] * gate * (1.0 - gate)
    half = 0.5 * before_ref[...]
    hidden = swish_of_half(half)
    squeeze_delta = highest(gate_grad_scr[...], excite, contract_lanes) * slope_of_half(half)
    own_delta = gate_grad_scr[:, own_lanes]
    lanes_ref[0:HIDDEN_ROWS, :] = highest(squeeze_delta, pooled_ref[:, own_lanes], contract_rows)
    lanes_ref[HIDDEN_ROWS : 2 * HIDDEN_ROWS, :] = highest(hidden, own_delta, contract_rows)
    lanes_ref[2 * HIDDEN_ROWS : 2 * HIDDEN_ROWS + 8, :] = rows_sum(own_delta)
    bias_ref[...] = rows_sum(squeeze_delta)
    squeeze = stack_ref[ROW_SQUEEZE : ROW_SQUEEZE + HIDDEN_ROWS, own_lanes]
    pooled_scr[...] = highest(squeeze_delta, squeeze, contract_plain) / POSITIONS
    sums_ref[...] = jnp.zeros_like(sums_ref)

    def two_block(block, carry):
        rows = pl.ds(pl.multiple_of(block * 8, 8), 8)

        def two_tile(tile, carry):
            lanes = lane_tile(tile)
            whole = lane_tile(tile, own)
            gain_half = norm_ref[0:8, whole]
            shift_half = norm_ref[8:16, whole]
            average = norm_ref[16:24, whole]
            gate = gate_ref[rows, whole]
            pooled_grad = pooled_scr[rows, lanes]
            total = jnp.zeros((8, 128), f32)
            product = jnp.zeros((8, 128), f32)
            for at in range(POSITIONS):
                spot = slice(8 * at, 8 * at + 8)
                depth = depth_ref[block, spot, whole]
                value = two_ref[block, spot, lanes] * gate + pooled_grad
                value = value * slope_of_half(depth * gain_half + shift_half)
                two_ref[block, spot, lanes] = value
                total = total + value
                product = product + value * (depth - average)
            sums_ref[0:8, lanes] += total
            sums_ref[8:16, lanes] += product
            return carry

        return lax.fori_loop(0, PAIR_LANES // 128, two_tile, carry)

    lax.fori_loop(0, blocks, two_block, 0)
    rows = blocks * POSITIONS * 8
    project_ref[...] = dot(
        scaled_ref[...].reshape(rows, PAIR_LANES), delta_scr[...].reshape(rows, C_IN), contract_rows
    )


def depth_back_kernel(
    total_rows, index_ref, sums_own, sums_other, two_ref, depth_ref, x_ref, we_ref, stack_ref,
    norm_one_ref, norm_two_ref,
    one_ref, sums_ref, kernel_ref, gains_grad_ref, expanded_scr, taps_scr, kernel_scr, factors_scr,
):
    blocks = depth_ref.shape[0]
    own = pl.multiple_of(index_ref[1] // 2 * PAIR_LANES, 128)
    own_lanes = pl.ds(own, PAIR_LANES)
    spread = norm_two_ref[24:32, own_lanes]
    average = norm_two_ref[16:24, own_lanes]
    beta = rows_sum(sums_own[0:8] + sums_other[0:8])
    gamma = rows_sum(sums_own[8:16] + sums_other[8:16]) * spread
    gains_grad_ref[0:1, :] = gamma[0:1]
    gains_grad_ref[1:2, :] = beta[0:1]
    outer = stack_ref[ROW_DEPTH_GAINS : ROW_DEPTH_GAINS + 1, own_lanes] * spread
    slope = outer * spread * gamma / total_rows
    factors_scr[0:8, :] = outer
    factors_scr[8:16, :] = slope
    factors_scr[16:24, :] = outer * (beta / total_rows)
    for tap in range(TAPS):
        taps_scr[tap] = jnp.broadcast_to(stack_ref[tap : tap + 1, own_lanes], (8, PAIR_LANES))
    sums_ref[...] = jnp.zeros_like(sums_ref)
    kernel_scr[...] = jnp.zeros_like(kernel_scr)
    own_weights = we_ref[own_lanes, :]

    def one_block(block, carry):
        expanded_scr[...] = dot(x_ref[block], own_weights, contract_lanes)

        def one_tile(tile, carry):
            lanes = lane_tile(tile)
            whole = lane_tile(tile, own)
            gain_half = norm_one_ref[0:8, whole]
            shift_half = norm_one_ref[8:16, whole]
            average_one = norm_one_ref[16:24, whole]
            average_two = norm_two_ref[16:24, whole]
            outer = factors_scr[0:8, lanes]
            slope = factors_scr[8:16, lanes]
            level = factors_scr[16:24, lanes]
            grads = []
            active = []
            for at in range(POSITIONS):
                spot = slice(8 * at, 8 * at + 8)
                grads.append(
                    outer * two_ref[block, spot, lanes]
                    - level
                    - slope * (depth_ref[block, spot, whole] - average_two)
                )
                active.append(swish_of_half(expanded_scr[spot, lanes] * gain_half + shift_half))
            pairs = {}
            for row in range(HT):
                for col in range(WD):
                    for tap, source in taps_of(row, col):
                        pairs.setdefault(tap, []).append((row * WD + col, source))
            for tap in range(TAPS):
                value = None
                for target, source in pairs[tap]:
                    term = grads[target] * active[source]
                    value = term if value is None else value + term
                kernel_scr[tap, :, lanes] += value
            back = {}
            for tap in range(TAPS):
                for target, source in pairs[tap]:
                    back.setdefault(source, []).append((tap, target))
            total = jnp.zeros((8, 128), f32)
            product = jnp.zeros((8, 128), f32)
            for at in range(POSITIONS):
                spot = slice(8 * at, 8 * at + 8)
                value = None
                for tap, target in back[at]:
                    term = taps_scr[tap, :, lanes] * grads[target]
                    value = term if value is None else value + term
                expanded = expanded_scr[spot, lanes]
                value = value * slope_of_half(expanded * gain_half + shift_half)
                one_ref[block, spot, lanes] = value
                total = total + value
                product = product + value * (expanded - average_one)
            sums_ref[0:8, lanes] += total
            sums_ref[8:16, lanes] += product
            return carry

        return lax.fori_loop(0, PAIR_LANES // 128, one_tile, carry)

    lax.fori_loop(0, blocks, one_block, 0)
    kernel_ref[...] = jnp.zeros_like(kernel_ref)
    for tap in range(TAPS):
        kernel_ref[tap : tap + 1, :] = jnp.sum(kernel_scr[tap], axis=0, keepdims=True)


def expand_back_kernel(
    total_rows, index_ref, sums_own, sums_other, one_ref, x_ref, we_ref, stack_ref, norm_ref,
    expand_ref, input_ref, gains_grad_ref, delta_scr,
):
    blocks = x_ref.shape[0]
    own = pl.multiple_of(index_ref[1] // 2 * PAIR_LANES, 128)
    own_lanes = pl.ds(own, PAIR_LANES)
    spread = norm_ref[24:32, own_lanes]
    average = norm_ref[16:17, own_lanes]
    beta = rows_sum(sums_own[0:8] + sums_other[0:8])
    gamma = rows_sum(sums_own[8:16] + sums_other[8:16]) * spread
    gains_grad_ref[0:1, :] = gamma[0:1]
    gains_grad_ref[1:2, :] = beta[0:1]
    outer = stack_ref[ROW_EXPAND_GAINS : ROW_EXPAND_GAINS + 1, own_lanes] * spread[0:1]
    slope = outer * spread[0:1] * gamma[0:1] / total_rows
    level = outer * (beta[0:1] / total_rows)
    own_weights = we_ref[own_lanes, :]

    def one_block(block, carry):
        expanded = dot(x_ref[block], own_weights, contract_lanes)
        delta = outer * one_ref[block] - level - slope * (expanded - average)
        delta_scr[block] = delta.astype(bf16)
        return carry

    lax.fori_loop(0, blocks, one_block, 0)
    rows = blocks * POSITIONS * 8
    expand_ref[...] = dot(
        delta_scr[...].reshape(rows, PAIR_LANES), x_ref[...].reshape(rows, C_IN), contract_rows
    )
    input_ref[...] = dot(delta_scr[index_ref[0]], own_weights, contract_plain)


def call(kernel, outs, operands, scratch=(), name=None):
    spaces = [
        pl.BlockSpec(memory_space=pltpu.SMEM)
        if operand.dtype == jnp.int32
        else pl.BlockSpec(memory_space=pltpu.VMEM)
        for operand in operands
    ]
    return pl.pallas_call(
        kernel,
        out_shape=[jax.ShapeDtypeStruct(shape, dtype) for shape, dtype in outs],
        in_specs=spaces,
        out_specs=[pl.BlockSpec(memory_space=pltpu.VMEM)] * len(outs),
        scratch_shapes=[pltpu.VMEM(shape, dtype) for shape, dtype in scratch],
        compiler_params=pltpu.CompilerParams(vmem_limit_bytes=56 * 1024 * 1024),
        name=name,
    )(*operands)


def settle_kernel(
    index_ref, expand_own, expand_other, project_own, project_other, lanes_own, lanes_other,
    kernel_own, kernel_other, bias_own, bias_other, three_ref, two_ref, one_ref, input_own, input_other,
    expand_ref, project_ref, lanes_ref, bias_ref, square_ref, input_ref,
):
    first = index_ref[1] % 2 == 0
    rows = expand_ref.shape[0]
    mine = pl.ds(pl.multiple_of(index_ref[1] % 2 * rows, 8), rows)
    total = jnp.zeros((1, 1), f32)

    def squared(values):
        return jnp.sum(jnp.sum(values * values, axis=0, keepdims=True), axis=1, keepdims=True)

    for own, other, out in (
        (expand_own, expand_other, expand_ref),
        (project_own, project_other, project_ref),
    ):
        total = total + squared(own[...] + other[...])
        out[...] = own[mine, :] + other[mine, :]

    def keep(start, values):
        lanes_ref[start : start + values.shape[0], :] = jnp.where(
            first, values[:, 0:rows], values[:, rows : 2 * rows]
        )

    summed = lanes_own[...] + lanes_other[...]
    summed = summed[0 : 2 * HIDDEN_ROWS + 1]
    kernel = kernel_own[...] + kernel_other[...]
    total = total + squared(summed) + squared(kernel)
    keep(0, kernel)
    keep(ROW_SQUEEZE, summed)
    for start, ref in ((ROW_EXPAND_GAINS, one_ref), (ROW_DEPTH_GAINS, two_ref)):
        values = ref[0:2, :]
        total = total + squared(values)
        keep(start, values)
    bias = bias_own[0:1, :] + bias_other[0:1, :]
    bias_ref[...] = bias
    square_ref[0:8, :] = jnp.broadcast_to(total, (8, 128))
    square_ref[8:16, :] = jnp.broadcast_to(squared(bias) + squared(three_ref[0:2, :]), (8, 128))
    input_ref[...] = input_own[...] + input_other[...].astype(f32)


def adam_kernel(
    index_ref, square_own, square_other, expand_grad, project_grad, lanes_grad, bias_grad, three_grad,
    input_own, input_other, output_own, output_other, cot_ref, *refs,
):
    first = index_ref[1] % 2 == 0
    params, outs = refs[:30], refs[30:]
    narrow = cot_ref.shape[2]
    total = square_own[0:1, 0:1] + square_other[0:1, 0:1] + square_own[8:9, 0:1]
    grad_norm = jnp.sqrt(total)
    factor = clip_limit / jnp.maximum(grad_norm, clip_limit)
    outs[32][...] = grad_norm
    pick = (
        lax.broadcasted_iota(jnp.int32, (C_IN, narrow), 0)
        == lax.broadcasted_iota(jnp.int32, (C_IN, narrow), 1) + index_ref[1] * narrow
    ).astype(f32)

    def halves(own, other):
        mine = highest(own[...].astype(f32), pick, contract_plain).reshape(POSITIONS, 8, narrow)
        theirs = highest(other[...].astype(f32), pick, contract_plain).reshape(POSITIONS, 8, narrow)
        return jnp.concatenate(
            [jnp.where(first, mine, theirs), jnp.where(first, theirs, mine)], axis=1
        )

    outs[0][...] = halves(output_own, output_other).astype(bf16)
    outs[1][...] = halves(input_own, input_other) + cot_ref[...].astype(f32)
    gradients = (
        expand_grad[...],
        lanes_grad[ROW_EXPAND_GAINS : ROW_EXPAND_GAINS + 2, :],
        lanes_grad[0:TAPS, :],
        lanes_grad[ROW_DEPTH_GAINS : ROW_DEPTH_GAINS + 2, :],
        lanes_grad[ROW_SQUEEZE : ROW_SQUEEZE + params[12].shape[0], :],
        bias_grad[:, 0 : params[15].shape[1]],
        lanes_grad[ROW_EXCITE : ROW_EXCITE + params[18].shape[0], :],
        lanes_grad[ROW_EXCITE_BIAS : ROW_EXCITE_BIAS + 1, :],
        project_grad[...],
        highest(three_grad[0:2, :], pick, contract_plain),
    )
    for entry in range(10):
        updated = adam_step(
            params[3 * entry][...],
            params[3 * entry + 1][...],
            params[3 * entry + 2][...],
            gradients[entry] * factor,
            step_rates[entry],
            decay_flags[entry],
        )
        for part in range(3):
            outs[2 + 3 * entry + part][...] = updated[part]


def on_device_paired(*arrays):
    block_input, cotangent = arrays[:2]
    (
        expand_weight, expand_gains, depth_weight, depth_gains, squeeze_weight,
        squeeze_bias, excite_weight, excite_bias, project_weight, project_gains,
    ) = arrays[2::3]
    segments = block_input.shape[3]
    if segments != 16:
        return on_device(*arrays)
    shards = lax.axis_size("dp")
    position = lax.axis_index("chan")
    core = position % 2
    index = jnp.stack([lax.axis_index("dp"), position]).astype(jnp.int32)
    total_rows = float(POSITIONS * segments * shards)
    narrow = cotangent.shape[0]
    channels = expand_weight.shape[0]
    hidden_units = squeeze_weight.shape[0]
    rows = POSITIONS * 8
    width = 2 * PAIR_LANES

    def swap(values, mask):
        return lax.ppermute(values, "chan", [(at, at ^ mask) for at in range(4)])

    def spread(values):
        copies = jnp.broadcast_to(values[None], (shards,) + values.shape)
        return lax.all_to_all(copies, "dp", 0, 0).reshape(shards, rows, C_IN)

    def whole(own, others):
        distance = [position ^ place for place in range(4)]
        return [
            jnp.where(
                at == 0, own, jnp.where(at == 1, others[0], jnp.where(at == 2, others[1], others[2]))
            )
            for at in distance
        ]

    def gather(values):
        return whole(values, [swap(values, mask) for mask in (1, 2, 3)])

    input_rows = jnp.transpose(block_input, (1, 2, 3, 0)).reshape(POSITIONS, segments, C_IN)
    cot_rows = jnp.transpose(cotangent, (1, 2, 3, 0)).reshape(POSITIONS, segments, narrow)
    x = spread(lax.dynamic_slice_in_dim(input_rows, core * 8, 8, 1))

    def padded(values, count):
        return jnp.pad(values, ((0, count - values.shape[0]), (0, channels - values.shape[1])))

    stack = jnp.concatenate(
        [
            padded(depth_weight, 32),
            padded(squeeze_weight, HIDDEN_ROWS),
            padded(excite_weight, HIDDEN_ROWS),
            excite_bias[None],
            expand_gains,
            depth_gains,
            padded(project_gains, 3),
        ],
        axis=0,
    )
    matrices = jnp.concatenate([expand_weight, project_weight.T], axis=0).astype(bf16)
    stacks = gather(stack)
    pairs = gather(matrices)
    kept = lax.dynamic_slice_in_dim(cot_rows, core * 8, 8, 1)
    sent = lax.dynamic_slice_in_dim(cot_rows, 8 - core * 8, 8, 1)
    cots = whole(kept, [swap(sent, 1), swap(kept, 2), swap(sent, 3)])
    cot = spread(jnp.concatenate(cots, axis=2))
    gap = jnp.zeros((PAIR_LANES - 2 * channels, C_IN), bf16)
    expand_all = jnp.concatenate(
        [pairs[0][:channels], pairs[1][:channels], gap, pairs[2][:channels], pairs[3][:channels], gap]
    )
    project_all = jnp.concatenate(
        [pairs[0][channels:], pairs[1][channels:], gap, pairs[2][channels:], pairs[3][channels:], gap]
    )
    side = jnp.zeros((STACK_ROWS, PAIR_LANES - 2 * channels), f32)
    stack_all = jnp.concatenate([stacks[0], stacks[1], side, stacks[2], stacks[3], side], axis=1)
    gains_all = jnp.concatenate(
        [part[ROW_PROJECT_GAINS : ROW_PROJECT_GAINS + 2, :narrow] for part in stacks], axis=1
    )
    bias_row = jnp.pad(squeeze_bias, (0, HIDDEN_ROWS - hidden_units))[None]

    (gram,) = call(gram_kernel, [((C_IN + 8, C_IN), f32)], [x], name="gram")
    depth, sums, norm_one = call(
        functools.partial(expand_kernel, total_rows),
        [((shards, rows, width), f32), ((16, width), f32), ((32, width), f32)],
        [gram, swap(gram, 1), x, expand_all, stack_all],
        [((rows, width), f32), ((TAPS, 8, width), f32)],
        name="expand",
    )
    projected, scaled, sums, gate, before, pooled, norm_two = call(
        functools.partial(squeeze_kernel, total_rows),
        [
            ((shards, rows, C_IN), f32),
            ((shards, rows, PAIR_LANES), bf16),
            ((32, C_IN), f32),
            ((shards * 8, width), f32),
            ((shards * 8, HIDDEN_ROWS), f32),
            ((shards * 8, width), f32),
            ((32, width), f32),
        ],
        [index, depth, sums, swap(sums, 1), stack_all, project_all, cot, bias_row],
        [((shards, rows, width), f32), ((rows, width), bf16)],
        name="squeeze",
    )
    two, sums, project_grad, lanes_grad, bias_grad, three_grad, output = call(
        functools.partial(gate_back_kernel, total_rows),
        [
            ((shards, rows, PAIR_LANES), f32),
            ((16, PAIR_LANES), f32),
            ((PAIR_LANES, C_IN), f32),
            ((2 * HIDDEN_ROWS + 8, PAIR_LANES), f32),
            ((8, HIDDEN_ROWS), f32),
            ((2, C_IN), f32),
            ((rows, C_IN), bf16),
        ],
        [
            index, projected, cot, sums, swap(sums, 1), gains_all, depth, norm_two, stack_all,
            project_all, gate, before, pooled, scaled, x,
        ],
        [
            ((shards, rows, C_IN), bf16),
            ((rows, width), f32),
            ((shards * 8, width), f32),
            ((shards * 8, PAIR_LANES), f32),
        ],
        name="gate_back",
    )
    sums_other = swap(sums, 1)
    early = [swap(project_grad, 1), swap(lanes_grad, 1), swap(bias_grad, 1), swap(output, 1)]
    one, sums, kernel_grad, two_grad = call(
        functools.partial(depth_back_kernel, total_rows),
        [
            ((shards, rows, PAIR_LANES), f32),
            ((16, PAIR_LANES), f32),
            ((32, PAIR_LANES), f32),
            ((2, PAIR_LANES), f32),
        ],
        [index, sums, sums_other, two, depth, x, expand_all, stack_all, norm_one, norm_two],
        [
            ((rows, PAIR_LANES), f32),
            ((TAPS, 8, PAIR_LANES), f32),
            ((TAPS, 8, PAIR_LANES), f32),
            ((24, PAIR_LANES), f32),
        ],
        name="depth_back",
    )
    expand_grad, input_part, one_grad = call(
        functools.partial(expand_back_kernel, total_rows),
        [((PAIR_LANES, C_IN), f32), ((rows, C_IN), f32), ((2, PAIR_LANES), f32)],
        [index, sums, swap(sums, 1), one, x, expand_all, stack_all, norm_one],
        [((shards, rows, PAIR_LANES), bf16)],
        name="expand_back",
    )
    expand_own, project_own, lanes_own, bias_own, square, input_half = call(
        settle_kernel,
        [
            ((channels, C_IN), f32),
            ((channels, C_IN), f32),
            ((STACK_ROWS, channels), f32),
            ((1, HIDDEN_ROWS), f32),
            ((16, 128), f32),
            ((rows, C_IN), f32),
        ],
        [
            index, expand_grad, swap(expand_grad, 1), project_grad, early[0], lanes_grad, early[1],
            kernel_grad, swap(kernel_grad, 1), bias_grad, early[2], three_grad, two_grad, one_grad,
            input_part, swap(input_part.astype(bf16), 2),
        ],
        name="settle",
    )
    params = list(arrays[2:])
    for at in (15, 16, 17, 21, 22, 23):
        params[at] = params[at][None]
    for at in (24, 25, 26):
        params[at] = params[at].T
    updated = call(
        adam_kernel,
        [((POSITIONS, segments, narrow), bf16), ((POSITIONS, segments, narrow), f32)]
        + [(value.shape, f32) for value in params]
        + [((1, 1), f32)],
        [
            index, square, swap(square, 2), expand_own, project_own, lanes_own, bias_own, three_grad,
            input_half, swap(input_half, 1), output, early[3], cot_rows, *params,
        ],
        name="adam",
    )
    results = list(updated)
    for at in (0, 1):
        results[at] = jnp.transpose(results[at].reshape(HT, WD, segments, narrow), (3, 0, 1, 2))
    for at in (17, 18, 19, 23, 24, 25):
        results[at] = results[at][0]
    for at in (26, 27, 28):
        results[at] = results[at].T
    results[32] = results[32][0, 0]
    return tuple(results)


def solution(mesh):
    body = on_device_paired if paired_fits(mesh) else on_device
    return jax.shard_map(
        body,
        mesh=mesh,
        in_specs=(
            P(None, None, None, "dp"),
            P("chan", None, None, "dp"),
            P("chan", None),
            P("chan", None),
            P("chan", None),
            P(None, "chan"),
            P(None, "chan"),
            P(None, "chan"),
            P(None, "chan"),
            P(None, "chan"),
            P(None, "chan"),
            P(None, "chan"),
            P(None, "chan"),
            P(None, "chan"),
            P(None, "chan"),
            P(None, "chan"),
            P(None, "chan"),
            P(),
            P(),
            P(),
            P(None, "chan"),
            P(None, "chan"),
            P(None, "chan"),
            P("chan"),
            P("chan"),
            P("chan"),
            P(None, "chan"),
            P(None, "chan"),
            P(None, "chan"),
            P(None, "chan"),
            P(None, "chan"),
            P(None, "chan"),
        ),
        out_specs=(
            P("chan", None, None, "dp"),
            P("chan", None, None, "dp"),
            P("chan", None),
            P("chan", None),
            P("chan", None),
            P(None, "chan"),
            P(None, "chan"),
            P(None, "chan"),
            P(None, "chan"),
            P(None, "chan"),
            P(None, "chan"),
            P(None, "chan"),
            P(None, "chan"),
            P(None, "chan"),
            P(None, "chan"),
            P(None, "chan"),
            P(None, "chan"),
            P(),
            P(),
            P(),
            P(None, "chan"),
            P(None, "chan"),
            P(None, "chan"),
            P("chan"),
            P("chan"),
            P("chan"),
            P(None, "chan"),
            P(None, "chan"),
            P(None, "chan"),
            P(None, "chan"),
            P(None, "chan"),
            P(None, "chan"),
            P(),
        ),
        check_vma=False,
    )
```

```python
import functools
import math

import jax
import jax.numpy as jnp
from jax import lax
from jax.experimental import pallas as pl
from jax.experimental.pallas import tpu as pltpu
from jax.sharding import PartitionSpec as P

C_IN = 112
KS = 5
HT = 6
WD = 4
STEP = 10


norm_epsilon = 1e-05
beta_first = 0.9
beta_second = 0.999
adam_epsilon = 1e-08
decay_rate = 0.01
clip_limit = 1.0
step_rates = (0.3, 0.6, 0.6, 0.6, 0.12, 0.6, 0.6, 0.6, 0.12, 0.6)
decay_flags = (1.0, 0.0, 1.0, 0.0, 1.0, 0.0, 1.0, 0.0, 1.0, 0.0)
contract_rows = (((0,), (0,)), ((), ()))
contract_cols = (((1,), (1,)), ((), ()))
contract_plain = (((1,), (0,)), ((), ()))


def swish(values):
    return values * jax.nn.sigmoid(values)


def swish_slope(values):
    logistic = jax.nn.sigmoid(values)
    return logistic * (1.0 + values * (1.0 - logistic))


def highest(left, right, numbers):
    return lax.dot_general(
        left, right, numbers, precision=lax.Precision.HIGHEST, preferred_element_type=jnp.float32
    )


def depthwise(activity, kernel):
    half = KS // 2
    padded = jnp.pad(activity, ((0, 0), (half, half), (half, half), (0, 0)))
    result = jnp.zeros_like(activity)
    for row_shift in range(KS):
        for col_shift in range(KS):
            window = padded[:, row_shift : row_shift + HT, col_shift : col_shift + WD, :]
            result = result + kernel[row_shift * KS + col_shift][:, None, None, None] * window
    return result


def depthwise_back(grad_field, activity, kernel):
    half = KS // 2
    padded = jnp.pad(activity, ((0, 0), (half, half), (half, half), (0, 0)))
    grad_padded = jnp.pad(grad_field, ((0, 0), (half, half), (half, half), (0, 0)))
    activity_grad = jnp.zeros_like(activity)
    kernel_rows = []
    for row_shift in range(KS):
        for col_shift in range(KS):
            window = padded[:, row_shift : row_shift + HT, col_shift : col_shift + WD, :]
            kernel_rows.append(jnp.sum(grad_field * window, axis=(1, 2, 3)))
            back_window = grad_padded[
                :,
                2 * half - row_shift : 2 * half - row_shift + HT,
                2 * half - col_shift : 2 * half - col_shift + WD,
                :,
            ]
            activity_grad = (
                activity_grad
                + kernel[row_shift * KS + col_shift][:, None, None, None] * back_window
            )
    return (activity_grad, jnp.stack(kernel_rows))


def adam_step(weight, first_moment, second, gradient, step_rate, decay_flag):
    first_new = beta_first * first_moment + (1.0 - beta_first) * gradient
    second_new = beta_second * second + (1.0 - beta_second) * gradient * gradient
    first_hat = first_new / (1.0 - beta_first**STEP)
    second_hat = second_new / (1.0 - beta_second**STEP)
    weight_new = weight - step_rate * (
        first_hat / (jnp.sqrt(second_hat) + adam_epsilon) + decay_flag * decay_rate * weight
    )
    return (weight_new, first_new, second_new)


def on_device(
    block_input,
    cotangent,
    expand_weight,
    expand_weight_first,
    expand_weight_second,
    expand_gains,
    expand_gains_first,
    expand_gains_second,
    depth_weight,
    depth_weight_first,
    depth_weight_second,
    depth_gains,
    depth_gains_first,
    depth_gains_second,
    squeeze_weight,
    squeeze_weight_first,
    squeeze_weight_second,
    squeeze_bias,
    squeeze_bias_first,
    squeeze_bias_second,
    excite_weight,
    excite_weight_first,
    excite_weight_second,
    excite_bias,
    excite_bias_first,
    excite_bias_second,
    project_weight,
    project_weight_first,
    project_weight_second,
    project_gains,
    project_gains_first,
    project_gains_second,
):
    shards = lax.axis_size("chan")
    position = lax.axis_index("chan")
    segments = block_input.shape[3]
    batch_rows = HT * WD * segments * lax.axis_size("dp")
    narrow = cotangent.shape[0]
    local_channels = expand_weight.shape[0]
    flattened = block_input.reshape(C_IN, -1)
    expand_low = expand_weight.astype(jnp.bfloat16)
    expanded = jnp.dot(expand_low, flattened, preferred_element_type=jnp.float32)
    one_sums, one_squares = lax.psum(
        (jnp.sum(expanded, axis=1), jnp.sum(expanded * expanded, axis=1)), "dp"
    )
    one_average = one_sums / batch_rows
    one_spread = lax.rsqrt(one_squares / batch_rows - one_average * one_average + norm_epsilon)
    one_normal = (expanded - one_average[:, None]) * one_spread[:, None]
    one_before = one_normal * expand_gains[0][:, None] + expand_gains[1][:, None]
    active_one = swish(one_before).reshape(local_channels, HT, WD, segments)
    depth_out = depthwise(active_one, depth_weight).reshape(local_channels, -1)
    two_sums, two_squares = lax.psum(
        (jnp.sum(depth_out, axis=1), jnp.sum(depth_out * depth_out, axis=1)), "dp"
    )
    two_average = two_sums / batch_rows
    two_spread = lax.rsqrt(two_squares / batch_rows - two_average * two_average + norm_epsilon)
    two_normal = (depth_out - two_average[:, None]) * two_spread[:, None]
    two_before = two_normal * depth_gains[0][:, None] + depth_gains[1][:, None]
    active_two = swish(two_before).reshape(local_channels, HT, WD, segments)
    pooled = jnp.mean(active_two, axis=(1, 2))
    squeeze_part = highest(squeeze_weight, pooled, contract_plain)
    squeeze_pre = lax.psum(squeeze_part, "chan") + squeeze_bias[:, None]
    hidden = swish(squeeze_pre)
    gating = jax.nn.sigmoid(highest(excite_weight, hidden, contract_rows) + excite_bias[:, None])
    scaled = (
        (active_two * gating[:, None, None, :]).astype(jnp.bfloat16).reshape(local_channels, -1)
    )
    project_low = project_weight.astype(jnp.bfloat16)
    projected = lax.psum_scatter(
        jnp.dot(project_low, scaled, preferred_element_type=jnp.float32),
        "chan",
        scatter_dimension=0,
        tiled=True,
    )
    three_sums, three_squares = lax.psum(
        (jnp.sum(projected, axis=1), jnp.sum(projected * projected, axis=1)), "dp"
    )
    three_average = three_sums / batch_rows
    three_spread = lax.rsqrt(
        three_squares / batch_rows - three_average * three_average + norm_epsilon
    )
    three_normal = (projected - three_average[:, None]) * three_spread[:, None]
    three_after = three_normal * project_gains[0][:, None] + project_gains[1][:, None]
    own_input = lax.dynamic_slice_in_dim(flattened, position * narrow, narrow, 0).astype(
        jnp.float32
    )
    block_output = (own_input + three_after).astype(jnp.bfloat16).reshape(narrow, HT, WD, segments)
    upstream = cotangent.astype(jnp.float32).reshape(narrow, -1)
    three_beta, three_gamma = lax.psum(
        (jnp.sum(upstream, axis=1), jnp.sum(upstream * three_normal, axis=1)), "dp"
    )
    project_gains_grad = jnp.stack([three_gamma, three_beta])
    three_delta = (project_gains[0] * three_spread)[:, None] * (
        upstream
        - (three_beta / batch_rows)[:, None]
        - three_normal * (three_gamma / batch_rows)[:, None]
    )
    delta_whole = lax.all_gather(three_delta.astype(jnp.bfloat16), "chan", axis=0, tiled=True)
    scaled_grad = lax.dot_general(
        project_low, delta_whole, contract_rows, preferred_element_type=jnp.float32
    )
    project_weight_grad = lax.dot_general(
        delta_whole, scaled, contract_cols, preferred_element_type=jnp.float32
    )
    scaled_four = scaled_grad.reshape(local_channels, HT, WD, segments)
    gating_grad = jnp.sum(scaled_four * active_two, axis=(1, 2))
    excite_delta = gating_grad * gating * (1.0 - gating)
    excite_bias_grad = jnp.sum(excite_delta, axis=1)
    excite_weight_grad = highest(hidden, excite_delta, contract_cols)
    hidden_part = highest(excite_weight, excite_delta, contract_plain)
    hidden_grad = lax.psum(hidden_part, "chan")
    squeeze_delta = hidden_grad * swish_slope(squeeze_pre)
    squeeze_bias_grad = jnp.sum(squeeze_delta, axis=1)
    squeeze_weight_grad = highest(squeeze_delta, pooled, contract_cols)
    pooled_grad = highest(squeeze_weight, squeeze_delta, contract_rows)
    active_grad = scaled_four * gating[:, None, None, :] + pooled_grad[:, None, None, :] / (HT * WD)
    two_delta = active_grad.reshape(local_channels, -1) * swish_slope(two_before)
    two_gamma, two_beta = lax.psum(
        (jnp.sum(two_delta * two_normal, axis=1), jnp.sum(two_delta, axis=1)), "dp"
    )
    depth_gains_grad = jnp.stack([two_gamma, two_beta])
    depth_grad = (depth_gains[0] * two_spread)[:, None] * (
        two_delta
        - (two_beta / batch_rows)[:, None]
        - two_normal * (two_gamma / batch_rows)[:, None]
    )
    active_one_grad, depth_weight_grad = depthwise_back(
        depth_grad.reshape(local_channels, HT, WD, segments), active_one, depth_weight
    )
    one_delta = active_one_grad.reshape(local_channels, -1) * swish_slope(one_before)
    one_gamma, one_beta = lax.psum(
        (jnp.sum(one_delta * one_normal, axis=1), jnp.sum(one_delta, axis=1)), "dp"
    )
    expand_gains_grad = jnp.stack([one_gamma, one_beta])
    expand_delta = (
        (expand_gains[0] * one_spread)[:, None]
        * (
            one_delta
            - (one_beta / batch_rows)[:, None]
            - one_normal * (one_gamma / batch_rows)[:, None]
        )
    ).astype(jnp.bfloat16)
    expand_weight_grad = lax.dot_general(
        expand_delta, flattened, contract_cols, preferred_element_type=jnp.float32
    )
    input_part = lax.psum_scatter(
        lax.dot_general(
            expand_low, expand_delta, contract_rows, preferred_element_type=jnp.float32
        ).astype(jnp.bfloat16),
        "chan",
        scatter_dimension=0,
        tiled=True,
    ).astype(jnp.float32)
    input_grad = (input_part + upstream).reshape(narrow, HT, WD, segments)
    partials = (
        expand_weight_grad,
        depth_weight_grad,
        squeeze_weight_grad,
        excite_weight_grad,
        excite_bias_grad,
        project_weight_grad,
        squeeze_bias_grad,
    )
    gains_square = (
        jnp.sum(expand_gains_grad * expand_gains_grad)
        + jnp.sum(depth_gains_grad * depth_gains_grad)
        + jnp.sum(project_gains_grad * project_gains_grad)
    )
    summed = lax.psum(
        (partials[0], partials[1], partials[2], partials[3], partials[4], partials[5], partials[6]),
        "dp",
    )
    local_square = gains_square + jnp.sum(summed[6] * summed[6]) / shards
    for member in summed[:6]:
        local_square = local_square + jnp.sum(member * member)
    total_square = lax.psum(local_square, "chan")
    grad_norm = jnp.sqrt(total_square)
    factor = clip_limit / jnp.maximum(grad_norm, clip_limit)
    weights = (
        expand_weight,
        expand_gains,
        depth_weight,
        depth_gains,
        squeeze_weight,
        squeeze_bias,
        excite_weight,
        excite_bias,
        project_weight,
        project_gains,
    )
    firsts = (
        expand_weight_first,
        expand_gains_first,
        depth_weight_first,
        depth_gains_first,
        squeeze_weight_first,
        squeeze_bias_first,
        excite_weight_first,
        excite_bias_first,
        project_weight_first,
        project_gains_first,
    )
    seconds = (
        expand_weight_second,
        expand_gains_second,
        depth_weight_second,
        depth_gains_second,
        squeeze_weight_second,
        squeeze_bias_second,
        excite_weight_second,
        excite_bias_second,
        project_weight_second,
        project_gains_second,
    )
    gradients = (
        summed[0],
        expand_gains_grad,
        summed[1],
        depth_gains_grad,
        summed[2],
        summed[6],
        summed[3],
        summed[4],
        summed[5],
        project_gains_grad,
    )
    updated = [
        adam_step(
            weights[entry],
            firsts[entry],
            seconds[entry],
            gradients[entry] * factor,
            step_rates[entry],
            decay_flags[entry],
        )
        for entry in range(10)
    ]
    return (
        block_output,
        input_grad,
        updated[0][0],
        updated[0][1],
        updated[0][2],
        updated[1][0],
        updated[1][1],
        updated[1][2],
        updated[2][0],
        updated[2][1],
        updated[2][2],
        updated[3][0],
        updated[3][1],
        updated[3][2],
        updated[4][0],
        updated[4][1],
        updated[4][2],
        updated[5][0],
        updated[5][1],
        updated[5][2],
        updated[6][0],
        updated[6][1],
        updated[6][2],
        updated[7][0],
        updated[7][1],
        updated[7][2],
        updated[8][0],
        updated[8][1],
        updated[8][2],
        updated[9][0],
        updated[9][1],
        updated[9][2],
        grad_norm,
    )


POSITIONS = HT * WD
HALF_KS = KS // 2
PAIR_LANES = 384
HIDDEN_ROWS = 32
TAPS = KS * KS
ROW_SQUEEZE = 32
ROW_EXCITE = 64
ROW_EXCITE_BIAS = 96
ROW_EXPAND_GAINS = 97
ROW_DEPTH_GAINS = 99
ROW_PROJECT_GAINS = 101
STACK_ROWS = 104
KEEP_BIASES = 64
KEEP_PROJECT = 80
KEEP_KERNEL = 192
KEEP_ROWS = 224
PACKED_ROWS = 96
BLOCK_ROWS = POSITIONS * 8
PAIRED_ROWS_LIMIT = 3072
contract_lanes = (((1,), (1,)), ((), ()))
f32 = jnp.float32
bf16 = jnp.bfloat16


def paired_fits(mesh):
    return mesh.shape["chan"] == 4 and mesh.shape["dp"] * POSITIONS * 8 <= PAIRED_ROWS_LIMIT


def dot(left, right, numbers):
    return lax.dot_general(left, right, numbers, preferred_element_type=f32)


def rows_sum(values):
    return jnp.broadcast_to(jnp.sum(values, axis=0, keepdims=True), (8, values.shape[1]))


def lane_tile(index, start=0):
    return pl.ds(pl.multiple_of(start + index * 128, 128), 128)


def swish_of_half(half):
    return half * jnp.tanh(half) + half


def slope_of_half(half):
    bent = jnp.tanh(half)
    up = 1.0 + bent
    return 0.5 * up * (1.0 + half * (1.0 - bent))


def taps_of(row, col):
    found = []
    for i in range(KS):
        for j in range(KS):
            r, c = row + i - HALF_KS, col + j - HALF_KS
            if 0 <= r < HT and 0 <= c < WD:
                found.append((i * KS + j, r * WD + c))
    return found


def gram_kernel(x_ref, gram_ref, packed_ref):
    blocks = x_ref.shape[0]
    flat = x_ref[:, 0:BLOCK_ROWS, :].reshape(blocks * BLOCK_ROWS, C_IN)
    gram_ref[0:C_IN, :] = dot(flat, flat, contract_rows)
    ones = jnp.ones((8, flat.shape[0]), bf16)
    gram_ref[C_IN : C_IN + 8, :] = dot(ones, flat, contract_plain)
    packed_ref[...] = x_ref[:, BLOCK_ROWS : BLOCK_ROWS + PACKED_ROWS, :]


def expand_kernel(
    total_rows, gram_own, gram_other, x_ref, we_ref, stack_ref,
    depth_ref, sums_ref, norm_ref, expanded_scr, taps_scr,
):
    blocks = x_ref.shape[0]
    width = we_ref.shape[0]
    gram = gram_own[...] + gram_other[...]
    weights = we_ref[...].astype(f32)
    average = highest(gram[C_IN : C_IN + 8], weights, contract_lanes) / total_rows
    turned = highest(weights, gram[0:C_IN], contract_plain)
    squares = highest(jnp.ones((8, C_IN), f32), turned * weights, contract_lanes) / total_rows
    spread = lax.rsqrt(squares - average * average + norm_epsilon)
    gain = stack_ref[ROW_EXPAND_GAINS : ROW_EXPAND_GAINS + 1, :] * spread
    shift = stack_ref[ROW_EXPAND_GAINS + 1 : ROW_EXPAND_GAINS + 2, :] - average * gain
    norm_ref[0:8, :] = 0.5 * gain
    norm_ref[8:16, :] = 0.5 * shift
    norm_ref[16:24, :] = average
    norm_ref[24:32, :] = spread
    for tap in range(TAPS):
        taps_scr[tap] = jnp.broadcast_to(stack_ref[tap : tap + 1, :], (8, width))
    sums_ref[...] = jnp.zeros_like(sums_ref)

    def one_block(block, carry):
        expanded_scr[...] = dot(x_ref[block, 0:BLOCK_ROWS, :], we_ref[...], contract_lanes)

        def one_tile(tile, carry):
            lanes = lane_tile(tile)
            gain_half = norm_ref[0:8, lanes]
            shift_half = norm_ref[8:16, lanes]
            active = [
                swish_of_half(expanded_scr[8 * at : 8 * at + 8, lanes] * gain_half + shift_half)
                for at in range(POSITIONS)
            ]
            total = jnp.zeros((8, 128), f32)
            square = jnp.zeros((8, 128), f32)
            for row in range(HT):
                for col in range(WD):
                    at = row * WD + col
                    value = None
                    for tap, source in taps_of(row, col):
                        term = taps_scr[tap, :, lanes] * active[source]
                        value = term if value is None else value + term
                    depth_ref[block, 8 * at : 8 * at + 8, lanes] = value
                    total = total + value
                    square = square + value * value
            sums_ref[0:8, lanes] += total
            sums_ref[8:16, lanes] += square
            return carry

        return lax.fori_loop(0, width // 128, one_tile, carry)

    lax.fori_loop(0, blocks, one_block, 0)


def squeeze_kernel(
    total_rows, index_ref, depth_ref, sums_own, sums_other, stack_ref, wp_ref, cot_ref, bias_ref,
    projected_ref, scaled_ref, sums_ref, gate_ref, before_ref, pooled_ref, norm_ref,
    active_scr, scaled_scr,
):
    blocks = depth_ref.shape[0]
    width = depth_ref.shape[2]
    own = pl.multiple_of(index_ref[1] // 2 * PAIR_LANES, 128)
    average = rows_sum(sums_own[0:8] + sums_other[0:8]) / total_rows
    squares = rows_sum(sums_own[8:16] + sums_other[8:16]) / total_rows
    spread = lax.rsqrt(squares - average * average + norm_epsilon)
    gain = stack_ref[ROW_DEPTH_GAINS : ROW_DEPTH_GAINS + 1, :] * spread
    shift = stack_ref[ROW_DEPTH_GAINS + 1 : ROW_DEPTH_GAINS + 2, :] - average * gain
    norm_ref[0:8, :] = 0.5 * gain
    norm_ref[8:16, :] = 0.5 * shift
    norm_ref[16:24, :] = average
    norm_ref[24:32, :] = spread

    def pool_block(block, carry):
        def pool_tile(tile, carry):
            lanes = lane_tile(tile)
            gain_half = norm_ref[0:8, lanes]
            shift_half = norm_ref[8:16, lanes]
            total = jnp.zeros((8, 128), f32)
            for at in range(POSITIONS):
                value = swish_of_half(
                    depth_ref[block, 8 * at : 8 * at + 8, lanes] * gain_half + shift_half
                )
                active_scr[block, 8 * at : 8 * at + 8, lanes] = value
                total = total + value
            pooled_ref[pl.ds(pl.multiple_of(block * 8, 8), 8), lanes] = total / POSITIONS
            return carry

        return lax.fori_loop(0, width // 128, pool_tile, carry)

    lax.fori_loop(0, blocks, pool_block, 0)
    squeeze = stack_ref[ROW_SQUEEZE : ROW_SQUEEZE + HIDDEN_ROWS, :]
    excite = stack_ref[ROW_EXCITE : ROW_EXCITE + HIDDEN_ROWS, :]
    before = highest(pooled_ref[...], squeeze, contract_lanes) + bias_ref[...]
    before_ref[...] = before
    hidden = swish_of_half(0.5 * before)
    raised = highest(hidden, excite, contract_plain)
    raised = raised + stack_ref[ROW_EXCITE_BIAS : ROW_EXCITE_BIAS + 1, :]
    gate_ref[...] = 0.5 + 0.5 * jnp.tanh(0.5 * raised)
    sums_ref[...] = jnp.zeros_like(sums_ref)

    def scale_block(block, carry):
        for tile in range(width // 128):
            lanes = slice(tile * 128, tile * 128 + 128)
            gate = gate_ref[pl.ds(pl.multiple_of(block * 8, 8), 8), lanes]
            value = active_scr[block, :, lanes].reshape(POSITIONS, 8, 128) * gate[None]
            scaled_scr[:, lanes] = value.reshape(POSITIONS * 8, 128).astype(bf16)
        projected = dot(scaled_scr[...], wp_ref[...], contract_plain)
        projected_ref[block] = projected
        scaled_ref[block] = scaled_scr[:, pl.ds(own, PAIR_LANES)]
        shaped = projected.reshape(POSITIONS, 8, C_IN)
        upstream = cot_ref[block].astype(f32).reshape(POSITIONS, 8, C_IN)
        sums_ref[0:8, :] += jnp.sum(shaped, axis=0)
        sums_ref[8:16, :] += jnp.sum(shaped * shaped, axis=0)
        sums_ref[16:24, :] += jnp.sum(shaped * upstream, axis=0)
        sums_ref[24:32, :] += jnp.sum(upstream, axis=0)
        return carry

    lax.fori_loop(0, blocks, scale_block, 0)


def gate_back_kernel(
    total_rows, index_ref, projected_ref, cot_ref, sums_own, sums_other, gains_ref, depth_ref,
    norm_ref, stack_ref, wp_ref, gate_ref, before_ref, pooled_ref, scaled_ref, x_ref,
    two_ref, sums_ref, lanes_ref, gains_grad_ref, output_ref,
    delta_scr, grad_scr, gate_grad_scr, pooled_scr,
):
    blocks = depth_ref.shape[0]
    width = depth_ref.shape[2]
    own = pl.multiple_of(index_ref[1] // 2 * PAIR_LANES, 128)
    own_lanes = pl.ds(own, PAIR_LANES)
    sums = [rows_sum(sums_own[8 * k : 8 * k + 8] + sums_other[8 * k : 8 * k + 8])[0:1] for k in range(4)]
    average = sums[0] / total_rows
    spread = lax.rsqrt(sums[1] / total_rows - average * average + norm_epsilon)
    beta = sums[3]
    gamma = spread * (sums[2] - average * beta)
    gains_grad_ref[0:1, :] = gamma
    gains_grad_ref[1:2, :] = beta
    gain = gains_ref[0:1, :]
    shift = gains_ref[1:2, :]
    mine = index_ref[0]
    output_ref[...] = (
        x_ref[mine, 0:BLOCK_ROWS, :].astype(f32) + (projected_ref[mine] - average) * spread * gain + shift
    ).astype(output_ref.dtype)
    outer = gain * spread

    def back_block(block, carry):
        normal = (projected_ref[block] - average) * spread
        delta = outer * (
            cot_ref[block].astype(f32) - beta / total_rows - normal * (gamma / total_rows)
        )
        delta_scr[block] = delta.astype(bf16)
        grad_scr[...] = dot(delta_scr[block], wp_ref[...], contract_lanes)
        two_ref[block] = grad_scr[:, own_lanes]

        def gate_tile(tile, carry):
            lanes = lane_tile(tile)
            gain_half = norm_ref[0:8, lanes]
            shift_half = norm_ref[8:16, lanes]
            total = jnp.zeros((8, 128), f32)
            for at in range(POSITIONS):
                active = swish_of_half(
                    depth_ref[block, 8 * at : 8 * at + 8, lanes] * gain_half + shift_half
                )
                total = total + active * grad_scr[8 * at : 8 * at + 8, lanes]
            gate_grad_scr[pl.ds(pl.multiple_of(block * 8, 8), 8), lanes] = total
            return carry

        return lax.fori_loop(0, width // 128, gate_tile, carry)

    lax.fori_loop(0, blocks, back_block, 0)
    excite = stack_ref[ROW_EXCITE : ROW_EXCITE + HIDDEN_ROWS, :]
    gate = gate_ref[...]
    gate_grad_scr[...] = gate_grad_scr[...] * gate * (1.0 - gate)
    half = 0.5 * before_ref[...]
    hidden = swish_of_half(half)
    squeeze_delta = highest(gate_grad_scr[...], excite, contract_lanes) * slope_of_half(half)
    own_delta = gate_grad_scr[:, own_lanes]
    lanes_ref[0:HIDDEN_ROWS, :] = highest(squeeze_delta, pooled_ref[:, own_lanes], contract_rows)
    lanes_ref[HIDDEN_ROWS : 2 * HIDDEN_ROWS, :] = highest(hidden, own_delta, contract_rows)
    lanes_ref[KEEP_BIASES : KEEP_BIASES + 8, :] = rows_sum(own_delta)
    lanes_ref[KEEP_BIASES + 8 : KEEP_BIASES + 16, :] = jnp.zeros((8, PAIR_LANES), f32)
    lanes_ref[KEEP_BIASES + 8 : KEEP_BIASES + 16, 0:HIDDEN_ROWS] = rows_sum(squeeze_delta)
    squeeze = stack_ref[ROW_SQUEEZE : ROW_SQUEEZE + HIDDEN_ROWS, own_lanes]
    pooled_scr[...] = highest(squeeze_delta, squeeze, contract_plain) / POSITIONS
    sums_ref[...] = jnp.zeros_like(sums_ref)

    def two_block(block, carry):
        rows = pl.ds(pl.multiple_of(block * 8, 8), 8)

        def two_tile(tile, carry):
            lanes = lane_tile(tile)
            whole = lane_tile(tile, own)
            gain_half = norm_ref[0:8, whole]
            shift_half = norm_ref[8:16, whole]
            average = norm_ref[16:24, whole]
            gate = gate_ref[rows, whole]
            pooled_grad = pooled_scr[rows, lanes]
            total = jnp.zeros((8, 128), f32)
            product = jnp.zeros((8, 128), f32)
            for at in range(POSITIONS):
                spot = slice(8 * at, 8 * at + 8)
                depth = depth_ref[block, spot, whole]
                value = two_ref[block, spot, lanes] * gate + pooled_grad
                value = value * slope_of_half(depth * gain_half + shift_half)
                two_ref[block, spot, lanes] = value
                total = total + value
                product = product + value * (depth - average)
            sums_ref[0:8, lanes] += total
            sums_ref[8:16, lanes] += product
            return carry

        return lax.fori_loop(0, PAIR_LANES // 128, two_tile, carry)

    lax.fori_loop(0, blocks, two_block, 0)
    rows = blocks * POSITIONS * 8
    lanes_ref[KEEP_PROJECT : KEEP_PROJECT + C_IN, :] = dot(
        delta_scr[...].reshape(rows, C_IN), scaled_ref[...].reshape(rows, PAIR_LANES), contract_rows
    )


def depth_back_kernel(
    total_rows, index_ref, sums_own, sums_other, two_ref, depth_ref, x_ref, we_ref, stack_ref, lanes_ref,
    norm_one_ref, norm_two_ref,
    one_ref, sums_ref, kernel_ref, gains_grad_ref, expanded_scr, taps_scr, kernel_scr, factors_scr,
):
    blocks = depth_ref.shape[0]
    own = pl.multiple_of(index_ref[1] // 2 * PAIR_LANES, 128)
    own_lanes = pl.ds(own, PAIR_LANES)
    spread = norm_two_ref[24:32, own_lanes]
    average = norm_two_ref[16:24, own_lanes]
    beta = rows_sum(sums_own[0:8] + sums_other[0:8])
    gamma = rows_sum(sums_own[8:16] + sums_other[8:16]) * spread
    gains_grad_ref[0:1, :] = gamma[0:1]
    gains_grad_ref[1:2, :] = beta[0:1]
    outer = stack_ref[ROW_DEPTH_GAINS : ROW_DEPTH_GAINS + 1, own_lanes] * spread
    slope = outer * spread * gamma / total_rows
    factors_scr[0:8, :] = outer
    factors_scr[8:16, :] = slope
    factors_scr[16:24, :] = outer * (beta / total_rows)
    for tap in range(TAPS):
        taps_scr[tap] = jnp.broadcast_to(stack_ref[tap : tap + 1, own_lanes], (8, PAIR_LANES))
    sums_ref[...] = jnp.zeros_like(sums_ref)
    kernel_scr[...] = jnp.zeros_like(kernel_scr)
    own_weights = we_ref[own_lanes, :]

    def one_block(block, carry):
        expanded_scr[...] = dot(x_ref[block, 0:BLOCK_ROWS, :], own_weights, contract_lanes)

        def one_tile(tile, carry):
            lanes = lane_tile(tile)
            whole = lane_tile(tile, own)
            gain_half = norm_one_ref[0:8, whole]
            shift_half = norm_one_ref[8:16, whole]
            average_one = norm_one_ref[16:24, whole]
            average_two = norm_two_ref[16:24, whole]
            outer = factors_scr[0:8, lanes]
            slope = factors_scr[8:16, lanes]
            level = factors_scr[16:24, lanes]
            grads = []
            active = []
            for at in range(POSITIONS):
                spot = slice(8 * at, 8 * at + 8)
                grads.append(
                    outer * two_ref[block, spot, lanes]
                    - level
                    - slope * (depth_ref[block, spot, whole] - average_two)
                )
                active.append(swish_of_half(expanded_scr[spot, lanes] * gain_half + shift_half))
            pairs = {}
            for row in range(HT):
                for col in range(WD):
                    for tap, source in taps_of(row, col):
                        pairs.setdefault(tap, []).append((row * WD + col, source))
            for tap in range(TAPS):
                value = None
                for target, source in pairs[tap]:
                    term = grads[target] * active[source]
                    value = term if value is None else value + term
                kernel_scr[tap, :, lanes] += value
            back = {}
            for tap in range(TAPS):
                for target, source in pairs[tap]:
                    back.setdefault(source, []).append((tap, target))
            total = jnp.zeros((8, 128), f32)
            product = jnp.zeros((8, 128), f32)
            for at in range(POSITIONS):
                spot = slice(8 * at, 8 * at + 8)
                value = None
                for tap, target in back[at]:
                    term = taps_scr[tap, :, lanes] * grads[target]
                    value = term if value is None else value + term
                expanded = expanded_scr[spot, lanes]
                value = value * slope_of_half(expanded * gain_half + shift_half)
                one_ref[block, spot, lanes] = value
                total = total + value
                product = product + value * (expanded - average_one)
            sums_ref[0:8, lanes] += total
            sums_ref[8:16, lanes] += product
            return carry

        return lax.fori_loop(0, PAIR_LANES // 128, one_tile, carry)

    lax.fori_loop(0, blocks, one_block, 0)
    kernel_ref[0:KEEP_KERNEL, :] = lanes_ref[...]
    kernel_ref[KEEP_KERNEL : KEEP_KERNEL + 32, :] = jnp.zeros((32, PAIR_LANES), f32)
    for tap in range(TAPS):
        row = KEEP_KERNEL + tap
        kernel_ref[row : row + 1, :] = jnp.sum(kernel_scr[tap], axis=0, keepdims=True)


def expand_back_kernel(
    total_rows, index_ref, sums_own, sums_other, one_ref, x_ref, we_ref, stack_ref, norm_ref,
    expand_ref, input_ref, gains_grad_ref, delta_scr,
):
    blocks = x_ref.shape[0]
    own = pl.multiple_of(index_ref[1] // 2 * PAIR_LANES, 128)
    own_lanes = pl.ds(own, PAIR_LANES)
    spread = norm_ref[24:32, own_lanes]
    average = norm_ref[16:17, own_lanes]
    beta = rows_sum(sums_own[0:8] + sums_other[0:8])
    gamma = rows_sum(sums_own[8:16] + sums_other[8:16]) * spread
    gains_grad_ref[0:1, :] = gamma[0:1]
    gains_grad_ref[1:2, :] = beta[0:1]
    outer = stack_ref[ROW_EXPAND_GAINS : ROW_EXPAND_GAINS + 1, own_lanes] * spread[0:1]
    slope = outer * spread[0:1] * gamma[0:1] / total_rows
    level = outer * (beta[0:1] / total_rows)
    own_weights = we_ref[own_lanes, :]

    def one_block(block, carry):
        expanded = dot(x_ref[block, 0:BLOCK_ROWS, :], own_weights, contract_lanes)
        delta = outer * one_ref[block] - level - slope * (expanded - average)
        delta_scr[block] = delta.astype(bf16)
        return carry

    lax.fori_loop(0, blocks, one_block, 0)
    rows = blocks * POSITIONS * 8
    expand_ref[...] = dot(
        x_ref[:, 0:BLOCK_ROWS, :].reshape(rows, C_IN), delta_scr[...].reshape(rows, PAIR_LANES), contract_rows
    )
    input_ref[...] = dot(delta_scr[index_ref[0]], own_weights, contract_plain)


def one_hot(rows, columns, matches):
    return matches(
        lax.broadcasted_iota(jnp.int32, (rows, columns), 0),
        lax.broadcasted_iota(jnp.int32, (rows, columns), 1),
    )


def copies_kernel(index_ref, rows_ref, cot_ref, copies_ref):
    whole = rows_ref[...].astype(f32)
    half = jnp.where(index_ref[1] % 2 == 0, whole[:, 0:8, :], whole[:, 8:16, :])
    half = half.reshape(BLOCK_ROWS, C_IN).astype(bf16)
    narrow = cot_ref.shape[2]
    rows = cot_ref[...].reshape(4 * PACKED_ROWS, narrow)
    packed = None
    for group in range(4):
        place = one_hot(narrow, C_IN, lambda r, c: c == r + group * narrow).astype(bf16)
        part = dot(rows[group * PACKED_ROWS : (group + 1) * PACKED_ROWS], place, contract_plain)
        packed = part if packed is None else packed + part
    packed = packed.astype(bf16)
    for at in range(copies_ref.shape[0]):
        copies_ref[at, 0:BLOCK_ROWS, :] = half
        copies_ref[at, BLOCK_ROWS : BLOCK_ROWS + PACKED_ROWS, :] = packed


def cot_kernel(index_ref, own_ref, near_ref, far_ref, cross_ref, cot_ref):
    position = index_ref[1]
    first = position % 2 == 0
    near = position + 1 - position % 2 * 2
    blocks = cot_ref.shape[0]
    narrow = C_IN // 4
    rows = blocks * PACKED_ROWS
    pieces = (
        (own_ref, position), (near_ref, near), (far_ref, (position + 2) % 4),
        (cross_ref, (near + 2) % 4),
    )
    for group in range(4):
        total = None
        for ref, place in pieces:
            move = one_hot(
                C_IN,
                C_IN,
                lambda r, c: (c - place * narrow == r - group * narrow)
                & (r >= group * narrow) & (r < (group + 1) * narrow),
            ).astype(bf16)
            part = dot(ref[...].reshape(rows, C_IN), move, contract_plain)
            total = part if total is None else total + part
        total = total.reshape(rows // 16, 16, C_IN)
        half = jnp.where(first, total[:, 0:8, :], total[:, 8:16, :])
        half = half.reshape(blocks, PACKED_ROWS // 2, C_IN).astype(bf16)
        start = group * (PACKED_ROWS // 2)
        cot_ref[:, start : start + PACKED_ROWS // 2, :] = half


def pack_kernel(
    expand_ref, project_ref, depth_ref, squeeze_ref, excite_ref, excite_bias_ref, expand_gains_ref,
    depth_gains_ref, project_gains_ref, stack_ref, matrix_ref,
):
    channels = expand_ref.shape[0]
    narrow = project_gains_ref.shape[1]
    stack_ref[...] = jnp.zeros_like(stack_ref)
    for start, ref in (
        (0, depth_ref), (ROW_SQUEEZE, squeeze_ref), (ROW_EXCITE, excite_ref),
        (ROW_EXCITE_BIAS, excite_bias_ref), (ROW_EXPAND_GAINS, expand_gains_ref),
        (ROW_DEPTH_GAINS, depth_gains_ref),
    ):
        stack_ref[start : start + ref.shape[0], :] = ref[...]
    stack_ref[ROW_PROJECT_GAINS : ROW_PROJECT_GAINS + 2, 0:narrow] = project_gains_ref[...]
    matrix_ref[...] = jnp.concatenate(
        [expand_ref[...], project_ref[...]], axis=0
    ).astype(bf16)


def assemble_kernel(
    index_ref, stack_0, stack_1, stack_2, stack_3, matrix_0, matrix_1, matrix_2, matrix_3,
    x_ref, stack_ref, expand_ref, project_ref, gains_ref,
):
    position = index_ref[1]
    first = position % 2 == 0
    front = position // 2 == 0
    channels = stack_0.shape[1]
    narrow = C_IN // 4

    def ordered(own, near, far, cross):
        low, high = jnp.where(first, own, near), jnp.where(first, near, own)
        far_low, far_high = jnp.where(first, far, cross), jnp.where(first, cross, far)
        return (
            jnp.where(front, low, far_low), jnp.where(front, high, far_high),
            jnp.where(front, far_low, low), jnp.where(front, far_high, high),
        )

    stacks = ordered(stack_0[...], stack_1[...], stack_2[...], stack_3[...])
    stack_ref[...] = jnp.zeros_like(stack_ref)
    for place in range(4):
        start = place // 2 * PAIR_LANES + place % 2 * channels
        stack_ref[:, start : start + channels] = stacks[place]
        gains_ref[:, place * narrow : (place + 1) * narrow] = stacks[place][
            ROW_PROJECT_GAINS : ROW_PROJECT_GAINS + 2, 0:narrow
        ]
    matrices = ordered(*[ref[...].astype(f32) for ref in (matrix_0, matrix_1, matrix_2, matrix_3)])
    gap = jnp.zeros((PAIR_LANES - 2 * channels, C_IN), f32)
    for ref, start in ((expand_ref, 0), (project_ref, channels)):
        parts = [matrix[start : start + channels] for matrix in matrices]
        ref[...] = jnp.concatenate(parts[0:2] + [gap] + parts[2:4] + [gap], axis=0).astype(bf16)


def settle_kernel(
    index_ref, expand_own, expand_other, keep_own, keep_other, three_ref, two_ref, one_ref,
    input_own, input_other,
    expand_ref, project_ref, lanes_ref, bias_ref, square_ref, input_ref, packed_ref,
):
    position = index_ref[1]
    first = position % 2 == 0
    channels = expand_ref.shape[0]
    narrow = C_IN // 4

    def squared(values):
        return jnp.sum(jnp.sum(values * values, axis=0, keepdims=True), axis=1, keepdims=True)

    def mine(values):
        return jnp.where(first, values[:, 0:channels], values[:, channels : 2 * channels])

    def both(start, stop):
        return keep_own[start:stop, :] + keep_other[start:stop, :]

    expand = expand_own[...] + expand_other[...]
    project = both(KEEP_PROJECT, KEEP_PROJECT + C_IN)
    hidden = both(0, 2 * HIDDEN_ROWS)
    excite_bias = both(KEEP_BIASES, KEEP_BIASES + 1)
    kernel = both(KEEP_KERNEL, KEEP_KERNEL + 32)
    total = squared(expand) + squared(project) + squared(hidden) + squared(kernel)
    total = total + squared(excite_bias) + squared(one_ref[...]) + squared(two_ref[...])
    bias = both(KEEP_BIASES + 8, KEEP_BIASES + 9)[:, 0:HIDDEN_ROWS]
    square_ref[0:8, :] = jnp.broadcast_to(total, (8, 128))
    square_ref[8:16, :] = jnp.broadcast_to(squared(bias) + squared(three_ref[...]), (8, 128))
    bias_ref[...] = bias
    expand_ref[...] = jnp.transpose(mine(expand))
    project_ref[...] = jnp.transpose(mine(project))
    lanes_ref[0:32, :] = mine(kernel)
    lanes_ref[ROW_SQUEEZE : ROW_SQUEEZE + 2 * HIDDEN_ROWS, :] = mine(hidden)
    lanes_ref[ROW_EXCITE_BIAS : ROW_EXCITE_BIAS + 1, :] = mine(excite_bias)
    lanes_ref[ROW_EXPAND_GAINS : ROW_EXPAND_GAINS + 2, :] = mine(one_ref[...])
    lanes_ref[ROW_DEPTH_GAINS : ROW_DEPTH_GAINS + 2, :] = mine(two_ref[...])
    own = input_own[...].reshape(POSITIONS, 8, C_IN)
    other = input_other[...].reshape(POSITIONS, 8, C_IN)
    whole = jnp.concatenate(
        [jnp.where(first, own, other), jnp.where(first, other, own)], axis=1
    ).reshape(4 * PACKED_ROWS, C_IN)
    pick = one_hot(C_IN, narrow, lambda r, c: r == c + position * narrow).astype(f32)
    input_ref[...] = highest(whole, pick, contract_plain).reshape(POSITIONS, 16, narrow)
    across = position + 2 - position // 2 * 4
    low = whole.astype(bf16)
    packed = None
    for group in range(4):
        move = one_hot(
            C_IN,
            C_IN,
            lambda r, c: (r - across * narrow == c - group * narrow)
            & (c >= group * narrow) & (c < (group + 1) * narrow),
        ).astype(bf16)
        part = dot(low[group * PACKED_ROWS : (group + 1) * PACKED_ROWS], move, contract_plain)
        packed = part if packed is None else packed + part
    packed_ref[...] = packed.astype(bf16)


def output_kernel(index_ref, own_ref, other_ref, output_ref):
    first = index_ref[1] % 2 == 0
    narrow = output_ref.shape[2]
    pick = one_hot(C_IN, narrow, lambda r, c: r == c + index_ref[1] * narrow).astype(bf16)
    own = dot(own_ref[...], pick, contract_plain).reshape(POSITIONS, 8, narrow)
    other = dot(other_ref[...], pick, contract_plain).reshape(POSITIONS, 8, narrow)
    output_ref[...] = jnp.concatenate(
        [jnp.where(first, own, other), jnp.where(first, other, own)], axis=1
    ).astype(bf16)


def adam_kernel(
    index_ref, square_own, square_other, expand_grad, project_grad, lanes_grad, bias_grad, three_grad,
    input_own, packed_other, cot_ref, *refs,
):
    params, outs = refs[:30], refs[30:]
    narrow = cot_ref.shape[2]
    total = square_own[0:1, 0:1] + square_other[0:1, 0:1] + square_own[8:9, 0:1]
    grad_norm = jnp.sqrt(total)
    factor = clip_limit / jnp.maximum(grad_norm, clip_limit)
    outs[31][...] = grad_norm
    groups = []
    for group in range(4):
        pick = one_hot(C_IN, narrow, lambda r, c: r == c + group * narrow).astype(bf16)
        groups.append(dot(packed_other[...], pick, contract_plain))
    crossed = jnp.concatenate(groups, axis=0).reshape(POSITIONS, 16, narrow)
    outs[0][...] = input_own[...] + crossed + cot_ref[...].astype(f32)
    pick = one_hot(C_IN, narrow, lambda r, c: r == c + index_ref[1] * narrow).astype(f32)
    gradients = (
        expand_grad[...],
        lanes_grad[ROW_EXPAND_GAINS : ROW_EXPAND_GAINS + 2, :],
        lanes_grad[0:TAPS, :],
        lanes_grad[ROW_DEPTH_GAINS : ROW_DEPTH_GAINS + 2, :],
        lanes_grad[ROW_SQUEEZE : ROW_SQUEEZE + params[12].shape[0], :],
        bias_grad[:, 0 : params[15].shape[1]],
        lanes_grad[ROW_EXCITE : ROW_EXCITE + params[18].shape[0], :],
        lanes_grad[ROW_EXCITE_BIAS : ROW_EXCITE_BIAS + 1, :],
        project_grad[...],
        highest(three_grad[0:2, :], pick, contract_plain),
    )
    for entry in range(10):
        updated = adam_step(
            params[3 * entry][...],
            params[3 * entry + 1][...],
            params[3 * entry + 2][...],
            gradients[entry] * factor,
            step_rates[entry],
            decay_flags[entry],
        )
        for part in range(3):
            outs[1 + 3 * entry + part][...] = updated[part]


def call(kernel, outs, operands, scratch=(), name=None, keep=True, place=True):
    spaces = [
        pl.BlockSpec(memory_space=pltpu.SMEM)
        if operand.dtype == jnp.int32
        else pl.BlockSpec(memory_space=pltpu.VMEM)
        for operand in operands
    ]
    operands = [
        operand
        if operand.dtype == jnp.int32
        else pltpu.with_memory_space_constraint(operand, pltpu.VMEM if place else pltpu.HBM)
        for operand in operands
    ]
    limit = 4 * 1024 * 1024 + sum(4 * math.prod(shape) for shape, _ in scratch)
    made = pltpu.VMEM if keep else jax.ShapeDtypeStruct
    return pl.pallas_call(
        kernel,
        out_shape=[made(shape, dtype) for shape, dtype in outs],
        in_specs=spaces,
        out_specs=[pl.BlockSpec(memory_space=pltpu.VMEM)] * len(outs),
        scratch_shapes=[pltpu.VMEM(shape, dtype) for shape, dtype in scratch],
        compiler_params=pltpu.CompilerParams(vmem_limit_bytes=limit),
        name=name,
    )(*operands)


def on_device_paired(*arrays):
    block_input, cotangent = arrays[:2]
    segments = block_input.shape[3]
    if segments != 16:
        return on_device(*arrays)
    params = list(arrays[2:])
    for at in (15, 16, 17, 21, 22, 23):
        params[at] = params[at][None]
    for at in (24, 25, 26):
        params[at] = params[at].T
    (
        expand_weight, expand_gains, depth_weight, depth_gains, squeeze_weight,
        squeeze_bias, excite_weight, excite_bias, project_weight, project_gains,
    ) = params[::3]
    shards = lax.axis_size("dp")
    index = jnp.stack([lax.axis_index("dp"), lax.axis_index("chan")]).astype(jnp.int32)
    total_rows = float(POSITIONS * segments * shards)
    narrow = cotangent.shape[0]
    channels = expand_weight.shape[0]
    rows = POSITIONS * 8
    width = 2 * PAIR_LANES

    def swap(values, mask):
        return lax.ppermute(values, "chan", [(at, at ^ mask) for at in range(4)])

    input_rows = jnp.transpose(block_input, (1, 2, 3, 0)).reshape(POSITIONS, segments, C_IN)
    cot_rows = jnp.transpose(cotangent, (1, 2, 3, 0)).reshape(POSITIONS, segments, narrow)
    (copies,) = call(
        copies_kernel,
        [((shards, rows + PACKED_ROWS, C_IN), bf16)],
        [index, input_rows, cot_rows],
        name="copies",
        keep=False,
        place=False,
    )
    x = lax.all_to_all(copies, "dp", 0, 0)
    stack, matrix = call(
        pack_kernel,
        [((STACK_ROWS, channels), f32), ((2 * channels, C_IN), bf16)],
        [
            expand_weight, project_weight, depth_weight, squeeze_weight, excite_weight, excite_bias,
            expand_gains, depth_gains, project_gains,
        ],
        name="pack",
        keep=False,
        place=False,
    )
    stack_far, matrix_far = swap(stack, 2), swap(matrix, 2)
    pieces = [
        stack, swap(stack, 1), stack_far, swap(stack_far, 1),
        matrix, swap(matrix, 1), matrix_far, swap(matrix_far, 1),
    ]
    gram, packed = call(
        gram_kernel,
        [((C_IN + 8, C_IN), f32), ((shards, PACKED_ROWS, C_IN), bf16)],
        [x],
        name="gram",
    )
    stack_all, expand_all, project_all, gains_all = call(
        assemble_kernel,
        [
            ((STACK_ROWS, width), f32),
            ((width, C_IN), bf16),
            ((width, C_IN), bf16),
            ((2, C_IN), f32),
        ],
        [index, *pieces, packed],
        name="assemble",
    )
    (cot,) = call(
        cot_kernel,
        [((shards, rows, C_IN), bf16)],
        [index, packed, swap(packed, 1), swap(packed, 2), swap(packed, 3)],
        name="cot",
    )
    bias_row = jnp.pad(squeeze_bias, ((0, 0), (0, HIDDEN_ROWS - squeeze_bias.shape[1])))

    depth, sums, norm_one = call(
        functools.partial(expand_kernel, total_rows),
        [((shards, rows, width), f32), ((16, width), f32), ((32, width), f32)],
        [gram, swap(gram, 1), x, expand_all, stack_all],
        [((rows, width), f32), ((TAPS, 8, width), f32)],
        name="expand",
    )
    projected, scaled, sums, gate, before, pooled, norm_two = call(
        functools.partial(squeeze_kernel, total_rows),
        [
            ((shards, rows, C_IN), f32),
            ((shards, rows, PAIR_LANES), bf16),
            ((32, C_IN), f32),
            ((shards * 8, width), f32),
            ((shards * 8, HIDDEN_ROWS), f32),
            ((shards * 8, width), f32),
            ((32, width), f32),
        ],
        [index, depth, sums, swap(sums, 1), stack_all, project_all, cot, bias_row],
        [((shards, rows, width), f32), ((rows, width), bf16)],
        name="squeeze",
    )
    two, sums, lanes_grad, three_grad, output = call(
        functools.partial(gate_back_kernel, total_rows),
        [
            ((shards, rows, PAIR_LANES), f32),
            ((16, PAIR_LANES), f32),
            ((KEEP_KERNEL, PAIR_LANES), f32),
            ((2, C_IN), f32),
            ((rows, C_IN), bf16),
        ],
        [
            index, projected, cot, sums, swap(sums, 1), gains_all, depth, norm_two, stack_all,
            project_all, gate, before, pooled, scaled, x,
        ],
        [
            ((shards, rows, C_IN), bf16),
            ((rows, width), f32),
            ((shards * 8, width), f32),
            ((shards * 8, PAIR_LANES), f32),
        ],
        name="gate_back",
    )
    one, sums, keep, two_grad = call(
        functools.partial(depth_back_kernel, total_rows),
        [
            ((shards, rows, PAIR_LANES), f32),
            ((16, PAIR_LANES), f32),
            ((KEEP_ROWS, PAIR_LANES), f32),
            ((2, PAIR_LANES), f32),
        ],
        [
            index, sums, swap(sums, 1), two, depth, x, expand_all, stack_all, lanes_grad,
            norm_one, norm_two,
        ],
        [
            ((rows, PAIR_LANES), f32),
            ((TAPS, 8, PAIR_LANES), f32),
            ((TAPS, 8, PAIR_LANES), f32),
            ((24, PAIR_LANES), f32),
        ],
        name="depth_back",
    )
    expand_grad, input_part, one_grad = call(
        functools.partial(expand_back_kernel, total_rows),
        [((C_IN, PAIR_LANES), f32), ((rows, C_IN), f32), ((2, PAIR_LANES), f32)],
        [index, sums, swap(sums, 1), one, x, expand_all, stack_all, norm_one],
        [((shards, rows, PAIR_LANES), bf16)],
        name="expand_back",
    )
    expand_own, project_own, lanes_own, bias_own, square, input_own, packed = call(
        settle_kernel,
        [
            ((channels, C_IN), f32),
            ((channels, C_IN), f32),
            ((STACK_ROWS, channels), f32),
            ((1, HIDDEN_ROWS), f32),
            ((16, 128), f32),
            ((POSITIONS, segments, narrow), f32),
            ((PACKED_ROWS, C_IN), bf16),
        ],
        [
            index, expand_grad, swap(expand_grad, 1), keep, swap(keep, 1), three_grad, two_grad,
            one_grad, input_part, swap(input_part, 1),
        ],
        name="settle",
    )
    (block_output,) = call(
        output_kernel,
        [((POSITIONS, segments, narrow), bf16)],
        [index, output, swap(output, 1)],
        name="output",
        keep=False,
    )
    updated = call(
        adam_kernel,
        [((POSITIONS, segments, narrow), f32)]
        + [(value.shape, f32) for value in params]
        + [((1, 1), f32)],
        [
            index, square, swap(square, 2), expand_own, project_own, lanes_own, bias_own, three_grad,
            input_own, swap(packed, 2), cot_rows, *params,
        ],
        name="adam",
        keep=False,
    )
    results = [block_output] + list(updated)
    for at in (0, 1):
        results[at] = jnp.transpose(results[at].reshape(HT, WD, segments, narrow), (3, 0, 1, 2))
    for at in (17, 18, 19, 23, 24, 25):
        results[at] = results[at][0]
    for at in (26, 27, 28):
        results[at] = results[at].T
    results[32] = results[32][0, 0]
    return tuple(results)


def solution(mesh):
    body = on_device_paired if paired_fits(mesh) else on_device
    return jax.shard_map(
        body,
        mesh=mesh,
        in_specs=(
            P(None, None, None, "dp"),
            P("chan", None, None, "dp"),
            P("chan", None),
            P("chan", None),
            P("chan", None),
            P(None, "chan"),
            P(None, "chan"),
            P(None, "chan"),
            P(None, "chan"),
            P(None, "chan"),
            P(None, "chan"),
            P(None, "chan"),
            P(None, "chan"),
            P(None, "chan"),
            P(None, "chan"),
            P(None, "chan"),
            P(None, "chan"),
            P(),
            P(),
            P(),
            P(None, "chan"),
            P(None, "chan"),
            P(None, "chan"),
            P("chan"),
            P("chan"),
            P("chan"),
            P(None, "chan"),
            P(None, "chan"),
            P(None, "chan"),
            P(None, "chan"),
            P(None, "chan"),
            P(None, "chan"),
        ),
        out_specs=(
            P("chan", None, None, "dp"),
            P("chan", None, None, "dp"),
            P("chan", None),
            P("chan", None),
            P("chan", None),
            P(None, "chan"),
            P(None, "chan"),
            P(None, "chan"),
            P(None, "chan"),
            P(None, "chan"),
            P(None, "chan"),
            P(None, "chan"),
            P(None, "chan"),
            P(None, "chan"),
            P(None, "chan"),
            P(None, "chan"),
            P(None, "chan"),
            P(),
            P(),
            P(),
            P(None, "chan"),
            P(None, "chan"),
            P(None, "chan"),
            P("chan"),
            P("chan"),
            P("chan"),
            P(None, "chan"),
            P(None, "chan"),
            P(None, "chan"),
            P(None, "chan"),
            P(None, "chan"),
            P(None, "chan"),
            P(),
        ),
        check_vma=False,
    )
```

```python
import functools
import math

import jax
import jax.numpy as jnp
from jax import lax
from jax.experimental import pallas as pl
from jax.experimental.pallas import tpu as pltpu
from jax.sharding import PartitionSpec as P

C_IN = 112
KS = 5
HT = 6
WD = 4
STEP = 10


norm_epsilon = 1e-05
beta_first = 0.9
beta_second = 0.999
adam_epsilon = 1e-08
decay_rate = 0.01
clip_limit = 1.0
step_rates = (0.3, 0.6, 0.6, 0.6, 0.12, 0.6, 0.6, 0.6, 0.12, 0.6)
decay_flags = (1.0, 0.0, 1.0, 0.0, 1.0, 0.0, 1.0, 0.0, 1.0, 0.0)
contract_rows = (((0,), (0,)), ((), ()))
contract_cols = (((1,), (1,)), ((), ()))
contract_plain = (((1,), (0,)), ((), ()))


def swish(values):
    return values * jax.nn.sigmoid(values)


def swish_slope(values):
    logistic = jax.nn.sigmoid(values)
    return logistic * (1.0 + values * (1.0 - logistic))


def highest(left, right, numbers):
    return lax.dot_general(
        left, right, numbers, precision=lax.Precision.HIGHEST, preferred_element_type=jnp.float32
    )


def depthwise(activity, kernel):
    half = KS // 2
    padded = jnp.pad(activity, ((0, 0), (half, half), (half, half), (0, 0)))
    result = jnp.zeros_like(activity)
    for row_shift in range(KS):
        for col_shift in range(KS):
            window = padded[:, row_shift : row_shift + HT, col_shift : col_shift + WD, :]
            result = result + kernel[row_shift * KS + col_shift][:, None, None, None] * window
    return result


def depthwise_back(grad_field, activity, kernel):
    half = KS // 2
    padded = jnp.pad(activity, ((0, 0), (half, half), (half, half), (0, 0)))
    grad_padded = jnp.pad(grad_field, ((0, 0), (half, half), (half, half), (0, 0)))
    activity_grad = jnp.zeros_like(activity)
    kernel_rows = []
    for row_shift in range(KS):
        for col_shift in range(KS):
            window = padded[:, row_shift : row_shift + HT, col_shift : col_shift + WD, :]
            kernel_rows.append(jnp.sum(grad_field * window, axis=(1, 2, 3)))
            back_window = grad_padded[
                :,
                2 * half - row_shift : 2 * half - row_shift + HT,
                2 * half - col_shift : 2 * half - col_shift + WD,
                :,
            ]
            activity_grad = (
                activity_grad
                + kernel[row_shift * KS + col_shift][:, None, None, None] * back_window
            )
    return (activity_grad, jnp.stack(kernel_rows))


def adam_step(weight, first_moment, second, gradient, step_rate, decay_flag):
    first_new = beta_first * first_moment + (1.0 - beta_first) * gradient
    second_new = beta_second * second + (1.0 - beta_second) * gradient * gradient
    first_hat = first_new / (1.0 - beta_first**STEP)
    second_hat = second_new / (1.0 - beta_second**STEP)
    weight_new = weight - step_rate * (
        first_hat / (jnp.sqrt(second_hat) + adam_epsilon) + decay_flag * decay_rate * weight
    )
    return (weight_new, first_new, second_new)


def on_device(
    block_input,
    cotangent,
    expand_weight,
    expand_weight_first,
    expand_weight_second,
    expand_gains,
    expand_gains_first,
    expand_gains_second,
    depth_weight,
    depth_weight_first,
    depth_weight_second,
    depth_gains,
    depth_gains_first,
    depth_gains_second,
    squeeze_weight,
    squeeze_weight_first,
    squeeze_weight_second,
    squeeze_bias,
    squeeze_bias_first,
    squeeze_bias_second,
    excite_weight,
    excite_weight_first,
    excite_weight_second,
    excite_bias,
    excite_bias_first,
    excite_bias_second,
    project_weight,
    project_weight_first,
    project_weight_second,
    project_gains,
    project_gains_first,
    project_gains_second,
):
    shards = lax.axis_size("chan")
    position = lax.axis_index("chan")
    segments = block_input.shape[3]
    batch_rows = HT * WD * segments * lax.axis_size("dp")
    narrow = cotangent.shape[0]
    local_channels = expand_weight.shape[0]
    flattened = block_input.reshape(C_IN, -1)
    expand_low = expand_weight.astype(jnp.bfloat16)
    expanded = jnp.dot(expand_low, flattened, preferred_element_type=jnp.float32)
    one_sums, one_squares = lax.psum(
        (jnp.sum(expanded, axis=1), jnp.sum(expanded * expanded, axis=1)), "dp"
    )
    one_average = one_sums / batch_rows
    one_spread = lax.rsqrt(one_squares / batch_rows - one_average * one_average + norm_epsilon)
    one_normal = (expanded - one_average[:, None]) * one_spread[:, None]
    one_before = one_normal * expand_gains[0][:, None] + expand_gains[1][:, None]
    active_one = swish(one_before).reshape(local_channels, HT, WD, segments)
    depth_out = depthwise(active_one, depth_weight).reshape(local_channels, -1)
    two_sums, two_squares = lax.psum(
        (jnp.sum(depth_out, axis=1), jnp.sum(depth_out * depth_out, axis=1)), "dp"
    )
    two_average = two_sums / batch_rows
    two_spread = lax.rsqrt(two_squares / batch_rows - two_average * two_average + norm_epsilon)
    two_normal = (depth_out - two_average[:, None]) * two_spread[:, None]
    two_before = two_normal * depth_gains[0][:, None] + depth_gains[1][:, None]
    active_two = swish(two_before).reshape(local_channels, HT, WD, segments)
    pooled = jnp.mean(active_two, axis=(1, 2))
    squeeze_part = highest(squeeze_weight, pooled, contract_plain)
    squeeze_pre = lax.psum(squeeze_part, "chan") + squeeze_bias[:, None]
    hidden = swish(squeeze_pre)
    gating = jax.nn.sigmoid(highest(excite_weight, hidden, contract_rows) + excite_bias[:, None])
    scaled = (
        (active_two * gating[:, None, None, :]).astype(jnp.bfloat16).reshape(local_channels, -1)
    )
    project_low = project_weight.astype(jnp.bfloat16)
    projected = lax.psum_scatter(
        jnp.dot(project_low, scaled, preferred_element_type=jnp.float32),
        "chan",
        scatter_dimension=0,
        tiled=True,
    )
    three_sums, three_squares = lax.psum(
        (jnp.sum(projected, axis=1), jnp.sum(projected * projected, axis=1)), "dp"
    )
    three_average = three_sums / batch_rows
    three_spread = lax.rsqrt(
        three_squares / batch_rows - three_average * three_average + norm_epsilon
    )
    three_normal = (projected - three_average[:, None]) * three_spread[:, None]
    three_after = three_normal * project_gains[0][:, None] + project_gains[1][:, None]
    own_input = lax.dynamic_slice_in_dim(flattened, position * narrow, narrow, 0).astype(
        jnp.float32
    )
    block_output = (own_input + three_after).astype(jnp.bfloat16).reshape(narrow, HT, WD, segments)
    upstream = cotangent.astype(jnp.float32).reshape(narrow, -1)
    three_beta, three_gamma = lax.psum(
        (jnp.sum(upstream, axis=1), jnp.sum(upstream * three_normal, axis=1)), "dp"
    )
    project_gains_grad = jnp.stack([three_gamma, three_beta])
    three_delta = (project_gains[0] * three_spread)[:, None] * (
        upstream
        - (three_beta / batch_rows)[:, None]
        - three_normal * (three_gamma / batch_rows)[:, None]
    )
    delta_whole = lax.all_gather(three_delta.astype(jnp.bfloat16), "chan", axis=0, tiled=True)
    scaled_grad = lax.dot_general(
        project_low, delta_whole, contract_rows, preferred_element_type=jnp.float32
    )
    project_weight_grad = lax.dot_general(
        delta_whole, scaled, contract_cols, preferred_element_type=jnp.float32
    )
    scaled_four = scaled_grad.reshape(local_channels, HT, WD, segments)
    gating_grad = jnp.sum(scaled_four * active_two, axis=(1, 2))
    excite_delta = gating_grad * gating * (1.0 - gating)
    excite_bias_grad = jnp.sum(excite_delta, axis=1)
    excite_weight_grad = highest(hidden, excite_delta, contract_cols)
    hidden_part = highest(excite_weight, excite_delta, contract_plain)
    hidden_grad = lax.psum(hidden_part, "chan")
    squeeze_delta = hidden_grad * swish_slope(squeeze_pre)
    squeeze_bias_grad = jnp.sum(squeeze_delta, axis=1)
    squeeze_weight_grad = highest(squeeze_delta, pooled, contract_cols)
    pooled_grad = highest(squeeze_weight, squeeze_delta, contract_rows)
    active_grad = scaled_four * gating[:, None, None, :] + pooled_grad[:, None, None, :] / (HT * WD)
    two_delta = active_grad.reshape(local_channels, -1) * swish_slope(two_before)
    two_gamma, two_beta = lax.psum(
        (jnp.sum(two_delta * two_normal, axis=1), jnp.sum(two_delta, axis=1)), "dp"
    )
    depth_gains_grad = jnp.stack([two_gamma, two_beta])
    depth_grad = (depth_gains[0] * two_spread)[:, None] * (
        two_delta
        - (two_beta / batch_rows)[:, None]
        - two_normal * (two_gamma / batch_rows)[:, None]
    )
    active_one_grad, depth_weight_grad = depthwise_back(
        depth_grad.reshape(local_channels, HT, WD, segments), active_one, depth_weight
    )
    one_delta = active_one_grad.reshape(local_channels, -1) * swish_slope(one_before)
    one_gamma, one_beta = lax.psum(
        (jnp.sum(one_delta * one_normal, axis=1), jnp.sum(one_delta, axis=1)), "dp"
    )
    expand_gains_grad = jnp.stack([one_gamma, one_beta])
    expand_delta = (
        (expand_gains[0] * one_spread)[:, None]
        * (
            one_delta
            - (one_beta / batch_rows)[:, None]
            - one_normal * (one_gamma / batch_rows)[:, None]
        )
    ).astype(jnp.bfloat16)
    expand_weight_grad = lax.dot_general(
        expand_delta, flattened, contract_cols, preferred_element_type=jnp.float32
    )
    input_part = lax.psum_scatter(
        lax.dot_general(
            expand_low, expand_delta, contract_rows, preferred_element_type=jnp.float32
        ).astype(jnp.bfloat16),
        "chan",
        scatter_dimension=0,
        tiled=True,
    ).astype(jnp.float32)
    input_grad = (input_part + upstream).reshape(narrow, HT, WD, segments)
    partials = (
        expand_weight_grad,
        depth_weight_grad,
        squeeze_weight_grad,
        excite_weight_grad,
        excite_bias_grad,
        project_weight_grad,
        squeeze_bias_grad,
    )
    gains_square = (
        jnp.sum(expand_gains_grad * expand_gains_grad)
        + jnp.sum(depth_gains_grad * depth_gains_grad)
        + jnp.sum(project_gains_grad * project_gains_grad)
    )
    summed = lax.psum(
        (partials[0], partials[1], partials[2], partials[3], partials[4], partials[5], partials[6]),
        "dp",
    )
    local_square = gains_square + jnp.sum(summed[6] * summed[6]) / shards
    for member in summed[:6]:
        local_square = local_square + jnp.sum(member * member)
    total_square = lax.psum(local_square, "chan")
    grad_norm = jnp.sqrt(total_square)
    factor = clip_limit / jnp.maximum(grad_norm, clip_limit)
    weights = (
        expand_weight,
        expand_gains,
        depth_weight,
        depth_gains,
        squeeze_weight,
        squeeze_bias,
        excite_weight,
        excite_bias,
        project_weight,
        project_gains,
    )
    firsts = (
        expand_weight_first,
        expand_gains_first,
        depth_weight_first,
        depth_gains_first,
        squeeze_weight_first,
        squeeze_bias_first,
        excite_weight_first,
        excite_bias_first,
        project_weight_first,
        project_gains_first,
    )
    seconds = (
        expand_weight_second,
        expand_gains_second,
        depth_weight_second,
        depth_gains_second,
        squeeze_weight_second,
        squeeze_bias_second,
        excite_weight_second,
        excite_bias_second,
        project_weight_second,
        project_gains_second,
    )
    gradients = (
        summed[0],
        expand_gains_grad,
        summed[1],
        depth_gains_grad,
        summed[2],
        summed[6],
        summed[3],
        summed[4],
        summed[5],
        project_gains_grad,
    )
    updated = [
        adam_step(
            weights[entry],
            firsts[entry],
            seconds[entry],
            gradients[entry] * factor,
            step_rates[entry],
            decay_flags[entry],
        )
        for entry in range(10)
    ]
    return (
        block_output,
        input_grad,
        updated[0][0],
        updated[0][1],
        updated[0][2],
        updated[1][0],
        updated[1][1],
        updated[1][2],
        updated[2][0],
        updated[2][1],
        updated[2][2],
        updated[3][0],
        updated[3][1],
        updated[3][2],
        updated[4][0],
        updated[4][1],
        updated[4][2],
        updated[5][0],
        updated[5][1],
        updated[5][2],
        updated[6][0],
        updated[6][1],
        updated[6][2],
        updated[7][0],
        updated[7][1],
        updated[7][2],
        updated[8][0],
        updated[8][1],
        updated[8][2],
        updated[9][0],
        updated[9][1],
        updated[9][2],
        grad_norm,
    )


POSITIONS = HT * WD
HALF_KS = KS // 2
PAIR_LANES = 384
HIDDEN_ROWS = 32
TAPS = KS * KS
ROW_SQUEEZE = 32
ROW_EXCITE = 64
ROW_EXCITE_BIAS = 96
ROW_EXPAND_GAINS = 97
ROW_DEPTH_GAINS = 99
ROW_PROJECT_GAINS = 101
STACK_ROWS = 104
KEEP_BIASES = 64
KEEP_PROJECT = 80
KEEP_KERNEL = 192
KEEP_ROWS = 224
PACKED_ROWS = 96
BLOCK_ROWS = POSITIONS * 8
PAIRED_ROWS_LIMIT = 3072
contract_lanes = (((1,), (1,)), ((), ()))
f32 = jnp.float32
bf16 = jnp.bfloat16


def paired_fits(mesh):
    return mesh.shape["chan"] == 4 and mesh.shape["dp"] * POSITIONS * 8 <= PAIRED_ROWS_LIMIT


def dot(left, right, numbers):
    return lax.dot_general(left, right, numbers, preferred_element_type=f32)


def rows_sum(values):
    return jnp.broadcast_to(jnp.sum(values, axis=0, keepdims=True), (8, values.shape[1]))


def lane_tile(index, start=0):
    if isinstance(start, int):
        return slice(start + index * 128, start + index * 128 + 128)
    return pl.ds(pl.multiple_of(start + index * 128, 128), 128)


def swish_of_half(half):
    return half * jnp.tanh(half) + half


def slope_of_half(half):
    bent = jnp.tanh(half)
    up = 1.0 + bent
    return 0.5 * up * (1.0 + half * (1.0 - bent))


def taps_of(row, col):
    found = []
    for i in range(KS):
        for j in range(KS):
            r, c = row + i - HALF_KS, col + j - HALF_KS
            if 0 <= r < HT and 0 <= c < WD:
                found.append((i * KS + j, r * WD + c))
    return found


def in_order(position, own, near, far, cross):
    first = position % 2 == 0
    front = position // 2 == 0
    low, high = jnp.where(first, own, near), jnp.where(first, near, own)
    far_low, far_high = jnp.where(first, far, cross), jnp.where(first, cross, far)
    return (
        jnp.where(front, low, far_low), jnp.where(front, high, far_high),
        jnp.where(front, far_low, low), jnp.where(front, far_high, high),
    )


def matrix_in_order(position, refs, start, channels):
    parts = in_order(position, *[ref[start : start + channels, :].astype(f32) for ref in refs])
    gap = jnp.zeros((PAIR_LANES - 2 * channels, C_IN), f32)
    return jnp.concatenate([*parts[0:2], gap, *parts[2:4], gap], axis=0).astype(bf16)


def first_kernel(
    index_ref, matrix_0, matrix_1, matrix_2, matrix_3, x_ref,
    expanded_ref, sums_ref, we_ref, packed_ref,
):
    blocks = x_ref.shape[0]
    width = we_ref.shape[0]
    refs = (matrix_0, matrix_1, matrix_2, matrix_3)
    we_ref[...] = matrix_in_order(index_ref[1], refs, 0, matrix_0.shape[0] // 2)
    packed_ref[...] = x_ref[:, BLOCK_ROWS : BLOCK_ROWS + PACKED_ROWS, :]
    for lanes in (slice(at, at + 256) for at in range(0, width, 256)):
        total = jnp.zeros((8, 256), f32)
        square = jnp.zeros((8, 256), f32)
        for block in range(blocks):
            value = dot(x_ref[block, 0:BLOCK_ROWS, :], we_ref[lanes, :], contract_lanes)
            expanded_ref[block, :, lanes] = value
            shaped = value.reshape(POSITIONS, 8, 256)
            total = total + jnp.sum(shaped, axis=0)
            square = square + jnp.sum(shaped * shaped, axis=0)
        sums_ref[0:8, lanes] = total
        sums_ref[8:16, lanes] = square


def norm_factors(total_rows, sums_own, sums_other, gain, shift, norm_ref):
    average = rows_sum(sums_own[0:8] + sums_other[0:8]) / total_rows
    squares = rows_sum(sums_own[8:16] + sums_other[8:16]) / total_rows
    spread = lax.rsqrt(squares - average * average + norm_epsilon)
    gain = gain * spread
    norm_ref[0:8, :] = 0.5 * gain
    norm_ref[8:16, :] = 0.5 * (shift - average * gain)
    norm_ref[16:24, :] = average
    norm_ref[24:32, :] = spread


def expand_kernel(
    total_rows, expanded_ref, sums_own, sums_other, stack_ref, depth_ref, sums_ref, norm_ref, taps_scr
):
    blocks, _, width = expanded_ref.shape
    norm_factors(
        total_rows, sums_own, sums_other, stack_ref[ROW_EXPAND_GAINS : ROW_EXPAND_GAINS + 1, :],
        stack_ref[ROW_EXPAND_GAINS + 1 : ROW_EXPAND_GAINS + 2, :], norm_ref,
    )
    for tap in range(TAPS):
        taps_scr[tap] = jnp.broadcast_to(stack_ref[tap : tap + 1, :], (8, width))
    sums_ref[...] = jnp.zeros_like(sums_ref)

    def one_block(block, carry):
        for tile in range(width // 128):
            lanes = lane_tile(tile)
            gain_half = norm_ref[0:8, lanes]
            shift_half = norm_ref[8:16, lanes]
            active = [
                swish_of_half(expanded_ref[block, 8 * at : 8 * at + 8, lanes] * gain_half + shift_half)
                for at in range(POSITIONS)
            ]
            total = jnp.zeros((8, 128), f32)
            square = jnp.zeros((8, 128), f32)
            for row in range(HT):
                for col in range(WD):
                    at = row * WD + col
                    value = None
                    for tap, source in taps_of(row, col):
                        term = taps_scr[tap, :, lanes] * active[source]
                        value = term if value is None else value + term
                    depth_ref[block, 8 * at : 8 * at + 8, lanes] = value
                    total = total + value
                    square = square + value * value
            sums_ref[0:8, lanes] += total
            sums_ref[8:16, lanes] += square
        return carry

    lax.fori_loop(0, blocks, one_block, 0)


def squeeze_kernel(
    total_rows, depth_ref, sums_own, sums_other, stack_ref, wp_ref, cot_ref, bias_ref,
    projected_ref, scaled_ref, sums_ref, gate_ref, before_ref, pooled_ref, norm_ref, active_ref,
):
    blocks, _, width = depth_ref.shape
    norm_factors(
        total_rows, sums_own, sums_other, stack_ref[ROW_DEPTH_GAINS : ROW_DEPTH_GAINS + 1, :],
        stack_ref[ROW_DEPTH_GAINS + 1 : ROW_DEPTH_GAINS + 2, :], norm_ref,
    )

    def pool_block(block, carry):
        for tile in range(width // 128):
            lanes = lane_tile(tile)
            gain_half = norm_ref[0:8, lanes]
            shift_half = norm_ref[8:16, lanes]
            total = jnp.zeros((8, 128), f32)
            for at in range(POSITIONS):
                value = swish_of_half(
                    depth_ref[block, 8 * at : 8 * at + 8, lanes] * gain_half + shift_half
                )
                active_ref[block, 8 * at : 8 * at + 8, lanes] = value
                total = total + value
            pooled_ref[pl.ds(pl.multiple_of(block * 8, 8), 8), lanes] = total / POSITIONS
        return carry

    lax.fori_loop(0, blocks, pool_block, 0)
    squeeze = stack_ref[ROW_SQUEEZE : ROW_SQUEEZE + HIDDEN_ROWS, :]
    excite = stack_ref[ROW_EXCITE : ROW_EXCITE + HIDDEN_ROWS, :]
    before = highest(pooled_ref[...], squeeze, contract_lanes) + bias_ref[...]
    before_ref[...] = before
    hidden = swish_of_half(0.5 * before)
    raised = highest(hidden, excite, contract_plain)
    raised = raised + stack_ref[ROW_EXCITE_BIAS : ROW_EXCITE_BIAS + 1, :]
    gate_ref[...] = 0.5 + 0.5 * jnp.tanh(0.5 * raised)
    totals = [jnp.zeros((8, C_IN), f32)] * 4
    for block in range(blocks):
        for tile in range(width // 128):
            lanes = lane_tile(tile)
            gate = gate_ref[8 * block : 8 * block + 8, lanes]
            value = active_ref[block, :, lanes].reshape(POSITIONS, 8, 128) * gate[None]
            scaled_ref[block, :, lanes] = value.reshape(BLOCK_ROWS, 128).astype(bf16)
        projected = dot(scaled_ref[block], wp_ref[...], contract_plain)
        projected_ref[block] = projected
        shaped = projected.reshape(POSITIONS, 8, C_IN)
        upstream = cot_ref[block].astype(f32).reshape(POSITIONS, 8, C_IN)
        terms = (shaped, shaped * shaped, shaped * upstream, upstream)
        totals = [total + jnp.sum(term, axis=0) for total, term in zip(totals, terms)]
    for at in range(4):
        sums_ref[8 * at : 8 * at + 8, :] = totals[at]


def gate_back_kernel(
    total_rows, index_ref, projected_ref, cot_ref, sums_own, sums_other, gains_ref, depth_ref,
    norm_ref, stack_ref, wp_ref, gate_ref, before_ref, pooled_ref, scaled_ref, active_ref, x_ref,
    two_ref, sums_ref, lanes_ref, gains_grad_ref, output_ref,
    delta_scr, grad_scr, gate_grad_scr, pooled_scr,
):
    blocks = depth_ref.shape[0]
    width = depth_ref.shape[2]
    own = pl.multiple_of(index_ref[1] // 2 * PAIR_LANES, 128)
    own_lanes = pl.ds(own, PAIR_LANES)
    sums = [rows_sum(sums_own[8 * k : 8 * k + 8] + sums_other[8 * k : 8 * k + 8])[0:1] for k in range(4)]
    average = sums[0] / total_rows
    spread = lax.rsqrt(sums[1] / total_rows - average * average + norm_epsilon)
    beta = sums[3]
    gamma = spread * (sums[2] - average * beta)
    gains_grad_ref[0:1, :] = gamma
    gains_grad_ref[1:2, :] = beta
    gain = gains_ref[0:1, :]
    shift = gains_ref[1:2, :]
    mine = index_ref[0]
    output_ref[...] = (
        x_ref[mine, 0:BLOCK_ROWS, :].astype(f32) + (projected_ref[mine] - average) * spread * gain + shift
    ).astype(output_ref.dtype)
    outer = gain * spread

    for block in range(blocks):
        normal = (projected_ref[block] - average) * spread
        delta = outer * (
            cot_ref[block].astype(f32) - beta / total_rows - normal * (gamma / total_rows)
        )
        delta_scr[block] = delta.astype(bf16)
    for block in range(blocks):
        for lanes in (slice(at, at + 256) for at in range(0, width, 256)):
            value = dot(delta_scr[block], wp_ref[lanes, :], contract_lanes)
            grad_scr[block, :, lanes] = value
            value = (value * active_ref[block, :, lanes]).reshape(POSITIONS, 8, 256)
            gate_grad_scr[8 * block : 8 * block + 8, lanes] = jnp.sum(value, axis=0)
    excite = stack_ref[ROW_EXCITE : ROW_EXCITE + HIDDEN_ROWS, :]
    gate = gate_ref[...]
    gate_grad_scr[...] = gate_grad_scr[...] * gate * (1.0 - gate)
    half = 0.5 * before_ref[...]
    hidden = swish_of_half(half)
    squeeze_delta = highest(gate_grad_scr[...], excite, contract_lanes) * slope_of_half(half)
    own_delta = gate_grad_scr[:, own_lanes]
    lanes_ref[0:HIDDEN_ROWS, :] = highest(squeeze_delta, pooled_ref[:, own_lanes], contract_rows)
    lanes_ref[HIDDEN_ROWS : 2 * HIDDEN_ROWS, :] = highest(hidden, own_delta, contract_rows)
    lanes_ref[KEEP_BIASES : KEEP_BIASES + 8, :] = rows_sum(own_delta)
    lanes_ref[KEEP_BIASES + 8 : KEEP_BIASES + 16, :] = jnp.zeros((8, PAIR_LANES), f32)
    lanes_ref[KEEP_BIASES + 8 : KEEP_BIASES + 16, 0:HIDDEN_ROWS] = rows_sum(squeeze_delta)
    squeeze = stack_ref[ROW_SQUEEZE : ROW_SQUEEZE + HIDDEN_ROWS, own_lanes]
    pooled_scr[...] = highest(squeeze_delta, squeeze, contract_plain) / POSITIONS
    sums_ref[...] = jnp.zeros_like(sums_ref)

    def two_block(block, carry):
        rows = pl.ds(pl.multiple_of(block * 8, 8), 8)
        for tile in range(PAIR_LANES // 128):
            lanes = lane_tile(tile)
            whole = lane_tile(tile, own)
            gain_half = norm_ref[0:8, whole]
            shift_half = norm_ref[8:16, whole]
            average = norm_ref[16:24, whole]
            gate = 0.5 * gate_ref[rows, whole]
            pooled_grad = 0.5 * pooled_scr[rows, lanes]
            total = jnp.zeros((8, 128), f32)
            product = jnp.zeros((8, 128), f32)
            for at in range(POSITIONS):
                spot = slice(8 * at, 8 * at + 8)
                depth = depth_ref[block, spot, whole]
                bent = jnp.tanh(depth * gain_half + shift_half)
                slope = (1.0 + bent) + active_ref[block, spot, whole] * (1.0 - bent)
                value = (grad_scr[block, spot, whole] * gate + pooled_grad) * slope
                two_ref[block, spot, lanes] = value
                total = total + value
                product = product + value * (depth - average)
            sums_ref[0:8, lanes] += total
            sums_ref[8:16, lanes] += product
        return carry

    lax.fori_loop(0, blocks, two_block, 0)
    rows = blocks * POSITIONS * 8
    lanes_ref[KEEP_PROJECT : KEEP_PROJECT + C_IN, :] = dot(
        delta_scr[...].reshape(rows, C_IN), scaled_ref[:, :, own_lanes].reshape(rows, PAIR_LANES), contract_rows
    )


def depth_back_kernel(
    total_rows, index_ref, sums_own, sums_other, two_ref, depth_ref, expanded_ref, stack_ref, lanes_ref,
    norm_one_ref, norm_two_ref,
    one_ref, sums_ref, kernel_ref, gains_grad_ref, taps_scr, kernel_scr, factors_scr,
):
    blocks = depth_ref.shape[0]
    own = pl.multiple_of(index_ref[1] // 2 * PAIR_LANES, 128)
    own_lanes = pl.ds(own, PAIR_LANES)
    spread = norm_two_ref[24:32, own_lanes]
    average = norm_two_ref[16:24, own_lanes]
    beta = rows_sum(sums_own[0:8] + sums_other[0:8])
    gamma = rows_sum(sums_own[8:16] + sums_other[8:16]) * spread
    gains_grad_ref[0:1, :] = gamma[0:1]
    gains_grad_ref[1:2, :] = beta[0:1]
    outer = stack_ref[ROW_DEPTH_GAINS : ROW_DEPTH_GAINS + 1, own_lanes] * spread
    slope = outer * spread * gamma / total_rows
    factors_scr[0:8, :] = outer
    factors_scr[8:16, :] = slope
    factors_scr[16:24, :] = outer * (beta / total_rows)
    for tap in range(TAPS):
        taps_scr[tap] = jnp.broadcast_to(stack_ref[tap : tap + 1, own_lanes], (8, PAIR_LANES))
    sums_ref[...] = jnp.zeros_like(sums_ref)
    kernel_scr[...] = jnp.zeros_like(kernel_scr)

    def one_block(block, carry):
        for tile in range(PAIR_LANES // 128):
            lanes = lane_tile(tile)
            whole = lane_tile(tile, own)
            gain_half = norm_one_ref[0:8, whole]
            shift_half = norm_one_ref[8:16, whole]
            average_one = norm_one_ref[16:24, whole]
            average_two = norm_two_ref[16:24, whole]
            outer = factors_scr[0:8, lanes]
            slope = factors_scr[8:16, lanes]
            level = factors_scr[16:24, lanes]
            grads = []
            active = []
            for at in range(POSITIONS):
                spot = slice(8 * at, 8 * at + 8)
                grads.append(
                    outer * two_ref[block, spot, lanes]
                    - level
                    - slope * (depth_ref[block, spot, whole] - average_two)
                )
                active.append(swish_of_half(expanded_ref[block, spot, whole] * gain_half + shift_half))
            pairs = {}
            for row in range(HT):
                for col in range(WD):
                    for tap, source in taps_of(row, col):
                        pairs.setdefault(tap, []).append((row * WD + col, source))
            for tap in range(TAPS):
                value = None
                for target, source in pairs[tap]:
                    term = grads[target] * active[source]
                    value = term if value is None else value + term
                kernel_scr[tap, :, lanes] += value
            back = {}
            for tap in range(TAPS):
                for target, source in pairs[tap]:
                    back.setdefault(source, []).append((tap, target))
            total = jnp.zeros((8, 128), f32)
            product = jnp.zeros((8, 128), f32)
            for at in range(POSITIONS):
                spot = slice(8 * at, 8 * at + 8)
                value = None
                for tap, target in back[at]:
                    term = taps_scr[tap, :, lanes] * grads[target]
                    value = term if value is None else value + term
                expanded = expanded_ref[block, spot, whole]
                value = value * slope_of_half(expanded * gain_half + shift_half)
                one_ref[block, spot, lanes] = value
                total = total + value
                product = product + value * (expanded - average_one)
            sums_ref[0:8, lanes] += total
            sums_ref[8:16, lanes] += product
        return carry

    lax.fori_loop(0, blocks, one_block, 0)
    kernel_ref[0:KEEP_KERNEL, :] = lanes_ref[...]
    kernel_ref[KEEP_KERNEL : KEEP_KERNEL + 32, :] = jnp.zeros((32, PAIR_LANES), f32)
    for tap in range(TAPS):
        row = KEEP_KERNEL + tap
        kernel_ref[row : row + 1, :] = jnp.sum(kernel_scr[tap], axis=0, keepdims=True)


def expand_back_kernel(
    total_rows, index_ref, sums_own, sums_other, one_ref, expanded_ref, x_ref, we_ref, stack_ref, norm_ref,
    expand_ref, input_ref, gains_grad_ref, delta_scr,
):
    blocks = x_ref.shape[0]
    own = pl.multiple_of(index_ref[1] // 2 * PAIR_LANES, 128)
    own_lanes = pl.ds(own, PAIR_LANES)
    spread = norm_ref[24:32, own_lanes]
    average = norm_ref[16:17, own_lanes]
    beta = rows_sum(sums_own[0:8] + sums_other[0:8])
    gamma = rows_sum(sums_own[8:16] + sums_other[8:16]) * spread
    gains_grad_ref[0:1, :] = gamma[0:1]
    gains_grad_ref[1:2, :] = beta[0:1]
    outer = stack_ref[ROW_EXPAND_GAINS : ROW_EXPAND_GAINS + 1, own_lanes] * spread[0:1]
    slope = outer * spread[0:1] * gamma[0:1] / total_rows
    level = outer * (beta[0:1] / total_rows)
    own_weights = we_ref[own_lanes, :]

    for block in range(blocks):
        centred = expanded_ref[block, :, own_lanes] - average
        delta = outer * one_ref[block] - level - slope * centred
        delta_scr[block] = delta.astype(bf16)
    rows = blocks * POSITIONS * 8
    expand_ref[...] = dot(
        x_ref[:, 0:BLOCK_ROWS, :].reshape(rows, C_IN), delta_scr[...].reshape(rows, PAIR_LANES), contract_rows
    )
    input_ref[...] = dot(delta_scr[index_ref[0]], own_weights, contract_plain)


def one_hot(rows, columns, matches):
    return matches(
        lax.broadcasted_iota(jnp.int32, (rows, columns), 0),
        lax.broadcasted_iota(jnp.int32, (rows, columns), 1),
    )


def copies_kernel(index_ref, rows_ref, cot_ref, copies_ref):
    whole = rows_ref[...].astype(f32)
    half = jnp.where(index_ref[1] % 2 == 0, whole[:, 0:8, :], whole[:, 8:16, :])
    half = half.reshape(BLOCK_ROWS, C_IN).astype(bf16)
    narrow = cot_ref.shape[2]
    rows = cot_ref[...].reshape(4 * PACKED_ROWS, narrow)
    packed = None
    for group in range(4):
        place = one_hot(narrow, C_IN, lambda r, c: c == r + group * narrow).astype(bf16)
        part = dot(rows[group * PACKED_ROWS : (group + 1) * PACKED_ROWS], place, contract_plain)
        packed = part if packed is None else packed + part
    packed = packed.astype(bf16)
    for at in range(copies_ref.shape[0]):
        copies_ref[at, 0:BLOCK_ROWS, :] = half
        copies_ref[at, BLOCK_ROWS : BLOCK_ROWS + PACKED_ROWS, :] = packed


def cot_kernel(index_ref, own_ref, near_ref, far_ref, cross_ref, cot_ref):
    position = index_ref[1]
    first = position % 2 == 0
    near = position + 1 - position % 2 * 2
    blocks = cot_ref.shape[0]
    narrow = C_IN // 4
    rows = blocks * PACKED_ROWS
    pieces = (
        (own_ref, position), (near_ref, near), (far_ref, (position + 2) % 4),
        (cross_ref, (near + 2) % 4),
    )
    for group in range(4):
        total = None
        for ref, place in pieces:
            move = one_hot(
                C_IN,
                C_IN,
                lambda r, c: (c - place * narrow == r - group * narrow)
                & (r >= group * narrow) & (r < (group + 1) * narrow),
            ).astype(bf16)
            part = dot(ref[...].reshape(rows, C_IN), move, contract_plain)
            total = part if total is None else total + part
        total = total.reshape(rows // 16, 16, C_IN)
        half = jnp.where(first, total[:, 0:8, :], total[:, 8:16, :])
        half = half.reshape(blocks, PACKED_ROWS // 2, C_IN).astype(bf16)
        start = group * (PACKED_ROWS // 2)
        cot_ref[:, start : start + PACKED_ROWS // 2, :] = half


def pack_kernel(
    expand_ref, project_ref, depth_ref, squeeze_ref, excite_ref, excite_bias_ref, expand_gains_ref,
    depth_gains_ref, project_gains_ref, stack_ref, matrix_ref,
):
    channels = expand_ref.shape[0]
    narrow = project_gains_ref.shape[1]
    stack_ref[...] = jnp.zeros_like(stack_ref)
    for start, ref in (
        (0, depth_ref), (ROW_SQUEEZE, squeeze_ref), (ROW_EXCITE, excite_ref),
        (ROW_EXCITE_BIAS, excite_bias_ref), (ROW_EXPAND_GAINS, expand_gains_ref),
        (ROW_DEPTH_GAINS, depth_gains_ref),
    ):
        stack_ref[start : start + ref.shape[0], :] = ref[...]
    stack_ref[ROW_PROJECT_GAINS : ROW_PROJECT_GAINS + 2, 0:narrow] = project_gains_ref[...]
    matrix_ref[...] = jnp.concatenate(
        [expand_ref[...], project_ref[...]], axis=0
    ).astype(bf16)


def assemble_kernel(
    index_ref, stack_0, stack_1, stack_2, stack_3, matrix_0, matrix_1, matrix_2, matrix_3,
    after_ref, stack_ref, project_ref, gains_ref,
):
    channels = stack_0.shape[1]
    narrow = C_IN // 4
    stacks = in_order(index_ref[1], stack_0[...], stack_1[...], stack_2[...], stack_3[...])
    stack_ref[...] = jnp.zeros_like(stack_ref)
    for place in range(4):
        start = place // 2 * PAIR_LANES + place % 2 * channels
        stack_ref[:, start : start + channels] = stacks[place]
        gains_ref[:, place * narrow : (place + 1) * narrow] = stacks[place][
            ROW_PROJECT_GAINS : ROW_PROJECT_GAINS + 2, 0:narrow
        ]
    refs = (matrix_0, matrix_1, matrix_2, matrix_3)
    project_ref[...] = matrix_in_order(index_ref[1], refs, channels, channels)


def settle_kernel(
    index_ref, expand_own, expand_other, keep_own, keep_other, three_ref, two_ref, one_ref,
    input_own, input_other,
    expand_ref, project_ref, lanes_ref, bias_ref, square_ref, input_ref, packed_ref,
):
    position = index_ref[1]
    first = position % 2 == 0
    channels = expand_ref.shape[0]
    narrow = C_IN // 4

    def squared(values):
        return jnp.sum(jnp.sum(values * values, axis=0, keepdims=True), axis=1, keepdims=True)

    def mine(values):
        return jnp.where(first, values[:, 0:channels], values[:, channels : 2 * channels])

    def both(start, stop):
        return keep_own[start:stop, :] + keep_other[start:stop, :]

    expand = expand_own[...] + expand_other[...]
    project = both(KEEP_PROJECT, KEEP_PROJECT + C_IN)
    hidden = both(0, 2 * HIDDEN_ROWS)
    excite_bias = both(KEEP_BIASES, KEEP_BIASES + 1)
    kernel = both(KEEP_KERNEL, KEEP_KERNEL + 32)
    total = squared(expand) + squared(project) + squared(hidden) + squared(kernel)
    total = total + squared(excite_bias) + squared(one_ref[...]) + squared(two_ref[...])
    bias = both(KEEP_BIASES + 8, KEEP_BIASES + 9)[:, 0:HIDDEN_ROWS]
    square_ref[0:8, :] = jnp.broadcast_to(total, (8, 128))
    square_ref[8:16, :] = jnp.broadcast_to(squared(bias) + squared(three_ref[...]), (8, 128))
    bias_ref[...] = bias
    expand_ref[...] = jnp.transpose(mine(expand))
    project_ref[...] = jnp.transpose(mine(project))
    lanes_ref[0:32, :] = mine(kernel)
    lanes_ref[ROW_SQUEEZE : ROW_SQUEEZE + 2 * HIDDEN_ROWS, :] = mine(hidden)
    lanes_ref[ROW_EXCITE_BIAS : ROW_EXCITE_BIAS + 1, :] = mine(excite_bias)
    lanes_ref[ROW_EXPAND_GAINS : ROW_EXPAND_GAINS + 2, :] = mine(one_ref[...])
    lanes_ref[ROW_DEPTH_GAINS : ROW_DEPTH_GAINS + 2, :] = mine(two_ref[...])
    own = input_own[...].reshape(POSITIONS, 8, C_IN)
    other = input_other[...].reshape(POSITIONS, 8, C_IN)
    whole = jnp.concatenate(
        [jnp.where(first, own, other), jnp.where(first, other, own)], axis=1
    ).reshape(4 * PACKED_ROWS, C_IN)
    pick = one_hot(C_IN, narrow, lambda r, c: r == c + position * narrow).astype(f32)
    input_ref[...] = highest(whole, pick, contract_plain).reshape(POSITIONS, 16, narrow)
    across = position + 2 - position // 2 * 4
    low = whole.astype(bf16)
    packed = None
    for group in range(4):
        move = one_hot(
            C_IN,
            C_IN,
            lambda r, c: (r - across * narrow == c - group * narrow)
            & (c >= group * narrow) & (c < (group + 1) * narrow),
        ).astype(bf16)
        part = dot(low[group * PACKED_ROWS : (group + 1) * PACKED_ROWS], move, contract_plain)
        packed = part if packed is None else packed + part
    packed_ref[...] = packed.astype(bf16)


def output_kernel(index_ref, own_ref, other_ref, output_ref):
    first = index_ref[1] % 2 == 0
    narrow = output_ref.shape[2]
    pick = one_hot(C_IN, narrow, lambda r, c: r == c + index_ref[1] * narrow).astype(bf16)
    own = dot(own_ref[...], pick, contract_plain).reshape(POSITIONS, 8, narrow)
    other = dot(other_ref[...], pick, contract_plain).reshape(POSITIONS, 8, narrow)
    output_ref[...] = jnp.concatenate(
        [jnp.where(first, own, other), jnp.where(first, other, own)], axis=1
    ).astype(bf16)


def adam_kernel(
    index_ref, square_own, square_other, expand_grad, project_grad, lanes_grad, bias_grad, three_grad,
    input_own, packed_other, cot_ref, *refs,
):
    params, outs = refs[:30], refs[30:]
    narrow = cot_ref.shape[2]
    total = square_own[0:1, 0:1] + square_other[0:1, 0:1] + square_own[8:9, 0:1]
    grad_norm = jnp.sqrt(total)
    factor = clip_limit / jnp.maximum(grad_norm, clip_limit)
    outs[31][...] = grad_norm
    groups = []
    for group in range(4):
        pick = one_hot(C_IN, narrow, lambda r, c: r == c + group * narrow).astype(bf16)
        groups.append(dot(packed_other[...], pick, contract_plain))
    crossed = jnp.concatenate(groups, axis=0).reshape(POSITIONS, 16, narrow)
    outs[0][...] = input_own[...] + crossed + cot_ref[...].astype(f32)
    pick = one_hot(C_IN, narrow, lambda r, c: r == c + index_ref[1] * narrow).astype(f32)
    gradients = (
        expand_grad[...],
        lanes_grad[ROW_EXPAND_GAINS : ROW_EXPAND_GAINS + 2, :],
        lanes_grad[0:TAPS, :],
        lanes_grad[ROW_DEPTH_GAINS : ROW_DEPTH_GAINS + 2, :],
        lanes_grad[ROW_SQUEEZE : ROW_SQUEEZE + params[12].shape[0], :],
        bias_grad[:, 0 : params[15].shape[1]],
        lanes_grad[ROW_EXCITE : ROW_EXCITE + params[18].shape[0], :],
        lanes_grad[ROW_EXCITE_BIAS : ROW_EXCITE_BIAS + 1, :],
        project_grad[...],
        highest(three_grad[0:2, :], pick, contract_plain),
    )
    for entry in range(10):
        updated = adam_step(
            params[3 * entry][...],
            params[3 * entry + 1][...],
            params[3 * entry + 2][...],
            gradients[entry] * factor,
            step_rates[entry],
            decay_flags[entry],
        )
        for part in range(3):
            outs[1 + 3 * entry + part][...] = updated[part]


def call(kernel, outs, operands, scratch=(), name=None, keep=True, place=True):
    spaces = [
        pl.BlockSpec(memory_space=pltpu.SMEM)
        if operand.dtype == jnp.int32
        else pl.BlockSpec(memory_space=pltpu.VMEM)
        for operand in operands
    ]
    operands = [
        operand
        if operand.dtype == jnp.int32
        else pltpu.with_memory_space_constraint(operand, pltpu.VMEM if place else pltpu.HBM)
        for operand in operands
    ]
    limit = 4 * 1024 * 1024 + sum(4 * math.prod(shape) for shape, _ in scratch)
    made = pltpu.VMEM if keep else jax.ShapeDtypeStruct
    return pl.pallas_call(
        kernel,
        out_shape=[made(shape, dtype) for shape, dtype in outs],
        in_specs=spaces,
        out_specs=[pl.BlockSpec(memory_space=pltpu.VMEM)] * len(outs),
        scratch_shapes=[pltpu.VMEM(shape, dtype) for shape, dtype in scratch],
        compiler_params=pltpu.CompilerParams(vmem_limit_bytes=limit),
        name=name,
    )(*operands)


def on_device_paired(*arrays):
    block_input, cotangent = arrays[:2]
    segments = block_input.shape[3]
    if segments != 16:
        return on_device(*arrays)
    params = list(arrays[2:])
    for at in (15, 16, 17, 21, 22, 23):
        params[at] = params[at][None]
    for at in (24, 25, 26):
        params[at] = params[at].T
    (
        expand_weight, expand_gains, depth_weight, depth_gains, squeeze_weight,
        squeeze_bias, excite_weight, excite_bias, project_weight, project_gains,
    ) = params[::3]
    shards = lax.axis_size("dp")
    index = jnp.stack([lax.axis_index("dp"), lax.axis_index("chan")]).astype(jnp.int32)
    total_rows = float(POSITIONS * segments * shards)
    narrow = cotangent.shape[0]
    channels = expand_weight.shape[0]
    rows = POSITIONS * 8
    width = 2 * PAIR_LANES

    def swap(values, mask):
        return lax.ppermute(values, "chan", [(at, at ^ mask) for at in range(4)])

    input_rows = jnp.transpose(block_input, (1, 2, 3, 0)).reshape(POSITIONS, segments, C_IN)
    cot_rows = jnp.transpose(cotangent, (1, 2, 3, 0)).reshape(POSITIONS, segments, narrow)
    (copies,) = call(
        copies_kernel,
        [((shards, rows + PACKED_ROWS, C_IN), bf16)],
        [index, input_rows, cot_rows],
        name="copies",
        keep=False,
        place=False,
    )
    x = lax.all_to_all(copies, "dp", 0, 0)
    stack, matrix = call(
        pack_kernel,
        [((STACK_ROWS, channels), f32), ((2 * channels, C_IN), bf16)],
        [
            expand_weight, project_weight, depth_weight, squeeze_weight, excite_weight, excite_bias,
            expand_gains, depth_gains, project_gains,
        ],
        name="pack",
        keep=False,
        place=False,
    )
    stack_far, matrix_far = swap(stack, 2), swap(matrix, 2)
    pieces = [
        stack, swap(stack, 1), stack_far, swap(stack_far, 1),
        matrix, swap(matrix, 1), matrix_far, swap(matrix_far, 1),
    ]
    expanded, sums_one, expand_all, packed = call(
        first_kernel,
        [
            ((shards, rows, width), f32),
            ((16, width), f32),
            ((width, C_IN), bf16),
            ((shards, PACKED_ROWS, C_IN), bf16),
        ],
        [index, *pieces[4:], x],
        name="first",
    )
    stack_all, project_all, gains_all = call(
        assemble_kernel,
        [((STACK_ROWS, width), f32), ((width, C_IN), bf16), ((2, C_IN), f32)],
        [index, *pieces, packed],
        name="assemble",
    )
    (cot,) = call(
        cot_kernel,
        [((shards, rows, C_IN), bf16)],
        [index, packed, swap(packed, 1), swap(packed, 2), swap(packed, 3)],
        name="cot",
    )
    bias_row = jnp.pad(squeeze_bias, ((0, 0), (0, HIDDEN_ROWS - squeeze_bias.shape[1])))

    depth, sums, norm_one = call(
        functools.partial(expand_kernel, total_rows),
        [((shards, rows, width), f32), ((16, width), f32), ((32, width), f32)],
        [expanded, sums_one, swap(sums_one, 1), stack_all],
        [((TAPS, 8, width), f32)],
        name="expand",
    )
    projected, scaled, sums, gate, before, pooled, norm_two, active = call(
        functools.partial(squeeze_kernel, total_rows),
        [
            ((shards, rows, C_IN), f32),
            ((shards, rows, width), bf16),
            ((32, C_IN), f32),
            ((shards * 8, width), f32),
            ((shards * 8, HIDDEN_ROWS), f32),
            ((shards * 8, width), f32),
            ((32, width), f32),
            ((shards, rows, width), f32),
        ],
        [depth, sums, swap(sums, 1), stack_all, project_all, cot, bias_row],
        name="squeeze",
    )
    two, sums, lanes_grad, three_grad, output = call(
        functools.partial(gate_back_kernel, total_rows),
        [
            ((shards, rows, PAIR_LANES), f32),
            ((16, PAIR_LANES), f32),
            ((KEEP_KERNEL, PAIR_LANES), f32),
            ((2, C_IN), f32),
            ((rows, C_IN), bf16),
        ],
        [
            index, projected, cot, sums, swap(sums, 1), gains_all, depth, norm_two, stack_all,
            project_all, gate, before, pooled, scaled, active, x,
        ],
        [
            ((shards, rows, C_IN), bf16),
            ((shards, rows, width), f32),
            ((shards * 8, width), f32),
            ((shards * 8, PAIR_LANES), f32),
        ],
        name="gate_back",
    )
    one, sums, keep, two_grad = call(
        functools.partial(depth_back_kernel, total_rows),
        [
            ((shards, rows, PAIR_LANES), f32),
            ((16, PAIR_LANES), f32),
            ((KEEP_ROWS, PAIR_LANES), f32),
            ((2, PAIR_LANES), f32),
        ],
        [
            index, sums, swap(sums, 1), two, depth, expanded, stack_all, lanes_grad,
            norm_one, norm_two,
        ],
        [
            ((TAPS, 8, PAIR_LANES), f32),
            ((TAPS, 8, PAIR_LANES), f32),
            ((24, PAIR_LANES), f32),
        ],
        name="depth_back",
    )
    expand_grad, input_part, one_grad = call(
        functools.partial(expand_back_kernel, total_rows),
        [((C_IN, PAIR_LANES), f32), ((rows, C_IN), f32), ((2, PAIR_LANES), f32)],
        [index, sums, swap(sums, 1), one, expanded, x, expand_all, stack_all, norm_one],
        [((shards, rows, PAIR_LANES), bf16)],
        name="expand_back",
    )
    expand_own, project_own, lanes_own, bias_own, square, input_own, packed = call(
        settle_kernel,
        [
            ((channels, C_IN), f32),
            ((channels, C_IN), f32),
            ((STACK_ROWS, channels), f32),
            ((1, HIDDEN_ROWS), f32),
            ((16, 128), f32),
            ((POSITIONS, segments, narrow), f32),
            ((PACKED_ROWS, C_IN), bf16),
        ],
        [
            index, expand_grad, swap(expand_grad, 1), keep, swap(keep, 1), three_grad, two_grad,
            one_grad, input_part, swap(input_part, 1),
        ],
        name="settle",
    )
    (block_output,) = call(
        output_kernel,
        [((POSITIONS, segments, narrow), bf16)],
        [index, output, swap(output, 1)],
        name="output",
        keep=False,
    )
    updated = call(
        adam_kernel,
        [((POSITIONS, segments, narrow), f32)]
        + [(value.shape, f32) for value in params]
        + [((1, 1), f32)],
        [
            index, square, swap(square, 2), expand_own, project_own, lanes_own, bias_own, three_grad,
            input_own, swap(packed, 2), cot_rows, *params,
        ],
        name="adam",
        keep=False,
    )
    results = [block_output] + list(updated)
    for at in (0, 1):
        results[at] = jnp.transpose(results[at].reshape(HT, WD, segments, narrow), (3, 0, 1, 2))
    for at in (17, 18, 19, 23, 24, 25):
        results[at] = results[at][0]
    for at in (26, 27, 28):
        results[at] = results[at].T
    results[32] = results[32][0, 0]
    return tuple(results)


def solution(mesh):
    body = on_device_paired if paired_fits(mesh) else on_device
    return jax.shard_map(
        body,
        mesh=mesh,
        in_specs=(
            P(None, None, None, "dp"),
            P("chan", None, None, "dp"),
            P("chan", None),
            P("chan", None),
            P("chan", None),
            P(None, "chan"),
            P(None, "chan"),
            P(None, "chan"),
            P(None, "chan"),
            P(None, "chan"),
            P(None, "chan"),
            P(None, "chan"),
            P(None, "chan"),
            P(None, "chan"),
            P(None, "chan"),
            P(None, "chan"),
            P(None, "chan"),
            P(),
            P(),
            P(),
            P(None, "chan"),
            P(None, "chan"),
            P(None, "chan"),
            P("chan"),
            P("chan"),
            P("chan"),
            P(None, "chan"),
            P(None, "chan"),
            P(None, "chan"),
            P(None, "chan"),
            P(None, "chan"),
            P(None, "chan"),
        ),
        out_specs=(
            P("chan", None, None, "dp"),
            P("chan", None, None, "dp"),
            P("chan", None),
            P("chan", None),
            P("chan", None),
            P(None, "chan"),
            P(None, "chan"),
            P(None, "chan"),
            P(None, "chan"),
            P(None, "chan"),
            P(None, "chan"),
            P(None, "chan"),
            P(None, "chan"),
            P(None, "chan"),
            P(None, "chan"),
            P(None, "chan"),
            P(None, "chan"),
            P(),
            P(),
            P(),
            P(None, "chan"),
            P(None, "chan"),
            P(None, "chan"),
            P("chan"),
            P("chan"),
            P("chan"),
            P(None, "chan"),
            P(None, "chan"),
            P(None, "chan"),
            P(None, "chan"),
            P(None, "chan"),
            P(None, "chan"),
            P(),
        ),
        check_vma=False,
    )
```

```python
import functools
import math

import jax
import jax.numpy as jnp
from jax import lax
from jax.experimental import pallas as pl
from jax.experimental.pallas import tpu as pltpu
from jax.sharding import PartitionSpec as P

C_IN = 112
KS = 5
HT = 6
WD = 4
STEP = 10


norm_epsilon = 1e-05
beta_first = 0.9
beta_second = 0.999
adam_epsilon = 1e-08
decay_rate = 0.01
clip_limit = 1.0
step_rates = (0.3, 0.6, 0.6, 0.6, 0.12, 0.6, 0.6, 0.6, 0.12, 0.6)
decay_flags = (1.0, 0.0, 1.0, 0.0, 1.0, 0.0, 1.0, 0.0, 1.0, 0.0)
contract_rows = (((0,), (0,)), ((), ()))
contract_cols = (((1,), (1,)), ((), ()))
contract_plain = (((1,), (0,)), ((), ()))


def swish(values):
    return values * jax.nn.sigmoid(values)


def swish_slope(values):
    logistic = jax.nn.sigmoid(values)
    return logistic * (1.0 + values * (1.0 - logistic))


def highest(left, right, numbers):
    return lax.dot_general(
        left, right, numbers, precision=lax.Precision.HIGHEST, preferred_element_type=jnp.float32
    )


def depthwise(activity, kernel):
    half = KS // 2
    padded = jnp.pad(activity, ((0, 0), (half, half), (half, half), (0, 0)))
    result = jnp.zeros_like(activity)
    for row_shift in range(KS):
        for col_shift in range(KS):
            window = padded[:, row_shift : row_shift + HT, col_shift : col_shift + WD, :]
            result = result + kernel[row_shift * KS + col_shift][:, None, None, None] * window
    return result


def depthwise_back(grad_field, activity, kernel):
    half = KS // 2
    padded = jnp.pad(activity, ((0, 0), (half, half), (half, half), (0, 0)))
    grad_padded = jnp.pad(grad_field, ((0, 0), (half, half), (half, half), (0, 0)))
    activity_grad = jnp.zeros_like(activity)
    kernel_rows = []
    for row_shift in range(KS):
        for col_shift in range(KS):
            window = padded[:, row_shift : row_shift + HT, col_shift : col_shift + WD, :]
            kernel_rows.append(jnp.sum(grad_field * window, axis=(1, 2, 3)))
            back_window = grad_padded[
                :,
                2 * half - row_shift : 2 * half - row_shift + HT,
                2 * half - col_shift : 2 * half - col_shift + WD,
                :,
            ]
            activity_grad = (
                activity_grad
                + kernel[row_shift * KS + col_shift][:, None, None, None] * back_window
            )
    return (activity_grad, jnp.stack(kernel_rows))


def adam_step(weight, first_moment, second, gradient, step_rate, decay_flag):
    first_new = beta_first * first_moment + (1.0 - beta_first) * gradient
    second_new = beta_second * second + (1.0 - beta_second) * gradient * gradient
    first_hat = first_new / (1.0 - beta_first**STEP)
    second_hat = second_new / (1.0 - beta_second**STEP)
    weight_new = weight - step_rate * (
        first_hat / (jnp.sqrt(second_hat) + adam_epsilon) + decay_flag * decay_rate * weight
    )
    return (weight_new, first_new, second_new)


def on_device(
    block_input,
    cotangent,
    expand_weight,
    expand_weight_first,
    expand_weight_second,
    expand_gains,
    expand_gains_first,
    expand_gains_second,
    depth_weight,
    depth_weight_first,
    depth_weight_second,
    depth_gains,
    depth_gains_first,
    depth_gains_second,
    squeeze_weight,
    squeeze_weight_first,
    squeeze_weight_second,
    squeeze_bias,
    squeeze_bias_first,
    squeeze_bias_second,
    excite_weight,
    excite_weight_first,
    excite_weight_second,
    excite_bias,
    excite_bias_first,
    excite_bias_second,
    project_weight,
    project_weight_first,
    project_weight_second,
    project_gains,
    project_gains_first,
    project_gains_second,
):
    shards = lax.axis_size("chan")
    position = lax.axis_index("chan")
    segments = block_input.shape[3]
    batch_rows = HT * WD * segments * lax.axis_size("dp")
    narrow = cotangent.shape[0]
    local_channels = expand_weight.shape[0]
    flattened = block_input.reshape(C_IN, -1)
    expand_low = expand_weight.astype(jnp.bfloat16)
    expanded = jnp.dot(expand_low, flattened, preferred_element_type=jnp.float32)
    one_sums, one_squares = lax.psum(
        (jnp.sum(expanded, axis=1), jnp.sum(expanded * expanded, axis=1)), "dp"
    )
    one_average = one_sums / batch_rows
    one_spread = lax.rsqrt(one_squares / batch_rows - one_average * one_average + norm_epsilon)
    one_normal = (expanded - one_average[:, None]) * one_spread[:, None]
    one_before = one_normal * expand_gains[0][:, None] + expand_gains[1][:, None]
    active_one = swish(one_before).reshape(local_channels, HT, WD, segments)
    depth_out = depthwise(active_one, depth_weight).reshape(local_channels, -1)
    two_sums, two_squares = lax.psum(
        (jnp.sum(depth_out, axis=1), jnp.sum(depth_out * depth_out, axis=1)), "dp"
    )
    two_average = two_sums / batch_rows
    two_spread = lax.rsqrt(two_squares / batch_rows - two_average * two_average + norm_epsilon)
    two_normal = (depth_out - two_average[:, None]) * two_spread[:, None]
    two_before = two_normal * depth_gains[0][:, None] + depth_gains[1][:, None]
    active_two = swish(two_before).reshape(local_channels, HT, WD, segments)
    pooled = jnp.mean(active_two, axis=(1, 2))
    squeeze_part = highest(squeeze_weight, pooled, contract_plain)
    squeeze_pre = lax.psum(squeeze_part, "chan") + squeeze_bias[:, None]
    hidden = swish(squeeze_pre)
    gating = jax.nn.sigmoid(highest(excite_weight, hidden, contract_rows) + excite_bias[:, None])
    scaled = (
        (active_two * gating[:, None, None, :]).astype(jnp.bfloat16).reshape(local_channels, -1)
    )
    project_low = project_weight.astype(jnp.bfloat16)
    projected = lax.psum_scatter(
        jnp.dot(project_low, scaled, preferred_element_type=jnp.float32),
        "chan",
        scatter_dimension=0,
        tiled=True,
    )
    three_sums, three_squares = lax.psum(
        (jnp.sum(projected, axis=1), jnp.sum(projected * projected, axis=1)), "dp"
    )
    three_average = three_sums / batch_rows
    three_spread = lax.rsqrt(
        three_squares / batch_rows - three_average * three_average + norm_epsilon
    )
    three_normal = (projected - three_average[:, None]) * three_spread[:, None]
    three_after = three_normal * project_gains[0][:, None] + project_gains[1][:, None]
    own_input = lax.dynamic_slice_in_dim(flattened, position * narrow, narrow, 0).astype(
        jnp.float32
    )
    block_output = (own_input + three_after).astype(jnp.bfloat16).reshape(narrow, HT, WD, segments)
    upstream = cotangent.astype(jnp.float32).reshape(narrow, -1)
    three_beta, three_gamma = lax.psum(
        (jnp.sum(upstream, axis=1), jnp.sum(upstream * three_normal, axis=1)), "dp"
    )
    project_gains_grad = jnp.stack([three_gamma, three_beta])
    three_delta = (project_gains[0] * three_spread)[:, None] * (
        upstream
        - (three_beta / batch_rows)[:, None]
        - three_normal * (three_gamma / batch_rows)[:, None]
    )
    delta_whole = lax.all_gather(three_delta.astype(jnp.bfloat16), "chan", axis=0, tiled=True)
    scaled_grad = lax.dot_general(
        project_low, delta_whole, contract_rows, preferred_element_type=jnp.float32
    )
    project_weight_grad = lax.dot_general(
        delta_whole, scaled, contract_cols, preferred_element_type=jnp.float32
    )
    scaled_four = scaled_grad.reshape(local_channels, HT, WD, segments)
    gating_grad = jnp.sum(scaled_four * active_two, axis=(1, 2))
    excite_delta = gating_grad * gating * (1.0 - gating)
    excite_bias_grad = jnp.sum(excite_delta, axis=1)
    excite_weight_grad = highest(hidden, excite_delta, contract_cols)
    hidden_part = highest(excite_weight, excite_delta, contract_plain)
    hidden_grad = lax.psum(hidden_part, "chan")
    squeeze_delta = hidden_grad * swish_slope(squeeze_pre)
    squeeze_bias_grad = jnp.sum(squeeze_delta, axis=1)
    squeeze_weight_grad = highest(squeeze_delta, pooled, contract_cols)
    pooled_grad = highest(squeeze_weight, squeeze_delta, contract_rows)
    active_grad = scaled_four * gating[:, None, None, :] + pooled_grad[:, None, None, :] / (HT * WD)
    two_delta = active_grad.reshape(local_channels, -1) * swish_slope(two_before)
    two_gamma, two_beta = lax.psum(
        (jnp.sum(two_delta * two_normal, axis=1), jnp.sum(two_delta, axis=1)), "dp"
    )
    depth_gains_grad = jnp.stack([two_gamma, two_beta])
    depth_grad = (depth_gains[0] * two_spread)[:, None] * (
        two_delta
        - (two_beta / batch_rows)[:, None]
        - two_normal * (two_gamma / batch_rows)[:, None]
    )
    active_one_grad, depth_weight_grad = depthwise_back(
        depth_grad.reshape(local_channels, HT, WD, segments), active_one, depth_weight
    )
    one_delta = active_one_grad.reshape(local_channels, -1) * swish_slope(one_before)
    one_gamma, one_beta = lax.psum(
        (jnp.sum(one_delta * one_normal, axis=1), jnp.sum(one_delta, axis=1)), "dp"
    )
    expand_gains_grad = jnp.stack([one_gamma, one_beta])
    expand_delta = (
        (expand_gains[0] * one_spread)[:, None]
        * (
            one_delta
            - (one_beta / batch_rows)[:, None]
            - one_normal * (one_gamma / batch_rows)[:, None]
        )
    ).astype(jnp.bfloat16)
    expand_weight_grad = lax.dot_general(
        expand_delta, flattened, contract_cols, preferred_element_type=jnp.float32
    )
    input_part = lax.psum_scatter(
        lax.dot_general(
            expand_low, expand_delta, contract_rows, preferred_element_type=jnp.float32
        ).astype(jnp.bfloat16),
        "chan",
        scatter_dimension=0,
        tiled=True,
    ).astype(jnp.float32)
    input_grad = (input_part + upstream).reshape(narrow, HT, WD, segments)
    partials = (
        expand_weight_grad,
        depth_weight_grad,
        squeeze_weight_grad,
        excite_weight_grad,
        excite_bias_grad,
        project_weight_grad,
        squeeze_bias_grad,
    )
    gains_square = (
        jnp.sum(expand_gains_grad * expand_gains_grad)
        + jnp.sum(depth_gains_grad * depth_gains_grad)
        + jnp.sum(project_gains_grad * project_gains_grad)
    )
    summed = lax.psum(
        (partials[0], partials[1], partials[2], partials[3], partials[4], partials[5], partials[6]),
        "dp",
    )
    local_square = gains_square + jnp.sum(summed[6] * summed[6]) / shards
    for member in summed[:6]:
        local_square = local_square + jnp.sum(member * member)
    total_square = lax.psum(local_square, "chan")
    grad_norm = jnp.sqrt(total_square)
    factor = clip_limit / jnp.maximum(grad_norm, clip_limit)
    weights = (
        expand_weight,
        expand_gains,
        depth_weight,
        depth_gains,
        squeeze_weight,
        squeeze_bias,
        excite_weight,
        excite_bias,
        project_weight,
        project_gains,
    )
    firsts = (
        expand_weight_first,
        expand_gains_first,
        depth_weight_first,
        depth_gains_first,
        squeeze_weight_first,
        squeeze_bias_first,
        excite_weight_first,
        excite_bias_first,
        project_weight_first,
        project_gains_first,
    )
    seconds = (
        expand_weight_second,
        expand_gains_second,
        depth_weight_second,
        depth_gains_second,
        squeeze_weight_second,
        squeeze_bias_second,
        excite_weight_second,
        excite_bias_second,
        project_weight_second,
        project_gains_second,
    )
    gradients = (
        summed[0],
        expand_gains_grad,
        summed[1],
        depth_gains_grad,
        summed[2],
        summed[6],
        summed[3],
        summed[4],
        summed[5],
        project_gains_grad,
    )
    updated = [
        adam_step(
            weights[entry],
            firsts[entry],
            seconds[entry],
            gradients[entry] * factor,
            step_rates[entry],
            decay_flags[entry],
        )
        for entry in range(10)
    ]
    return (
        block_output,
        input_grad,
        updated[0][0],
        updated[0][1],
        updated[0][2],
        updated[1][0],
        updated[1][1],
        updated[1][2],
        updated[2][0],
        updated[2][1],
        updated[2][2],
        updated[3][0],
        updated[3][1],
        updated[3][2],
        updated[4][0],
        updated[4][1],
        updated[4][2],
        updated[5][0],
        updated[5][1],
        updated[5][2],
        updated[6][0],
        updated[6][1],
        updated[6][2],
        updated[7][0],
        updated[7][1],
        updated[7][2],
        updated[8][0],
        updated[8][1],
        updated[8][2],
        updated[9][0],
        updated[9][1],
        updated[9][2],
        grad_norm,
    )


POSITIONS = HT * WD
HALF_KS = KS // 2
PAIR_LANES = 384
HIDDEN_ROWS = 32
TAPS = KS * KS
ROW_SQUEEZE = 32
ROW_EXCITE = 64
ROW_EXCITE_BIAS = 96
ROW_EXPAND_GAINS = 97
ROW_DEPTH_GAINS = 99
ROW_PROJECT_GAINS = 101
STACK_ROWS = 104
KEEP_BIASES = 64
KEEP_PROJECT = 80
KEEP_ROWS = 192
PACKED_ROWS = 96
BLOCK_ROWS = POSITIONS * 8
SENT_ROWS = 256
TAIL_ROWS = BLOCK_ROWS + PACKED_ROWS - SENT_ROWS
TAIL_LANES = 128 - C_IN
PAIRED_ROWS_LIMIT = 3072
contract_lanes = (((1,), (1,)), ((), ()))
f32 = jnp.float32
bf16 = jnp.bfloat16


def paired_fits(mesh):
    return mesh.shape["chan"] == 4 and mesh.shape["dp"] * POSITIONS * 8 <= PAIRED_ROWS_LIMIT


def dot(left, right, numbers):
    return lax.dot_general(left, right, numbers, preferred_element_type=f32)


def rows_sum(values):
    return jnp.broadcast_to(jnp.sum(values, axis=0, keepdims=True), (8, values.shape[1]))


def lane_tile(index, start=0):
    if isinstance(start, int):
        return slice(start + index * 128, start + index * 128 + 128)
    return pl.ds(pl.multiple_of(start + index * 128, 128), 128)


def swish_of_half(half):
    return half * jnp.tanh(half) + half


def slope_of_half(half):
    bent = jnp.tanh(half)
    up = 1.0 + bent
    return 0.5 * up * (1.0 + half * (1.0 - bent))


PRODUCTS = 9
FILTER_SIGNS = (
    ((2, 1),),
    ((3, 1), (2, -1)),
    ((1, 1), (2, -1)),
    ((4, 1), (2, -1)),
    ((2, 1), (3, -1), (4, -1)),
    ((2, 1), (3, 1), (1, -1), (4, -1)),
    ((0, 1), (2, -1)),
    ((2, 1), (1, 1), (3, -1), (0, -1)),
    ((2, 1), (1, -1), (0, -1)),
)


def signed(terms):
    total = None
    for value, sign in terms:
        if total is None:
            total = value if sign > 0 else -value
        else:
            total = total + value if sign > 0 else total - value
    return total


def product_filters(taps, out_ref):
    for i in range(KS):
        for at, signs in enumerate(FILTER_SIGNS):
            value = signed([(taps(i, column), sign) for column, sign in signs])
            out_ref[i * PRODUCTS + at] = jnp.broadcast_to(value, out_ref.shape[1:])


def product_inputs(field):
    rows = []
    for row in range(HT):
        x0, x1, x2, x3 = field[row * WD : row * WD + WD]
        even, odd = x0 + x2, x1 + x3
        rows.append((even + odd, odd, even, x2 + x3, x3, x2, x0 + x1, x1, x0))
    return list(zip(*rows))


def product_targets(inputs):
    both, odd, even, right, x3, x2, left, x1, x0 = inputs
    return (both, even, odd, left, x0, x1, right, x2, x3)


def rows_of(row):
    return [(i, row + i - HALF_KS) for i in range(KS) if 0 <= row + i - HALF_KS < HT]


def product_sum(filters, inputs):
    sums = []
    for at in range(PRODUCTS):
        weights = [filters(i * PRODUCTS + at) for i in range(KS)]
        found = []
        for row in range(HT):
            value = None
            for i, source in rows_of(row):
                term = weights[i] * inputs[at][source]
                value = term if value is None else value + term
            found.append(value)
        sums.append(found)
    return sums


def product_outputs(sums, row):
    q = [found[row] for found in sums]
    near_0, near_1 = q[0] + q[1], q[0] + q[2]
    return (
        near_0 + (q[3] + q[4]), near_1 + (q[3] + q[5]), near_0 + (q[6] + q[7]), near_1 + (q[6] + q[8])
    )


def in_order(position, own, near, far, cross):
    first = position % 2 == 0
    front = position // 2 == 0
    low, high = jnp.where(first, own, near), jnp.where(first, near, own)
    far_low, far_high = jnp.where(first, far, cross), jnp.where(first, cross, far)
    return (
        jnp.where(front, low, far_low), jnp.where(front, high, far_high),
        jnp.where(front, far_low, low), jnp.where(front, far_high, high),
    )


def matrix_in_order(position, refs, start, channels):
    parts = in_order(position, *[ref[start : start + channels, :].astype(f32) for ref in refs])
    gap = jnp.zeros((PAIR_LANES - 2 * channels, C_IN), f32)
    return jnp.concatenate([*parts[0:2], gap, *parts[2:4], gap], axis=0).astype(bf16)


def first_kernel(
    index_ref, matrix_0, matrix_1, matrix_2, matrix_3, x_ref, _after_ref,
    expanded_ref, sums_ref, we_ref, keep_ref, send_ref,
):
    blocks = x_ref.shape[0]
    width = we_ref.shape[0]
    refs = (matrix_0, matrix_1, matrix_2, matrix_3)
    we_ref[...] = matrix_in_order(index_ref[1], refs, 0, matrix_0.shape[0] // 2)
    tail = None
    for piece in range(C_IN // TAIL_LANES):
        rows = x_ref[:, piece * TAIL_ROWS : (piece + 1) * TAIL_ROWS, :].reshape(-1, 128)
        move = one_hot(
            128, C_IN, lambda r, c: (r - C_IN == c - piece * TAIL_LANES) & (r >= C_IN)
        ).astype(bf16)
        part = dot(rows, move, contract_plain)
        tail = part if tail is None else tail + part
    packed = jnp.concatenate(
        [
            x_ref[:, BLOCK_ROWS:SENT_ROWS, 0:C_IN].astype(f32),
            tail.reshape(blocks, TAIL_ROWS, C_IN),
        ],
        axis=1,
    )
    packed = packed.reshape(blocks * PACKED_ROWS // 16, 2, 8, C_IN)
    first = index_ref[1] % 2 == 0
    for ref, at in ((keep_ref, 0), (send_ref, 1)):
        half = jnp.where(first, packed[:, at], packed[:, 1 - at])
        ref[...] = half.reshape(blocks, PACKED_ROWS // 2, C_IN).astype(bf16)
    for lanes in (slice(at, at + 256) for at in range(0, width, 256)):
        total = jnp.zeros((8, 256), f32)
        square = jnp.zeros((8, 256), f32)
        for block in range(blocks):
            value = dot(x_ref[block, 0:BLOCK_ROWS, 0:C_IN], we_ref[lanes, :], contract_lanes)
            expanded_ref[block, :, lanes] = value
            shaped = value.reshape(POSITIONS, 8, 256)
            total = total + jnp.sum(shaped, axis=0)
            square = square + jnp.sum(shaped * shaped, axis=0)
        sums_ref[0:8, lanes] = total
        sums_ref[8:16, lanes] = square


def norm_factors(total_rows, sums_own, sums_other, gain, shift, norm_ref):
    average = rows_sum(sums_own[0:8] + sums_other[0:8]) / total_rows
    squares = rows_sum(sums_own[8:16] + sums_other[8:16]) / total_rows
    spread = lax.rsqrt(squares - average * average + norm_epsilon)
    gain = gain * spread
    norm_ref[0:8, :] = 0.5 * gain
    norm_ref[8:16, :] = 0.5 * (shift - average * gain)
    norm_ref[16:24, :] = average
    norm_ref[24:32, :] = spread


def expand_kernel(
    total_rows, expanded_ref, sums_own, sums_other, stack_ref, depth_ref, sums_ref, norm_ref, taps_scr
):
    blocks, _, width = expanded_ref.shape
    norm_factors(
        total_rows, sums_own, sums_other, stack_ref[ROW_EXPAND_GAINS : ROW_EXPAND_GAINS + 1, :],
        stack_ref[ROW_EXPAND_GAINS + 1 : ROW_EXPAND_GAINS + 2, :], norm_ref,
    )
    product_filters(lambda i, j: stack_ref[i * KS + j : i * KS + j + 1, :], taps_scr)
    sums_ref[...] = jnp.zeros_like(sums_ref)

    def one_block(block, carry):
        for tile in range(width // 128):
            lanes = lane_tile(tile)
            gain_half = norm_ref[0:8, lanes]
            shift_half = norm_ref[8:16, lanes]
            active = [
                swish_of_half(expanded_ref[block, 8 * at : 8 * at + 8, lanes] * gain_half + shift_half)
                for at in range(POSITIONS)
            ]
            total = jnp.zeros((8, 128), f32)
            square = jnp.zeros((8, 128), f32)
            sums = product_sum(lambda at: taps_scr[at, :, lanes], product_inputs(active))
            for row in range(HT):
                for col, value in enumerate(product_outputs(sums, row)):
                    at = row * WD + col
                    depth_ref[block, 8 * at : 8 * at + 8, lanes] = value
                    total = total + value
                    square = square + value * value
            sums_ref[0:8, lanes] += total
            sums_ref[8:16, lanes] += square
        return carry

    lax.fori_loop(0, blocks, one_block, 0)


def squeeze_kernel(
    total_rows, depth_ref, sums_own, sums_other, stack_ref, wp_ref, cot_ref, bias_ref,
    projected_ref, scaled_ref, sums_ref, gate_ref, before_ref, pooled_ref, norm_ref, active_ref,
):
    blocks, _, width = depth_ref.shape
    norm_factors(
        total_rows, sums_own, sums_other, stack_ref[ROW_DEPTH_GAINS : ROW_DEPTH_GAINS + 1, :],
        stack_ref[ROW_DEPTH_GAINS + 1 : ROW_DEPTH_GAINS + 2, :], norm_ref,
    )

    def pool_block(block, carry):
        for tile in range(width // 128):
            lanes = lane_tile(tile)
            gain_half = norm_ref[0:8, lanes]
            shift_half = norm_ref[8:16, lanes]
            total = jnp.zeros((8, 128), f32)
            for at in range(POSITIONS):
                value = swish_of_half(
                    depth_ref[block, 8 * at : 8 * at + 8, lanes] * gain_half + shift_half
                )
                active_ref[block, 8 * at : 8 * at + 8, lanes] = value
                total = total + value
            pooled_ref[pl.ds(pl.multiple_of(block * 8, 8), 8), lanes] = total / POSITIONS
        return carry

    lax.fori_loop(0, blocks, pool_block, 0)
    squeeze = stack_ref[ROW_SQUEEZE : ROW_SQUEEZE + HIDDEN_ROWS, :]
    excite = stack_ref[ROW_EXCITE : ROW_EXCITE + HIDDEN_ROWS, :]
    before = highest(pooled_ref[...], squeeze, contract_lanes) + bias_ref[...]
    before_ref[...] = before
    hidden = swish_of_half(0.5 * before)
    raised = highest(hidden, excite, contract_plain)
    raised = raised + stack_ref[ROW_EXCITE_BIAS : ROW_EXCITE_BIAS + 1, :]
    gate_ref[...] = 0.5 + 0.5 * jnp.tanh(0.5 * raised)
    totals = [jnp.zeros((8, C_IN), f32)] * 4
    for block in range(blocks):
        for tile in range(width // 128):
            lanes = lane_tile(tile)
            gate = gate_ref[8 * block : 8 * block + 8, lanes]
            value = active_ref[block, :, lanes].reshape(POSITIONS, 8, 128) * gate[None]
            scaled_ref[block, :, lanes] = value.reshape(BLOCK_ROWS, 128).astype(bf16)
        projected = dot(scaled_ref[block], wp_ref[...], contract_plain)
        projected_ref[block] = projected
        shaped = projected.reshape(POSITIONS, 8, C_IN)
        upstream = cot_ref[block].astype(f32).reshape(POSITIONS, 8, C_IN)
        terms = (shaped, shaped * shaped, shaped * upstream, upstream)
        totals = [total + jnp.sum(term, axis=0) for total, term in zip(totals, terms)]
    for at in range(4):
        sums_ref[8 * at : 8 * at + 8, :] = totals[at]


def gate_back_kernel(
    total_rows, index_ref, projected_ref, cot_ref, sums_own, sums_other, gains_ref, depth_ref,
    norm_ref, stack_ref, wp_ref, gate_ref, before_ref, pooled_ref, scaled_ref, active_ref, x_ref,
    two_ref, sums_ref, lanes_ref, gains_grad_ref, output_ref,
    delta_scr, grad_scr, gate_grad_scr, pooled_scr,
):
    blocks = depth_ref.shape[0]
    width = depth_ref.shape[2]
    own = pl.multiple_of(index_ref[1] // 2 * PAIR_LANES, 128)
    own_lanes = pl.ds(own, PAIR_LANES)
    sums = [rows_sum(sums_own[8 * k : 8 * k + 8] + sums_other[8 * k : 8 * k + 8])[0:1] for k in range(4)]
    average = sums[0] / total_rows
    spread = lax.rsqrt(sums[1] / total_rows - average * average + norm_epsilon)
    beta = sums[3]
    gamma = spread * (sums[2] - average * beta)
    gains_grad_ref[0:1, :] = gamma
    gains_grad_ref[1:2, :] = beta
    gain = gains_ref[0:1, :]
    shift = gains_ref[1:2, :]
    mine = index_ref[0]
    output_ref[...] = (
        x_ref[mine, 0:BLOCK_ROWS, 0:C_IN].astype(f32) + (projected_ref[mine] - average) * spread * gain + shift
    ).astype(output_ref.dtype)
    outer = gain * spread

    for block in range(blocks):
        normal = (projected_ref[block] - average) * spread
        delta = outer * (
            cot_ref[block].astype(f32) - beta / total_rows - normal * (gamma / total_rows)
        )
        delta_scr[block] = delta.astype(bf16)
    for block in range(blocks):
        for lanes in (slice(at, at + 256) for at in range(0, width, 256)):
            value = dot(delta_scr[block], wp_ref[lanes, :], contract_lanes)
            grad_scr[block, :, lanes] = value
            value = (value * active_ref[block, :, lanes]).reshape(POSITIONS, 8, 256)
            gate_grad_scr[8 * block : 8 * block + 8, lanes] = jnp.sum(value, axis=0)
    excite = stack_ref[ROW_EXCITE : ROW_EXCITE + HIDDEN_ROWS, :]
    gate = gate_ref[...]
    gate_grad_scr[...] = gate_grad_scr[...] * gate * (1.0 - gate)
    half = 0.5 * before_ref[...]
    hidden = swish_of_half(half)
    squeeze_delta = highest(gate_grad_scr[...], excite, contract_lanes) * slope_of_half(half)
    own_delta = gate_grad_scr[:, own_lanes]
    lanes_ref[0:HIDDEN_ROWS, :] = highest(squeeze_delta, pooled_ref[:, own_lanes], contract_rows)
    lanes_ref[HIDDEN_ROWS : 2 * HIDDEN_ROWS, :] = highest(hidden, own_delta, contract_rows)
    lanes_ref[KEEP_BIASES : KEEP_BIASES + 8, :] = rows_sum(own_delta)
    lanes_ref[KEEP_BIASES + 8 : KEEP_BIASES + 16, :] = jnp.zeros((8, PAIR_LANES), f32)
    lanes_ref[KEEP_BIASES + 8 : KEEP_BIASES + 16, 0:HIDDEN_ROWS] = rows_sum(squeeze_delta)
    squeeze = stack_ref[ROW_SQUEEZE : ROW_SQUEEZE + HIDDEN_ROWS, own_lanes]
    pooled_scr[...] = highest(squeeze_delta, squeeze, contract_plain) / POSITIONS
    sums_ref[...] = jnp.zeros_like(sums_ref)

    def two_block(block, carry):
        rows = pl.ds(pl.multiple_of(block * 8, 8), 8)
        for tile in range(PAIR_LANES // 128):
            lanes = lane_tile(tile)
            whole = lane_tile(tile, own)
            gain_half = norm_ref[0:8, whole]
            shift_half = norm_ref[8:16, whole]
            average = norm_ref[16:24, whole]
            gate = 0.5 * gate_ref[rows, whole]
            pooled_grad = 0.5 * pooled_scr[rows, lanes]
            total = jnp.zeros((8, 128), f32)
            product = jnp.zeros((8, 128), f32)
            for at in range(POSITIONS):
                spot = slice(8 * at, 8 * at + 8)
                depth = depth_ref[block, spot, whole]
                bent = jnp.tanh(depth * gain_half + shift_half)
                slope = (1.0 + bent) + active_ref[block, spot, whole] * (1.0 - bent)
                value = (grad_scr[block, spot, whole] * gate + pooled_grad) * slope
                two_ref[block, spot, lanes] = value
                total = total + value
                product = product + value * (depth - average)
            sums_ref[0:8, lanes] += total
            sums_ref[8:16, lanes] += product
        return carry

    lax.fori_loop(0, blocks, two_block, 0)
    rows = blocks * POSITIONS * 8
    lanes_ref[KEEP_PROJECT : KEEP_PROJECT + C_IN, :] = dot(
        delta_scr[...].reshape(rows, C_IN), scaled_ref[:, :, own_lanes].reshape(rows, PAIR_LANES), contract_rows
    )


def depth_back_kernel(
    total_rows, index_ref, sums_own, sums_other, two_ref, depth_ref, expanded_ref, stack_ref,
    norm_one_ref, norm_two_ref,
    one_ref, sums_ref, gains_grad_ref, taps_scr, kernel_scr, factors_scr,
):
    blocks = depth_ref.shape[0]
    own = pl.multiple_of(index_ref[1] // 2 * PAIR_LANES, 128)
    own_lanes = pl.ds(own, PAIR_LANES)
    spread = norm_two_ref[24:32, own_lanes]
    average = norm_two_ref[16:24, own_lanes]
    beta = rows_sum(sums_own[0:8] + sums_other[0:8])
    gamma = rows_sum(sums_own[8:16] + sums_other[8:16]) * spread
    gains_grad_ref[0:1, :] = gamma[0:1]
    gains_grad_ref[1:2, :] = beta[0:1]
    outer = stack_ref[ROW_DEPTH_GAINS : ROW_DEPTH_GAINS + 1, own_lanes] * spread
    slope = outer * spread * gamma / total_rows
    factors_scr[0:8, :] = outer
    factors_scr[8:16, :] = slope
    factors_scr[16:24, :] = outer * (beta / total_rows)
    product_filters(
        lambda i, j: stack_ref[TAPS - 1 - i * KS - j : TAPS - i * KS - j, own_lanes], taps_scr
    )
    sums_ref[...] = jnp.zeros_like(sums_ref)
    kernel_scr[...] = jnp.zeros_like(kernel_scr)

    def one_block(block, carry):
        for tile in range(PAIR_LANES // 128):
            lanes = lane_tile(tile)
            whole = lane_tile(tile, own)
            gain_half = norm_one_ref[0:8, whole]
            shift_half = norm_one_ref[8:16, whole]
            average_one = norm_one_ref[16:24, whole]
            average_two = norm_two_ref[16:24, whole]
            outer = factors_scr[0:8, lanes]
            slope = factors_scr[8:16, lanes]
            level = factors_scr[16:24, lanes]
            grads = []
            active = []
            for at in range(POSITIONS):
                spot = slice(8 * at, 8 * at + 8)
                grads.append(
                    outer * two_ref[block, spot, lanes]
                    - level
                    - slope * (depth_ref[block, spot, whole] - average_two)
                )
                active.append(swish_of_half(expanded_ref[block, spot, whole] * gain_half + shift_half))
            sources = product_inputs(active)
            inputs = product_inputs(grads)
            targets = product_targets(inputs)
            for at in range(PRODUCTS):
                for i in range(KS):
                    value = None
                    for row in range(HT):
                        if 0 <= row + i - HALF_KS < HT:
                            term = targets[at][row] * sources[at][row + i - HALF_KS]
                            value = term if value is None else value + term
                    kernel_scr[i * PRODUCTS + at, :, lanes] += value
            sums = product_sum(lambda at: taps_scr[at, :, lanes], inputs)
            total = jnp.zeros((8, 128), f32)
            product = jnp.zeros((8, 128), f32)
            for row in range(HT):
                for col, value in enumerate(product_outputs(sums, row)):
                    at = row * WD + col
                    spot = slice(8 * at, 8 * at + 8)
                    expanded = expanded_ref[block, spot, whole]
                    value = value * slope_of_half(expanded * gain_half + shift_half)
                    one_ref[block, spot, lanes] = value
                    total = total + value
                    product = product + value * (expanded - average_one)
            sums_ref[0:8, lanes] += total
            sums_ref[8:16, lanes] += product
        return carry

    lax.fori_loop(0, blocks, one_block, 0)
    for i in range(KS):
        for j in range(KS):
            terms = [
                (jnp.sum(kernel_scr[i * PRODUCTS + at], axis=0, keepdims=True), sign)
                for at, signs in enumerate(FILTER_SIGNS)
                for column, sign in signs
                if column == j
            ]
            row = 16 + i * KS + j
            sums_ref[row : row + 1, :] = signed(terms)


def expand_back_kernel(
    total_rows, index_ref, sums_own, sums_other, one_ref, expanded_ref, x_ref, we_ref, stack_ref, norm_ref,
    _output_ref, _lanes_ref,
    expand_ref, input_ref, gains_grad_ref, delta_scr,
):
    blocks = x_ref.shape[0]
    own = pl.multiple_of(index_ref[1] // 2 * PAIR_LANES, 128)
    own_lanes = pl.ds(own, PAIR_LANES)
    spread = norm_ref[24:32, own_lanes]
    average = norm_ref[16:17, own_lanes]
    beta = rows_sum(sums_own[0:8] + sums_other[0:8])
    gamma = rows_sum(sums_own[8:16] + sums_other[8:16]) * spread
    gains_grad_ref[0:1, :] = gamma[0:1]
    gains_grad_ref[1:2, :] = beta[0:1]
    outer = stack_ref[ROW_EXPAND_GAINS : ROW_EXPAND_GAINS + 1, own_lanes] * spread[0:1]
    slope = outer * spread[0:1] * gamma[0:1] / total_rows
    level = outer * (beta[0:1] / total_rows)
    own_weights = we_ref[own_lanes, :]

    for block in range(blocks):
        centred = expanded_ref[block, :, own_lanes] - average
        delta = outer * one_ref[block] - level - slope * centred
        delta_scr[block] = delta.astype(bf16)
    rows = blocks * POSITIONS * 8
    expand_ref[...] = dot(
        x_ref[:, 0:BLOCK_ROWS, 0:C_IN].reshape(rows, C_IN), delta_scr[...].reshape(rows, PAIR_LANES), contract_rows
    )
    input_ref[...] = dot(delta_scr[index_ref[0]], own_weights, contract_plain)


def one_hot(rows, columns, matches):
    return matches(
        lax.broadcasted_iota(jnp.int32, (rows, columns), 0),
        lax.broadcasted_iota(jnp.int32, (rows, columns), 1),
    )


def copies_kernel(index_ref, rows_ref, cot_ref, copies_ref):
    whole = rows_ref[...].astype(f32)
    half = jnp.where(index_ref[1] % 2 == 0, whole[:, 0:8, :], whole[:, 8:16, :])
    half = half.reshape(BLOCK_ROWS, C_IN)
    narrow = cot_ref.shape[2]
    rows = cot_ref[...].reshape(4 * PACKED_ROWS, narrow)
    packed = None
    for group in range(4):
        place = one_hot(narrow, C_IN, lambda r, c: c == r + group * narrow).astype(bf16)
        part = dot(rows[group * PACKED_ROWS : (group + 1) * PACKED_ROWS], place, contract_plain)
        packed = part if packed is None else packed + part
    value = jnp.concatenate([half, packed], axis=0).astype(bf16)
    widen = one_hot(C_IN, 128, lambda r, c: r == c).astype(bf16)
    dense = dot(value[0:SENT_ROWS], widen, contract_plain)
    parts = []
    for piece in range(SENT_ROWS // TAIL_ROWS):
        move = one_hot(
            C_IN, 128, lambda r, c: (c - C_IN == r - piece * TAIL_LANES) & (c >= C_IN)
        ).astype(bf16)
        parts.append(dot(value[SENT_ROWS:], move, contract_plain))
    dense = (dense + jnp.concatenate(parts, axis=0)).astype(bf16)
    for at in range(copies_ref.shape[0]):
        copies_ref[at] = dense


def cot_kernel(index_ref, own_ref, near_ref, far_ref, cross_ref, cot_ref):
    position = index_ref[1]
    near = position + 1 - position % 2 * 2
    blocks = cot_ref.shape[0]
    narrow = C_IN // 4
    rows = blocks * PACKED_ROWS // 2
    pieces = (
        (own_ref, position), (near_ref, near), (far_ref, (position + 2) % 4),
        (cross_ref, (near + 2) % 4),
    )
    for group in range(4):
        total = None
        for ref, place in pieces:
            move = one_hot(
                C_IN,
                C_IN,
                lambda r, c: (c - place * narrow == r - group * narrow)
                & (r >= group * narrow) & (r < (group + 1) * narrow),
            ).astype(bf16)
            part = dot(ref[...].reshape(rows, C_IN), move, contract_plain)
            total = part if total is None else total + part
        half = total.reshape(blocks, PACKED_ROWS // 2, C_IN).astype(bf16)
        start = group * (PACKED_ROWS // 2)
        cot_ref[:, start : start + PACKED_ROWS // 2, :] = half


def pack_kernel(
    expand_ref, project_ref, depth_ref, squeeze_ref, excite_ref, excite_bias_ref, expand_gains_ref,
    depth_gains_ref, project_gains_ref, stack_ref, matrix_ref,
):
    channels = expand_ref.shape[0]
    narrow = project_gains_ref.shape[1]
    stack_ref[...] = jnp.zeros_like(stack_ref)
    for start, ref in (
        (0, depth_ref), (ROW_SQUEEZE, squeeze_ref), (ROW_EXCITE, excite_ref),
        (ROW_EXCITE_BIAS, excite_bias_ref), (ROW_EXPAND_GAINS, expand_gains_ref),
        (ROW_DEPTH_GAINS, depth_gains_ref),
    ):
        stack_ref[start : start + ref.shape[0], :] = ref[...]
    stack_ref[ROW_PROJECT_GAINS : ROW_PROJECT_GAINS + 2, 0:narrow] = project_gains_ref[...]
    matrix_ref[...] = jnp.concatenate(
        [expand_ref[...], project_ref[...]], axis=0
    ).astype(bf16)


def assemble_kernel(
    index_ref, stack_0, stack_1, stack_2, stack_3, matrix_0, matrix_1, matrix_2, matrix_3,
    stack_ref, project_ref, gains_ref,
):
    channels = stack_0.shape[1]
    narrow = C_IN // 4
    stacks = in_order(index_ref[1], stack_0[...], stack_1[...], stack_2[...], stack_3[...])
    stack_ref[...] = jnp.zeros_like(stack_ref)
    for place in range(4):
        start = place // 2 * PAIR_LANES + place % 2 * channels
        stack_ref[:, start : start + channels] = stacks[place]
        gains_ref[:, place * narrow : (place + 1) * narrow] = stacks[place][
            ROW_PROJECT_GAINS : ROW_PROJECT_GAINS + 2, 0:narrow
        ]
    refs = (matrix_0, matrix_1, matrix_2, matrix_3)
    project_ref[...] = matrix_in_order(index_ref[1], refs, channels, channels)


def kept_sums(keep_own, keep_other, sums_own, sums_other):
    def both(start, stop):
        return keep_own[start:stop, :] + keep_other[start:stop, :]

    return (
        both(KEEP_PROJECT, KEEP_PROJECT + C_IN), both(0, 2 * HIDDEN_ROWS),
        sums_own[16 : 16 + TAPS, :] + sums_other[16 : 16 + TAPS, :],
        both(KEEP_BIASES, KEEP_BIASES + 1), both(KEEP_BIASES + 8, KEEP_BIASES + 9)[:, 0:HIDDEN_ROWS],
    )


def both_halves(first, own, other):
    own = own.reshape(POSITIONS, 8, own.shape[-1])
    other = other.reshape(POSITIONS, 8, other.shape[-1])
    return jnp.concatenate(
        [jnp.where(first, own, other), jnp.where(first, other, own)], axis=1
    )


def settle_kernel(
    index_ref, expand_own, expand_other, keep_own, keep_other, sums_own, sums_other, three_ref, two_ref, one_ref,
    input_own, input_other, square_ref, packed_ref,
):
    position = index_ref[1]
    narrow = C_IN // 4

    def squared(values):
        return jnp.sum(jnp.sum(values * values, axis=0, keepdims=True), axis=1, keepdims=True)

    project, hidden, kernel, excite_bias, bias = kept_sums(keep_own, keep_other, sums_own, sums_other)
    total = squared(expand_own[...] + expand_other[...]) + squared(project) + squared(hidden)
    total = total + squared(kernel) + squared(excite_bias)
    total = total + squared(one_ref[...]) + squared(two_ref[...])
    square_ref[0:8, :] = jnp.broadcast_to(total, (8, 128))
    square_ref[8:16, :] = jnp.broadcast_to(squared(bias) + squared(three_ref[...]), (8, 128))
    whole = both_halves(position % 2 == 0, input_own[...], input_other[...])
    whole = whole.reshape(4 * PACKED_ROWS, C_IN).astype(bf16)
    across = position + 2 - position // 2 * 4
    packed = None
    for group in range(4):
        move = one_hot(
            C_IN,
            C_IN,
            lambda r, c: (r - across * narrow == c - group * narrow)
            & (c >= group * narrow) & (c < (group + 1) * narrow),
        ).astype(bf16)
        part = dot(whole[group * PACKED_ROWS : (group + 1) * PACKED_ROWS], move, contract_plain)
        packed = part if packed is None else packed + part
    packed_ref[0:PACKED_ROWS, :] = packed.astype(bf16)
    rest = jnp.broadcast_to(total, (16, C_IN))
    parts = jnp.zeros((16, C_IN), f32)
    row = lax.broadcasted_iota(jnp.int32, (16, C_IN), 0)
    for at in range(3):
        part = rest.astype(bf16).astype(f32)
        rest = rest - part
        parts = jnp.where(row == at, part, parts)
    packed_ref[PACKED_ROWS : PACKED_ROWS + 16, :] = parts.astype(bf16)


def own_kernel(
    index_ref, expand_own, expand_other, keep_own, keep_other, sums_own, sums_other, two_ref, one_ref,
    input_own, input_other, output_own, output_other,
    expand_ref, project_ref, lanes_ref, bias_ref, input_ref, output_ref,
):
    position = index_ref[1]
    first = position % 2 == 0
    channels = expand_ref.shape[0]
    narrow = C_IN // 4

    def mine(values):
        return jnp.where(first, values[:, 0:channels], values[:, channels : 2 * channels])

    project, hidden, kernel, excite_bias, bias = kept_sums(keep_own, keep_other, sums_own, sums_other)
    bias_ref[...] = bias
    expand_ref[...] = jnp.transpose(mine(expand_own[...] + expand_other[...]))
    project_ref[...] = jnp.transpose(mine(project))
    lanes_ref[0:TAPS, :] = mine(kernel)
    lanes_ref[ROW_SQUEEZE : ROW_SQUEEZE + 2 * HIDDEN_ROWS, :] = mine(hidden)
    lanes_ref[ROW_EXCITE_BIAS : ROW_EXCITE_BIAS + 1, :] = mine(excite_bias)
    lanes_ref[ROW_EXPAND_GAINS : ROW_EXPAND_GAINS + 2, :] = mine(one_ref[...])
    lanes_ref[ROW_DEPTH_GAINS : ROW_DEPTH_GAINS + 2, :] = mine(two_ref[...])
    pick = one_hot(C_IN, narrow, lambda r, c: r == c + position * narrow)
    halves = [
        highest(ref[...], pick.astype(f32), contract_plain) for ref in (input_own, input_other)
    ]
    input_ref[...] = both_halves(first, *halves)
    halves = [dot(ref[...], pick.astype(bf16), contract_plain) for ref in (output_own, output_other)]
    output_ref[...] = both_halves(first, *halves).astype(bf16)


def adam_kernel(
    index_ref, square_ref, expand_grad, project_grad, lanes_grad, bias_grad, three_grad,
    input_own, packed_other, cot_ref, *refs,
):
    params, outs = refs[:30], refs[30:]
    narrow = cot_ref.shape[2]
    parts = packed_other[PACKED_ROWS : PACKED_ROWS + 16, :].astype(f32)
    other = (parts[0:1, 0:1] + parts[1:2, 0:1]) + parts[2:3, 0:1]
    total = square_ref[0:1, 0:1] + other + square_ref[8:9, 0:1]
    grad_norm = jnp.sqrt(total)
    factor = clip_limit / jnp.maximum(grad_norm, clip_limit)
    outs[31][...] = grad_norm
    groups = []
    for group in range(4):
        pick = one_hot(C_IN, narrow, lambda r, c: r == c + group * narrow).astype(bf16)
        groups.append(dot(packed_other[0:PACKED_ROWS, :], pick, contract_plain))
    crossed = jnp.concatenate(groups, axis=0).reshape(POSITIONS, 16, narrow)
    outs[0][...] = input_own[...] + crossed + cot_ref[...].astype(f32)
    pick = one_hot(C_IN, narrow, lambda r, c: r == c + index_ref[1] * narrow).astype(f32)
    gradients = (
        expand_grad[...],
        lanes_grad[ROW_EXPAND_GAINS : ROW_EXPAND_GAINS + 2, :],
        lanes_grad[0:TAPS, :],
        lanes_grad[ROW_DEPTH_GAINS : ROW_DEPTH_GAINS + 2, :],
        lanes_grad[ROW_SQUEEZE : ROW_SQUEEZE + params[12].shape[0], :],
        bias_grad[:, 0 : params[15].shape[1]],
        lanes_grad[ROW_EXCITE : ROW_EXCITE + params[18].shape[0], :],
        lanes_grad[ROW_EXCITE_BIAS : ROW_EXCITE_BIAS + 1, :],
        project_grad[...],
        highest(three_grad[0:2, :], pick, contract_plain),
    )
    for entry in range(10):
        updated = adam_step(
            params[3 * entry][...],
            params[3 * entry + 1][...],
            params[3 * entry + 2][...],
            gradients[entry] * factor,
            step_rates[entry],
            decay_flags[entry],
        )
        for part in range(3):
            outs[1 + 3 * entry + part][...] = updated[part]


def call(kernel, outs, operands, scratch=(), name=None, keep=True, place=True, after=()):
    spaces = [
        pl.BlockSpec(memory_space=pltpu.SMEM)
        if operand.dtype == jnp.int32
        else pl.BlockSpec(memory_space=pltpu.VMEM)
        for operand in operands
    ]
    spaces += [pl.BlockSpec(memory_space=pl.ANY)] * len(after)
    operands = [
        operand
        if operand.dtype == jnp.int32
        else pltpu.with_memory_space_constraint(operand, pltpu.VMEM if place else pltpu.HBM)
        for operand in operands
    ] + [pltpu.with_memory_space_constraint(operand, pltpu.HBM) for operand in after]
    limit = 4 * 1024 * 1024 + sum(4 * math.prod(shape) for shape, _ in scratch)
    made = pltpu.VMEM if keep else jax.ShapeDtypeStruct
    return pl.pallas_call(
        kernel,
        out_shape=[
            (jax.ShapeDtypeStruct if out[2:] else made)(out[0], out[1]) for out in outs
        ],
        in_specs=spaces,
        out_specs=[pl.BlockSpec(memory_space=pltpu.VMEM)] * len(outs),
        scratch_shapes=[pltpu.VMEM(shape, dtype) for shape, dtype in scratch],
        compiler_params=pltpu.CompilerParams(vmem_limit_bytes=limit),
        name=name,
    )(*operands)


def on_device_paired(*arrays):
    block_input, cotangent = arrays[:2]
    segments = block_input.shape[3]
    if segments != 16:
        return on_device(*arrays)
    params = list(arrays[2:])
    for at in (15, 16, 17, 21, 22, 23):
        params[at] = params[at][None]
    for at in (24, 25, 26):
        params[at] = params[at].T
    (
        expand_weight, expand_gains, depth_weight, depth_gains, squeeze_weight,
        squeeze_bias, excite_weight, excite_bias, project_weight, project_gains,
    ) = params[::3]
    shards = lax.axis_size("dp")
    index = jnp.stack([lax.axis_index("dp"), lax.axis_index("chan")]).astype(jnp.int32)
    total_rows = float(POSITIONS * segments * shards)
    narrow = cotangent.shape[0]
    channels = expand_weight.shape[0]
    rows = POSITIONS * 8
    width = 2 * PAIR_LANES

    def swap(values, mask):
        return lax.ppermute(values, "chan", [(at, at ^ mask) for at in range(4)])

    input_rows = jnp.transpose(block_input, (1, 2, 3, 0)).reshape(POSITIONS, segments, C_IN)
    cot_rows = jnp.transpose(cotangent, (1, 2, 3, 0)).reshape(POSITIONS, segments, narrow)
    (copies,) = call(
        copies_kernel,
        [((shards, SENT_ROWS, 128), bf16)],
        [index, input_rows, cot_rows],
        name="copies",
        keep=False,
        place=False,
    )
    x = lax.all_to_all(copies, "dp", 0, 0)
    stack, matrix = call(
        pack_kernel,
        [((STACK_ROWS, channels), f32), ((2 * channels, C_IN), bf16)],
        [
            expand_weight, project_weight, depth_weight, squeeze_weight, excite_weight, excite_bias,
            expand_gains, depth_gains, project_gains,
        ],
        name="pack",
        keep=False,
        place=False,
    )
    stack_far, matrix_far = swap(stack, 2), swap(matrix, 2)
    pieces = [
        stack, swap(stack, 1), stack_far, swap(stack_far, 1),
        matrix, swap(matrix, 1), matrix_far, swap(matrix_far, 1),
    ]
    stack_all, project_all, gains_all = call(
        assemble_kernel,
        [((STACK_ROWS, width), f32), ((width, C_IN), bf16), ((2, C_IN), f32)],
        [index, *pieces],
        name="assemble",
        keep=False,
    )
    expanded, sums_one, expand_all, kept, sent = call(
        first_kernel,
        [
            ((shards, rows, width), f32),
            ((16, width), f32),
            ((width, C_IN), bf16),
            ((shards, PACKED_ROWS // 2, C_IN), bf16),
            ((shards, PACKED_ROWS // 2, C_IN), bf16),
        ],
        [index, *pieces[4:], x],
        name="first",
        after=[gains_all],
    )
    (cot,) = call(
        cot_kernel,
        [((shards, rows, C_IN), bf16)],
        [index, kept, swap(sent, 1), swap(kept, 2), swap(sent, 3)],
        name="cot",
    )
    bias_row = jnp.pad(squeeze_bias, ((0, 0), (0, HIDDEN_ROWS - squeeze_bias.shape[1])))

    depth, sums, norm_one = call(
        functools.partial(expand_kernel, total_rows),
        [((shards, rows, width), f32), ((16, width), f32), ((32, width), f32)],
        [expanded, sums_one, swap(sums_one, 1), stack_all],
        [((KS * PRODUCTS, 8, width), f32)],
        name="expand",
    )
    projected, scaled, sums, gate, before, pooled, norm_two, active = call(
        functools.partial(squeeze_kernel, total_rows),
        [
            ((shards, rows, C_IN), f32),
            ((shards, rows, width), bf16),
            ((32, C_IN), f32),
            ((shards * 8, width), f32),
            ((shards * 8, HIDDEN_ROWS), f32),
            ((shards * 8, width), f32),
            ((32, width), f32),
            ((shards, rows, width), f32),
        ],
        [depth, sums, swap(sums, 1), stack_all, project_all, cot, bias_row],
        name="squeeze",
    )
    two, sums, lanes_grad, three_grad, output = call(
        functools.partial(gate_back_kernel, total_rows),
        [
            ((shards, rows, PAIR_LANES), f32),
            ((16, PAIR_LANES), f32),
            ((KEEP_ROWS, PAIR_LANES), f32),
            ((2, C_IN), f32),
            ((rows, C_IN), bf16),
        ],
        [
            index, projected, cot, sums, swap(sums, 1), gains_all, depth, norm_two, stack_all,
            project_all, gate, before, pooled, scaled, active, x,
        ],
        [
            ((shards, rows, C_IN), bf16),
            ((shards, rows, width), f32),
            ((shards * 8, width), f32),
            ((shards * 8, PAIR_LANES), f32),
        ],
        name="gate_back",
    )
    output_other = swap(output, 1)
    lanes_other = swap(lanes_grad, 1)
    one, sums, two_grad = call(
        functools.partial(depth_back_kernel, total_rows),
        [
            ((shards, rows, PAIR_LANES), f32),
            ((48, PAIR_LANES), f32),
            ((2, PAIR_LANES), f32),
        ],
        [
            index, sums, swap(sums, 1), two, depth, expanded, stack_all, norm_one, norm_two,
        ],
        [
            ((KS * PRODUCTS, 8, PAIR_LANES), f32),
            ((KS * PRODUCTS, 8, PAIR_LANES), f32),
            ((24, PAIR_LANES), f32),
        ],
        name="depth_back",
    )
    sums_other = swap(sums, 1)
    expand_grad, input_part, one_grad = call(
        functools.partial(expand_back_kernel, total_rows),
        [((C_IN, PAIR_LANES), f32), ((rows, C_IN), f32), ((2, PAIR_LANES), f32)],
        [
            index, sums, sums_other, one, expanded, x, expand_all, stack_all, norm_one,
            output_other, lanes_other,
        ],
        [((shards, rows, PAIR_LANES), bf16)],
        name="expand_back",
    )
    expand_pair = [expand_grad, swap(expand_grad, 1)]
    keep_pair = [lanes_grad, lanes_other, sums, sums_other]
    input_pair = [input_part, swap(input_part, 1)]
    square, packed = call(
        settle_kernel,
        [((16, 128), f32), ((PACKED_ROWS + 16, C_IN), bf16)],
        [index, *expand_pair, *keep_pair, three_grad, two_grad, one_grad, *input_pair],
        name="settle",
    )
    expand_own, project_own, lanes_own, bias_own, input_own, block_output = call(
        own_kernel,
        [
            ((channels, C_IN), f32),
            ((channels, C_IN), f32),
            ((STACK_ROWS, channels), f32),
            ((1, HIDDEN_ROWS), f32),
            ((POSITIONS, segments, narrow), f32),
            ((POSITIONS, segments, narrow), bf16, False),
        ],
        [index, *expand_pair, *keep_pair, two_grad, one_grad, *input_pair, output, output_other],
        name="own",
    )
    updated = call(
        adam_kernel,
        [((POSITIONS, segments, narrow), f32)]
        + [(value.shape, f32) for value in params]
        + [((1, 1), f32)],
        [
            index, square, expand_own, project_own, lanes_own, bias_own, three_grad,
            input_own, swap(packed, 2), cot_rows, *params,
        ],
        name="adam",
        keep=False,
    )
    results = [block_output] + list(updated)
    for at in (0, 1):
        results[at] = jnp.transpose(results[at].reshape(HT, WD, segments, narrow), (3, 0, 1, 2))
    for at in (17, 18, 19, 23, 24, 25):
        results[at] = results[at][0]
    for at in (26, 27, 28):
        results[at] = results[at].T
    results[32] = results[32][0, 0]
    return tuple(results)


def solution(mesh):
    body = on_device_paired if paired_fits(mesh) else on_device
    return jax.shard_map(
        body,
        mesh=mesh,
        in_specs=(
            P(None, None, None, "dp"),
            P("chan", None, None, "dp"),
            P("chan", None),
            P("chan", None),
            P("chan", None),
            P(None, "chan"),
            P(None, "chan"),
            P(None, "chan"),
            P(None, "chan"),
            P(None, "chan"),
            P(None, "chan"),
            P(None, "chan"),
            P(None, "chan"),
            P(None, "chan"),
            P(None, "chan"),
            P(None, "chan"),
            P(None, "chan"),
            P(),
            P(),
            P(),
            P(None, "chan"),
            P(None, "chan"),
            P(None, "chan"),
            P("chan"),
            P("chan"),
            P("chan"),
            P(None, "chan"),
            P(None, "chan"),
            P(None, "chan"),
            P(None, "chan"),
            P(None, "chan"),
            P(None, "chan"),
        ),
        out_specs=(
            P("chan", None, None, "dp"),
            P("chan", None, None, "dp"),
            P("chan", None),
            P("chan", None),
            P("chan", None),
            P(None, "chan"),
            P(None, "chan"),
            P(None, "chan"),
            P(None, "chan"),
            P(None, "chan"),
            P(None, "chan"),
            P(None, "chan"),
            P(None, "chan"),
            P(None, "chan"),
            P(None, "chan"),
            P(None, "chan"),
            P(None, "chan"),
            P(),
            P(),
            P(),
            P(None, "chan"),
            P(None, "chan"),
            P(None, "chan"),
            P("chan"),
            P("chan"),
            P("chan"),
            P(None, "chan"),
            P(None, "chan"),
            P(None, "chan"),
            P(None, "chan"),
            P(None, "chan"),
            P(None, "chan"),
            P(),
        ),
        check_vma=False,
    )
```

```python
import functools
import math

import jax
import jax.numpy as jnp
from jax import lax
from jax.experimental import pallas as pl
from jax.experimental.pallas import tpu as pltpu
from jax.sharding import PartitionSpec as P

C_IN = 112
KS = 5
HT = 6
WD = 4
STEP = 10


norm_epsilon = 1e-05
beta_first = 0.9
beta_second = 0.999
adam_epsilon = 1e-08
decay_rate = 0.01
clip_limit = 1.0
step_rates = (0.3, 0.6, 0.6, 0.6, 0.12, 0.6, 0.6, 0.6, 0.12, 0.6)
decay_flags = (1.0, 0.0, 1.0, 0.0, 1.0, 0.0, 1.0, 0.0, 1.0, 0.0)
contract_rows = (((0,), (0,)), ((), ()))
contract_cols = (((1,), (1,)), ((), ()))
contract_plain = (((1,), (0,)), ((), ()))


def swish(values):
    return values * jax.nn.sigmoid(values)


def swish_slope(values):
    logistic = jax.nn.sigmoid(values)
    return logistic * (1.0 + values * (1.0 - logistic))


def highest(left, right, numbers):
    return lax.dot_general(
        left, right, numbers, precision=lax.Precision.HIGHEST, preferred_element_type=jnp.float32
    )


def depthwise(activity, kernel):
    half = KS // 2
    padded = jnp.pad(activity, ((0, 0), (half, half), (half, half), (0, 0)))
    result = jnp.zeros_like(activity)
    for row_shift in range(KS):
        for col_shift in range(KS):
            window = padded[:, row_shift : row_shift + HT, col_shift : col_shift + WD, :]
            result = result + kernel[row_shift * KS + col_shift][:, None, None, None] * window
    return result


def depthwise_back(grad_field, activity, kernel):
    half = KS // 2
    padded = jnp.pad(activity, ((0, 0), (half, half), (half, half), (0, 0)))
    grad_padded = jnp.pad(grad_field, ((0, 0), (half, half), (half, half), (0, 0)))
    activity_grad = jnp.zeros_like(activity)
    kernel_rows = []
    for row_shift in range(KS):
        for col_shift in range(KS):
            window = padded[:, row_shift : row_shift + HT, col_shift : col_shift + WD, :]
            kernel_rows.append(jnp.sum(grad_field * window, axis=(1, 2, 3)))
            back_window = grad_padded[
                :,
                2 * half - row_shift : 2 * half - row_shift + HT,
                2 * half - col_shift : 2 * half - col_shift + WD,
                :,
            ]
            activity_grad = (
                activity_grad
                + kernel[row_shift * KS + col_shift][:, None, None, None] * back_window
            )
    return (activity_grad, jnp.stack(kernel_rows))


def adam_step(weight, first_moment, second, gradient, step_rate, decay_flag):
    first_new = beta_first * first_moment + (1.0 - beta_first) * gradient
    second_new = beta_second * second + (1.0 - beta_second) * gradient * gradient
    first_hat = first_new / (1.0 - beta_first**STEP)
    second_hat = second_new / (1.0 - beta_second**STEP)
    weight_new = weight - step_rate * (
        first_hat / (jnp.sqrt(second_hat) + adam_epsilon) + decay_flag * decay_rate * weight
    )
    return (weight_new, first_new, second_new)


def on_device(
    block_input,
    cotangent,
    expand_weight,
    expand_weight_first,
    expand_weight_second,
    expand_gains,
    expand_gains_first,
    expand_gains_second,
    depth_weight,
    depth_weight_first,
    depth_weight_second,
    depth_gains,
    depth_gains_first,
    depth_gains_second,
    squeeze_weight,
    squeeze_weight_first,
    squeeze_weight_second,
    squeeze_bias,
    squeeze_bias_first,
    squeeze_bias_second,
    excite_weight,
    excite_weight_first,
    excite_weight_second,
    excite_bias,
    excite_bias_first,
    excite_bias_second,
    project_weight,
    project_weight_first,
    project_weight_second,
    project_gains,
    project_gains_first,
    project_gains_second,
):
    shards = lax.axis_size("chan")
    position = lax.axis_index("chan")
    segments = block_input.shape[3]
    batch_rows = HT * WD * segments * lax.axis_size("dp")
    narrow = cotangent.shape[0]
    local_channels = expand_weight.shape[0]
    flattened = block_input.reshape(C_IN, -1)
    expand_low = expand_weight.astype(jnp.bfloat16)
    expanded = jnp.dot(expand_low, flattened, preferred_element_type=jnp.float32)
    one_sums, one_squares = lax.psum(
        (jnp.sum(expanded, axis=1), jnp.sum(expanded * expanded, axis=1)), "dp"
    )
    one_average = one_sums / batch_rows
    one_spread = lax.rsqrt(one_squares / batch_rows - one_average * one_average + norm_epsilon)
    one_normal = (expanded - one_average[:, None]) * one_spread[:, None]
    one_before = one_normal * expand_gains[0][:, None] + expand_gains[1][:, None]
    active_one = swish(one_before).reshape(local_channels, HT, WD, segments)
    depth_out = depthwise(active_one, depth_weight).reshape(local_channels, -1)
    two_sums, two_squares = lax.psum(
        (jnp.sum(depth_out, axis=1), jnp.sum(depth_out * depth_out, axis=1)), "dp"
    )
    two_average = two_sums / batch_rows
    two_spread = lax.rsqrt(two_squares / batch_rows - two_average * two_average + norm_epsilon)
    two_normal = (depth_out - two_average[:, None]) * two_spread[:, None]
    two_before = two_normal * depth_gains[0][:, None] + depth_gains[1][:, None]
    active_two = swish(two_before).reshape(local_channels, HT, WD, segments)
    pooled = jnp.mean(active_two, axis=(1, 2))
    squeeze_part = highest(squeeze_weight, pooled, contract_plain)
    squeeze_pre = lax.psum(squeeze_part, "chan") + squeeze_bias[:, None]
    hidden = swish(squeeze_pre)
    gating = jax.nn.sigmoid(highest(excite_weight, hidden, contract_rows) + excite_bias[:, None])
    scaled = (
        (active_two * gating[:, None, None, :]).astype(jnp.bfloat16).reshape(local_channels, -1)
    )
    project_low = project_weight.astype(jnp.bfloat16)
    projected = lax.psum_scatter(
        jnp.dot(project_low, scaled, preferred_element_type=jnp.float32),
        "chan",
        scatter_dimension=0,
        tiled=True,
    )
    three_sums, three_squares = lax.psum(
        (jnp.sum(projected, axis=1), jnp.sum(projected * projected, axis=1)), "dp"
    )
    three_average = three_sums / batch_rows
    three_spread = lax.rsqrt(
        three_squares / batch_rows - three_average * three_average + norm_epsilon
    )
    three_normal = (projected - three_average[:, None]) * three_spread[:, None]
    three_after = three_normal * project_gains[0][:, None] + project_gains[1][:, None]
    own_input = lax.dynamic_slice_in_dim(flattened, position * narrow, narrow, 0).astype(
        jnp.float32
    )
    block_output = (own_input + three_after).astype(jnp.bfloat16).reshape(narrow, HT, WD, segments)
    upstream = cotangent.astype(jnp.float32).reshape(narrow, -1)
    three_beta, three_gamma = lax.psum(
        (jnp.sum(upstream, axis=1), jnp.sum(upstream * three_normal, axis=1)), "dp"
    )
    project_gains_grad = jnp.stack([three_gamma, three_beta])
    three_delta = (project_gains[0] * three_spread)[:, None] * (
        upstream
        - (three_beta / batch_rows)[:, None]
        - three_normal * (three_gamma / batch_rows)[:, None]
    )
    delta_whole = lax.all_gather(three_delta.astype(jnp.bfloat16), "chan", axis=0, tiled=True)
    scaled_grad = lax.dot_general(
        project_low, delta_whole, contract_rows, preferred_element_type=jnp.float32
    )
    project_weight_grad = lax.dot_general(
        delta_whole, scaled, contract_cols, preferred_element_type=jnp.float32
    )
    scaled_four = scaled_grad.reshape(local_channels, HT, WD, segments)
    gating_grad = jnp.sum(scaled_four * active_two, axis=(1, 2))
    excite_delta = gating_grad * gating * (1.0 - gating)
    excite_bias_grad = jnp.sum(excite_delta, axis=1)
    excite_weight_grad = highest(hidden, excite_delta, contract_cols)
    hidden_part = highest(excite_weight, excite_delta, contract_plain)
    hidden_grad = lax.psum(hidden_part, "chan")
    squeeze_delta = hidden_grad * swish_slope(squeeze_pre)
    squeeze_bias_grad = jnp.sum(squeeze_delta, axis=1)
    squeeze_weight_grad = highest(squeeze_delta, pooled, contract_cols)
    pooled_grad = highest(squeeze_weight, squeeze_delta, contract_rows)
    active_grad = scaled_four * gating[:, None, None, :] + pooled_grad[:, None, None, :] / (HT * WD)
    two_delta = active_grad.reshape(local_channels, -1) * swish_slope(two_before)
    two_gamma, two_beta = lax.psum(
        (jnp.sum(two_delta * two_normal, axis=1), jnp.sum(two_delta, axis=1)), "dp"
    )
    depth_gains_grad = jnp.stack([two_gamma, two_beta])
    depth_grad = (depth_gains[0] * two_spread)[:, None] * (
        two_delta
        - (two_beta / batch_rows)[:, None]
        - two_normal * (two_gamma / batch_rows)[:, None]
    )
    active_one_grad, depth_weight_grad = depthwise_back(
        depth_grad.reshape(local_channels, HT, WD, segments), active_one, depth_weight
    )
    one_delta = active_one_grad.reshape(local_channels, -1) * swish_slope(one_before)
    one_gamma, one_beta = lax.psum(
        (jnp.sum(one_delta * one_normal, axis=1), jnp.sum(one_delta, axis=1)), "dp"
    )
    expand_gains_grad = jnp.stack([one_gamma, one_beta])
    expand_delta = (
        (expand_gains[0] * one_spread)[:, None]
        * (
            one_delta
            - (one_beta / batch_rows)[:, None]
            - one_normal * (one_gamma / batch_rows)[:, None]
        )
    ).astype(jnp.bfloat16)
    expand_weight_grad = lax.dot_general(
        expand_delta, flattened, contract_cols, preferred_element_type=jnp.float32
    )
    input_part = lax.psum_scatter(
        lax.dot_general(
            expand_low, expand_delta, contract_rows, preferred_element_type=jnp.float32
        ).astype(jnp.bfloat16),
        "chan",
        scatter_dimension=0,
        tiled=True,
    ).astype(jnp.float32)
    input_grad = (input_part + upstream).reshape(narrow, HT, WD, segments)
    partials = (
        expand_weight_grad,
        depth_weight_grad,
        squeeze_weight_grad,
        excite_weight_grad,
        excite_bias_grad,
        project_weight_grad,
        squeeze_bias_grad,
    )
    gains_square = (
        jnp.sum(expand_gains_grad * expand_gains_grad)
        + jnp.sum(depth_gains_grad * depth_gains_grad)
        + jnp.sum(project_gains_grad * project_gains_grad)
    )
    summed = lax.psum(
        (partials[0], partials[1], partials[2], partials[3], partials[4], partials[5], partials[6]),
        "dp",
    )
    local_square = gains_square + jnp.sum(summed[6] * summed[6]) / shards
    for member in summed[:6]:
        local_square = local_square + jnp.sum(member * member)
    total_square = lax.psum(local_square, "chan")
    grad_norm = jnp.sqrt(total_square)
    factor = clip_limit / jnp.maximum(grad_norm, clip_limit)
    weights = (
        expand_weight,
        expand_gains,
        depth_weight,
        depth_gains,
        squeeze_weight,
        squeeze_bias,
        excite_weight,
        excite_bias,
        project_weight,
        project_gains,
    )
    firsts = (
        expand_weight_first,
        expand_gains_first,
        depth_weight_first,
        depth_gains_first,
        squeeze_weight_first,
        squeeze_bias_first,
        excite_weight_first,
        excite_bias_first,
        project_weight_first,
        project_gains_first,
    )
    seconds = (
        expand_weight_second,
        expand_gains_second,
        depth_weight_second,
        depth_gains_second,
        squeeze_weight_second,
        squeeze_bias_second,
        excite_weight_second,
        excite_bias_second,
        project_weight_second,
        project_gains_second,
    )
    gradients = (
        summed[0],
        expand_gains_grad,
        summed[1],
        depth_gains_grad,
        summed[2],
        summed[6],
        summed[3],
        summed[4],
        summed[5],
        project_gains_grad,
    )
    updated = [
        adam_step(
            weights[entry],
            firsts[entry],
            seconds[entry],
            gradients[entry] * factor,
            step_rates[entry],
            decay_flags[entry],
        )
        for entry in range(10)
    ]
    return (
        block_output,
        input_grad,
        updated[0][0],
        updated[0][1],
        updated[0][2],
        updated[1][0],
        updated[1][1],
        updated[1][2],
        updated[2][0],
        updated[2][1],
        updated[2][2],
        updated[3][0],
        updated[3][1],
        updated[3][2],
        updated[4][0],
        updated[4][1],
        updated[4][2],
        updated[5][0],
        updated[5][1],
        updated[5][2],
        updated[6][0],
        updated[6][1],
        updated[6][2],
        updated[7][0],
        updated[7][1],
        updated[7][2],
        updated[8][0],
        updated[8][1],
        updated[8][2],
        updated[9][0],
        updated[9][1],
        updated[9][2],
        grad_norm,
    )


POSITIONS = HT * WD
HALF_KS = KS // 2
PAIR_LANES = 384
HIDDEN_ROWS = 32
TAPS = KS * KS
ROW_SQUEEZE = 32
ROW_EXCITE = 64
ROW_EXCITE_BIAS = 96
ROW_EXPAND_GAINS = 97
ROW_DEPTH_GAINS = 99
ROW_PROJECT_GAINS = 101
STACK_ROWS = 104
KEEP_BIASES = 64
KEEP_PROJECT = 80
KEEP_ROWS = 192
LATE_ROWS = 48
PACKED_ROWS = 96
BLOCK_ROWS = POSITIONS * 8
SENT_ROWS = 256
TAIL_ROWS = BLOCK_ROWS + PACKED_ROWS - SENT_ROWS
TAIL_LANES = 128 - C_IN
PAIRED_ROWS_LIMIT = 3072
contract_lanes = (((1,), (1,)), ((), ()))
f32 = jnp.float32
bf16 = jnp.bfloat16


def paired_fits(mesh):
    return mesh.shape["chan"] == 4 and mesh.shape["dp"] * POSITIONS * 8 <= PAIRED_ROWS_LIMIT


def dot(left, right, numbers):
    return lax.dot_general(left, right, numbers, preferred_element_type=f32)


def split_dot(left, right, numbers):
    left_high, right_high = left.astype(bf16), right.astype(bf16)
    left_low = (left - left_high.astype(f32)).astype(bf16)
    right_low = (right - right_high.astype(f32)).astype(bf16)
    mixed = dot(left_high, right_low, numbers) + dot(left_low, right_high, numbers)
    return dot(left_high, right_high, numbers) + mixed


def rows_sum(values):
    return jnp.broadcast_to(jnp.sum(values, axis=0, keepdims=True), (8, values.shape[1]))


def lane_tile(index, start=0):
    if isinstance(start, int):
        return slice(start + index * 128, start + index * 128 + 128)
    return pl.ds(pl.multiple_of(start + index * 128, 128), 128)


def swish_of_half(half):
    return half * jnp.tanh(half) + half


def slope_of_half(half):
    bent = jnp.tanh(half)
    up = 1.0 + bent
    return 0.5 * up * (1.0 + half * (1.0 - bent))


PRODUCTS = 9
FILTER_SIGNS = (
    ((2, 1),),
    ((3, 1), (2, -1)),
    ((1, 1), (2, -1)),
    ((4, 1), (2, -1)),
    ((2, 1), (3, -1), (4, -1)),
    ((2, 1), (3, 1), (1, -1), (4, -1)),
    ((0, 1), (2, -1)),
    ((2, 1), (1, 1), (3, -1), (0, -1)),
    ((2, 1), (1, -1), (0, -1)),
)


def signed(terms):
    total = None
    for value, sign in terms:
        if total is None:
            total = value if sign > 0 else -value
        else:
            total = total + value if sign > 0 else total - value
    return total


def product_filters(taps, out_ref):
    for i in range(KS):
        for at, signs in enumerate(FILTER_SIGNS):
            value = signed([(taps(i, column), sign) for column, sign in signs])
            out_ref[i * PRODUCTS + at] = jnp.broadcast_to(value, out_ref.shape[1:])


def product_inputs(field):
    rows = []
    for row in range(HT):
        x0, x1, x2, x3 = field[row * WD : row * WD + WD]
        even, odd = x0 + x2, x1 + x3
        rows.append((even + odd, odd, even, x2 + x3, x3, x2, x0 + x1, x1, x0))
    return list(zip(*rows))


def product_targets(inputs):
    both, odd, even, right, x3, x2, left, x1, x0 = inputs
    return (both, even, odd, left, x0, x1, right, x2, x3)


def rows_of(row):
    return [(i, row + i - HALF_KS) for i in range(KS) if 0 <= row + i - HALF_KS < HT]


def product_sum(filters, inputs):
    sums = []
    for at in range(PRODUCTS):
        weights = [filters(i * PRODUCTS + at) for i in range(KS)]
        found = []
        for row in range(HT):
            value = None
            for i, source in rows_of(row):
                term = weights[i] * inputs[at][source]
                value = term if value is None else value + term
            found.append(value)
        sums.append(found)
    return sums


def product_outputs(sums, row):
    q = [found[row] for found in sums]
    near_0, near_1 = q[0] + q[1], q[0] + q[2]
    return (
        near_0 + (q[3] + q[4]), near_1 + (q[3] + q[5]), near_0 + (q[6] + q[7]), near_1 + (q[6] + q[8])
    )


def in_order(position, own, near, far, cross):
    first = position % 2 == 0
    front = position // 2 == 0
    low, high = jnp.where(first, own, near), jnp.where(first, near, own)
    far_low, far_high = jnp.where(first, far, cross), jnp.where(first, cross, far)
    return (
        jnp.where(front, low, far_low), jnp.where(front, high, far_high),
        jnp.where(front, far_low, low), jnp.where(front, far_high, high),
    )


def matrix_in_order(position, refs, start, channels):
    parts = in_order(position, *[ref[start : start + channels, :].astype(f32) for ref in refs])
    gap = jnp.zeros((PAIR_LANES - 2 * channels, C_IN), f32)
    return jnp.concatenate([*parts[0:2], gap, *parts[2:4], gap], axis=0).astype(bf16)


def first_kernel(
    index_ref, matrix_0, matrix_1, matrix_2, matrix_3, x_ref, _after_ref,
    expanded_ref, sums_ref, we_ref, keep_ref, send_ref,
):
    blocks = x_ref.shape[0]
    width = we_ref.shape[0]
    refs = (matrix_0, matrix_1, matrix_2, matrix_3)
    we_ref[...] = matrix_in_order(index_ref[1], refs, 0, matrix_0.shape[0] // 2)
    tail = None
    for piece in range(C_IN // TAIL_LANES):
        rows = x_ref[:, piece * TAIL_ROWS : (piece + 1) * TAIL_ROWS, :].reshape(-1, 128)
        move = one_hot(
            128, C_IN, lambda r, c: (r - C_IN == c - piece * TAIL_LANES) & (r >= C_IN)
        ).astype(bf16)
        part = dot(rows, move, contract_plain)
        tail = part if tail is None else tail + part
    packed = jnp.concatenate(
        [
            x_ref[:, BLOCK_ROWS:SENT_ROWS, 0:C_IN].astype(f32),
            tail.reshape(blocks, TAIL_ROWS, C_IN),
        ],
        axis=1,
    )
    packed = packed.reshape(blocks * PACKED_ROWS // 16, 2, 8, C_IN)
    first = index_ref[1] % 2 == 0
    for ref, at in ((keep_ref, 0), (send_ref, 1)):
        half = jnp.where(first, packed[:, at], packed[:, 1 - at])
        ref[...] = half.reshape(blocks, PACKED_ROWS // 2, C_IN).astype(bf16)
    for lanes in (slice(at, at + 256) for at in range(0, width, 256)):
        total = jnp.zeros((8, 256), f32)
        square = jnp.zeros((8, 256), f32)
        for block in range(blocks):
            value = dot(x_ref[block, 0:BLOCK_ROWS, 0:C_IN], we_ref[lanes, :], contract_lanes)
            expanded_ref[block, :, lanes] = value
            shaped = value.reshape(POSITIONS, 8, 256)
            total = total + jnp.sum(shaped, axis=0)
            square = square + jnp.sum(shaped * shaped, axis=0)
        sums_ref[0:8, lanes] = total
        sums_ref[8:16, lanes] = square


def norm_factors(total_rows, sums_own, sums_other, gain, shift, norm_ref):
    average = rows_sum(sums_own[0:8] + sums_other[0:8]) / total_rows
    squares = rows_sum(sums_own[8:16] + sums_other[8:16]) / total_rows
    spread = lax.rsqrt(squares - average * average + norm_epsilon)
    gain = gain * spread
    norm_ref[0:8, :] = 0.5 * gain
    norm_ref[8:16, :] = 0.5 * (shift - average * gain)
    norm_ref[16:24, :] = average
    norm_ref[24:32, :] = spread


def expand_kernel(
    total_rows, expanded_ref, sums_own, sums_other, stack_ref, depth_ref, sums_ref, norm_ref, taps_scr
):
    blocks, _, width = expanded_ref.shape
    norm_factors(
        total_rows, sums_own, sums_other, stack_ref[ROW_EXPAND_GAINS : ROW_EXPAND_GAINS + 1, :],
        stack_ref[ROW_EXPAND_GAINS + 1 : ROW_EXPAND_GAINS + 2, :], norm_ref,
    )
    product_filters(lambda i, j: stack_ref[i * KS + j : i * KS + j + 1, :], taps_scr)
    sums_ref[...] = jnp.zeros_like(sums_ref)

    def one_block(block, carry):
        for tile in range(width // 128):
            lanes = lane_tile(tile)
            gain_half = norm_ref[0:8, lanes]
            shift_half = norm_ref[8:16, lanes]
            active = [
                swish_of_half(expanded_ref[block, 8 * at : 8 * at + 8, lanes] * gain_half + shift_half)
                for at in range(POSITIONS)
            ]
            total = jnp.zeros((8, 128), f32)
            square = jnp.zeros((8, 128), f32)
            sums = product_sum(lambda at: taps_scr[at, :, lanes], product_inputs(active))
            for row in range(HT):
                for col, value in enumerate(product_outputs(sums, row)):
                    at = row * WD + col
                    depth_ref[block, 8 * at : 8 * at + 8, lanes] = value
                    total = total + value
                    square = square + value * value
            sums_ref[0:8, lanes] += total
            sums_ref[8:16, lanes] += square
        return carry

    lax.fori_loop(0, blocks, one_block, 0)


def squeeze_kernel(
    total_rows, depth_ref, sums_own, sums_other, stack_ref, wp_ref, cot_ref, bias_ref,
    projected_ref, scaled_ref, sums_ref, gate_ref, before_ref, pooled_ref, norm_ref, active_ref,
):
    blocks, _, width = depth_ref.shape
    norm_factors(
        total_rows, sums_own, sums_other, stack_ref[ROW_DEPTH_GAINS : ROW_DEPTH_GAINS + 1, :],
        stack_ref[ROW_DEPTH_GAINS + 1 : ROW_DEPTH_GAINS + 2, :], norm_ref,
    )

    def pool_block(block):
        for tile in range(width // 128):
            lanes = lane_tile(tile)
            gain_half = norm_ref[0:8, lanes]
            shift_half = norm_ref[8:16, lanes]
            total = jnp.zeros((8, 128), f32)
            for at in range(POSITIONS):
                value = swish_of_half(
                    depth_ref[block, 8 * at : 8 * at + 8, lanes] * gain_half + shift_half
                )
                active_ref[block, 8 * at : 8 * at + 8, lanes] = value
                total = total + value
            pooled_ref[slice(8 * block, 8 * block + 8), lanes] = total / POSITIONS

    for block in range(blocks):
        pool_block(block)
    squeeze = stack_ref[ROW_SQUEEZE : ROW_SQUEEZE + HIDDEN_ROWS, :]
    excite = stack_ref[ROW_EXCITE : ROW_EXCITE + HIDDEN_ROWS, :]
    before = split_dot(pooled_ref[...], squeeze, contract_lanes) + bias_ref[...]
    before_ref[...] = before
    hidden = swish_of_half(0.5 * before)
    raised = split_dot(hidden, excite, contract_plain)
    raised = raised + stack_ref[ROW_EXCITE_BIAS : ROW_EXCITE_BIAS + 1, :]
    gate_ref[...] = 0.5 + 0.5 * jnp.tanh(0.5 * raised)
    totals = [jnp.zeros((8, C_IN), f32)] * 4
    for block in range(blocks):
        for tile in range(width // 128):
            lanes = lane_tile(tile)
            gate = gate_ref[8 * block : 8 * block + 8, lanes]
            value = active_ref[block, :, lanes].reshape(POSITIONS, 8, 128) * gate[None]
            scaled_ref[block, :, lanes] = value.reshape(BLOCK_ROWS, 128).astype(bf16)
        projected = dot(scaled_ref[block], wp_ref[...], contract_plain)
        projected_ref[block] = projected
        shaped = projected.reshape(POSITIONS, 8, C_IN)
        upstream = cot_ref[block].astype(f32).reshape(POSITIONS, 8, C_IN)
        terms = (shaped, shaped * shaped, shaped * upstream, upstream)
        totals = [total + jnp.sum(term, axis=0) for total, term in zip(totals, terms)]
    for at in range(4):
        sums_ref[8 * at : 8 * at + 8, :] = totals[at]


def gate_back_kernel(
    total_rows, index_ref, projected_ref, cot_ref, sums_own, sums_other, gains_ref, depth_ref,
    norm_ref, stack_ref, wp_ref, gate_ref, before_ref, pooled_ref, scaled_ref, active_ref, x_ref,
    two_ref, sums_ref, lanes_ref, gains_grad_ref,
    delta_scr, grad_scr, gate_grad_scr, pooled_scr,
):
    blocks = depth_ref.shape[0]
    width = depth_ref.shape[2]
    own = pl.multiple_of(index_ref[1] // 2 * PAIR_LANES, 128)
    own_lanes = pl.ds(own, PAIR_LANES)
    sums = [rows_sum(sums_own[8 * k : 8 * k + 8] + sums_other[8 * k : 8 * k + 8])[0:1] for k in range(4)]
    average = sums[0] / total_rows
    spread = lax.rsqrt(sums[1] / total_rows - average * average + norm_epsilon)
    beta = sums[3]
    gamma = spread * (sums[2] - average * beta)
    gains_grad_ref[0:1, :] = gamma
    gains_grad_ref[1:2, :] = beta
    gain = gains_ref[0:1, :]
    shift = gains_ref[1:2, :]
    mine = index_ref[0]
    output = x_ref[mine, 0:BLOCK_ROWS, 0:C_IN].astype(f32)
    output = output + ((projected_ref[mine] - average) * spread * gain + shift)
    lanes_ref[:, PAIR_LANES : PAIR_LANES + C_IN] = output
    outer = gain * spread

    for block in range(blocks):
        normal = (projected_ref[block] - average) * spread
        delta = outer * (
            cot_ref[block].astype(f32) - beta / total_rows - normal * (gamma / total_rows)
        )
        delta_scr[block] = delta.astype(bf16)
    for block in range(blocks):
        for lanes in (slice(at, at + 256) for at in range(0, width, 256)):
            value = dot(delta_scr[block], wp_ref[lanes, :], contract_lanes)
            grad_scr[block, :, lanes] = value
            value = (value * active_ref[block, :, lanes]).reshape(POSITIONS, 8, 256)
            gate_grad_scr[8 * block : 8 * block + 8, lanes] = jnp.sum(value, axis=0)
    excite = stack_ref[ROW_EXCITE : ROW_EXCITE + HIDDEN_ROWS, :]
    gate = gate_ref[...]
    gate_grad_scr[...] = gate_grad_scr[...] * gate * (1.0 - gate)
    half = 0.5 * before_ref[...]
    hidden = swish_of_half(half)
    squeeze_delta = split_dot(gate_grad_scr[...], excite, contract_lanes) * slope_of_half(half)
    own_delta = gate_grad_scr[:, own_lanes]
    lanes_ref[0:HIDDEN_ROWS, 0:PAIR_LANES] = split_dot(squeeze_delta, pooled_ref[:, own_lanes], contract_rows)
    lanes_ref[HIDDEN_ROWS : 2 * HIDDEN_ROWS, 0:PAIR_LANES] = split_dot(hidden, own_delta, contract_rows)
    lanes_ref[KEEP_BIASES : KEEP_BIASES + 8, 0:PAIR_LANES] = rows_sum(own_delta)
    lanes_ref[KEEP_BIASES + 8 : KEEP_BIASES + 16, 0:PAIR_LANES] = jnp.zeros((8, PAIR_LANES), f32)
    lanes_ref[KEEP_BIASES + 8 : KEEP_BIASES + 16, 0:HIDDEN_ROWS] = rows_sum(squeeze_delta)
    squeeze = stack_ref[ROW_SQUEEZE : ROW_SQUEEZE + HIDDEN_ROWS, own_lanes]
    pooled_scr[...] = split_dot(squeeze_delta, squeeze, contract_plain) / POSITIONS
    sums_ref[...] = jnp.zeros_like(sums_ref)

    def two_block(block):
        rows = slice(8 * block, 8 * block + 8)
        for tile in range(PAIR_LANES // 128):
            lanes = lane_tile(tile)
            whole = lane_tile(tile, own)
            gain_half = norm_ref[0:8, whole]
            shift_half = norm_ref[8:16, whole]
            average = norm_ref[16:24, whole]
            gate = 0.5 * gate_ref[rows, whole]
            pooled_grad = 0.5 * pooled_scr[rows, lanes]
            total = jnp.zeros((8, 128), f32)
            product = jnp.zeros((8, 128), f32)
            for at in range(POSITIONS):
                spot = slice(8 * at, 8 * at + 8)
                depth = depth_ref[block, spot, whole]
                bent = jnp.tanh(depth * gain_half + shift_half)
                slope = (1.0 + bent) + active_ref[block, spot, whole] * (1.0 - bent)
                value = (grad_scr[block, spot, whole] * gate + pooled_grad) * slope
                two_ref[block, spot, lanes] = value
                total = total + value
                product = product + value * (depth - average)
            sums_ref[0:8, lanes] += total
            sums_ref[8:16, lanes] += product

    for block in range(blocks):
        two_block(block)
    rows = blocks * POSITIONS * 8
    lanes_ref[KEEP_PROJECT : KEEP_PROJECT + C_IN, 0:PAIR_LANES] = dot(
        delta_scr[...].reshape(rows, C_IN), scaled_ref[:, :, own_lanes].reshape(rows, PAIR_LANES), contract_rows
    )


def depth_back_kernel(
    total_rows, index_ref, sums_own, sums_other, two_ref, depth_ref, expanded_ref, stack_ref,
    norm_one_ref, norm_two_ref,
    one_ref, sums_ref, gains_grad_ref, taps_scr, kernel_scr, factors_scr,
):
    blocks = depth_ref.shape[0]
    own = pl.multiple_of(index_ref[1] // 2 * PAIR_LANES, 128)
    own_lanes = pl.ds(own, PAIR_LANES)
    spread = norm_two_ref[24:32, own_lanes]
    average = norm_two_ref[16:24, own_lanes]
    beta = rows_sum(sums_own[0:8] + sums_other[0:8])
    gamma = rows_sum(sums_own[8:16] + sums_other[8:16]) * spread
    gains_grad_ref[0:1, :] = gamma[0:1]
    gains_grad_ref[1:2, :] = beta[0:1]
    outer = stack_ref[ROW_DEPTH_GAINS : ROW_DEPTH_GAINS + 1, own_lanes] * spread
    slope = outer * spread * gamma / total_rows
    factors_scr[0:8, :] = outer
    factors_scr[8:16, :] = slope
    factors_scr[16:24, :] = outer * (beta / total_rows) - slope * average
    product_filters(
        lambda i, j: 0.5 * stack_ref[TAPS - 1 - i * KS - j : TAPS - i * KS - j, own_lanes], taps_scr
    )
    sums_ref[...] = jnp.zeros_like(sums_ref)
    kernel_scr[...] = jnp.zeros_like(kernel_scr)

    def one_block(block, carry):
        for tile in range(PAIR_LANES // 128):
            lanes = lane_tile(tile)
            whole = lane_tile(tile, own)
            gain_half = norm_one_ref[0:8, whole]
            shift_half = norm_one_ref[8:16, whole]
            average_one = norm_one_ref[16:24, whole]
            outer = factors_scr[0:8, lanes]
            slope = factors_scr[8:16, lanes]
            level = factors_scr[16:24, lanes]
            grads = []
            active = []
            bents = []
            for at in range(POSITIONS):
                spot = slice(8 * at, 8 * at + 8)
                grads.append(
                    outer * two_ref[block, spot, lanes]
                    - level
                    - slope * depth_ref[block, spot, whole]
                )
                half = expanded_ref[block, spot, whole] * gain_half + shift_half
                bents.append(jnp.tanh(half))
                active.append(half * bents[at] + half)
            sources = product_inputs(active)
            inputs = product_inputs(grads)
            targets = product_targets(inputs)
            for at in range(PRODUCTS):
                for i in range(KS):
                    value = None
                    for row in range(HT):
                        if 0 <= row + i - HALF_KS < HT:
                            term = targets[at][row] * sources[at][row + i - HALF_KS]
                            value = term if value is None else value + term
                    kernel_scr[i * PRODUCTS + at, :, lanes] += value
            sums = product_sum(lambda at: taps_scr[at, :, lanes], inputs)
            total = jnp.zeros((8, 128), f32)
            product = jnp.zeros((8, 128), f32)
            for row in range(HT):
                for col, value in enumerate(product_outputs(sums, row)):
                    at = row * WD + col
                    spot = slice(8 * at, 8 * at + 8)
                    expanded = expanded_ref[block, spot, whole]
                    value = value * ((1.0 + bents[at]) + active[at] * (1.0 - bents[at]))
                    one_ref[block, spot, lanes] = value
                    total = total + value
                    product = product + value * (expanded - average_one)
            sums_ref[0:8, lanes] += total
            sums_ref[8:16, lanes] += product
        return carry

    lax.fori_loop(0, blocks, one_block, 0)
    for i in range(KS):
        for j in range(KS):
            terms = [
                (jnp.sum(kernel_scr[i * PRODUCTS + at], axis=0, keepdims=True), sign)
                for at, signs in enumerate(FILTER_SIGNS)
                for column, sign in signs
                if column == j
            ]
            row = 16 + i * KS + j
            sums_ref[row : row + 1, :] = signed(terms)


def expand_back_kernel(
    total_rows, index_ref, sums_own, sums_other, one_ref, expanded_ref, x_ref, we_ref, stack_ref, norm_ref,
    _lanes_ref,
    late_ref, gains_grad_ref, delta_scr,
):
    blocks = x_ref.shape[0]
    own = pl.multiple_of(index_ref[1] // 2 * PAIR_LANES, 128)
    own_lanes = pl.ds(own, PAIR_LANES)
    spread = norm_ref[24:32, own_lanes]
    average = norm_ref[16:17, own_lanes]
    beta = rows_sum(sums_own[0:8] + sums_other[0:8])
    gamma = rows_sum(sums_own[8:16] + sums_other[8:16]) * spread
    gains_grad_ref[0:1, :] = gamma[0:1]
    gains_grad_ref[1:2, :] = beta[0:1]
    outer = stack_ref[ROW_EXPAND_GAINS : ROW_EXPAND_GAINS + 1, own_lanes] * spread[0:1]
    slope = outer * spread[0:1] * gamma[0:1] / total_rows
    level = outer * (beta[0:1] / total_rows)
    own_weights = we_ref[own_lanes, :]

    for block in range(blocks):
        centred = expanded_ref[block, :, own_lanes] - average
        delta = outer * one_ref[block] - level - slope * centred
        delta_scr[block] = delta.astype(bf16)
    rows = blocks * POSITIONS * 8
    late_ref[0:C_IN, 0:PAIR_LANES] = dot(
        x_ref[:, 0:BLOCK_ROWS, 0:C_IN].reshape(rows, C_IN), delta_scr[...].reshape(rows, PAIR_LANES), contract_rows
    )
    part = dot(delta_scr[index_ref[0]], own_weights, contract_plain)
    for group in range(4):
        late_ref[C_IN : C_IN + LATE_ROWS, group * 128 : group * 128 + C_IN] = part[
            group * LATE_ROWS : (group + 1) * LATE_ROWS
        ]


def one_hot(rows, columns, matches):
    return matches(
        lax.broadcasted_iota(jnp.int32, (rows, columns), 0),
        lax.broadcasted_iota(jnp.int32, (rows, columns), 1),
    )


def copies_kernel(index_ref, rows_ref, cot_ref, copies_ref):
    whole = rows_ref[...].astype(f32)
    half = jnp.where(index_ref[1] % 2 == 0, whole[:, 0:8, :], whole[:, 8:16, :])
    half = half.reshape(BLOCK_ROWS, C_IN)
    narrow = cot_ref.shape[2]
    rows = cot_ref[...].reshape(4 * PACKED_ROWS, narrow)
    packed = None
    for group in range(4):
        place = one_hot(narrow, C_IN, lambda r, c: c == r + group * narrow).astype(bf16)
        part = dot(rows[group * PACKED_ROWS : (group + 1) * PACKED_ROWS], place, contract_plain)
        packed = part if packed is None else packed + part
    value = jnp.concatenate([half, packed], axis=0).astype(bf16)
    widen = one_hot(C_IN, 128, lambda r, c: r == c).astype(bf16)
    dense = dot(value[0:SENT_ROWS], widen, contract_plain)
    parts = []
    for piece in range(SENT_ROWS // TAIL_ROWS):
        move = one_hot(
            C_IN, 128, lambda r, c: (c - C_IN == r - piece * TAIL_LANES) & (c >= C_IN)
        ).astype(bf16)
        parts.append(dot(value[SENT_ROWS:], move, contract_plain))
    dense = (dense + jnp.concatenate(parts, axis=0)).astype(bf16)
    for at in range(copies_ref.shape[0]):
        copies_ref[at] = dense


def cot_kernel(index_ref, own_ref, near_ref, far_ref, cross_ref, cot_ref):
    position = index_ref[1]
    near = position + 1 - position % 2 * 2
    blocks = cot_ref.shape[0]
    narrow = C_IN // 4
    rows = blocks * PACKED_ROWS // 2
    pieces = (
        (own_ref, position), (near_ref, near), (far_ref, (position + 2) % 4),
        (cross_ref, (near + 2) % 4),
    )
    for group in range(4):
        total = None
        for ref, place in pieces:
            move = one_hot(
                C_IN,
                C_IN,
                lambda r, c: (c - place * narrow == r - group * narrow)
                & (r >= group * narrow) & (r < (group + 1) * narrow),
            ).astype(bf16)
            part = dot(ref[...].reshape(rows, C_IN), move, contract_plain)
            total = part if total is None else total + part
        half = total.reshape(blocks, PACKED_ROWS // 2, C_IN).astype(bf16)
        start = group * (PACKED_ROWS // 2)
        cot_ref[:, start : start + PACKED_ROWS // 2, :] = half


def pack_kernel(
    expand_ref, project_ref, depth_ref, squeeze_ref, excite_ref, excite_bias_ref, expand_gains_ref,
    depth_gains_ref, project_gains_ref, stack_ref, matrix_ref,
):
    channels = expand_ref.shape[0]
    narrow = project_gains_ref.shape[1]
    stack_ref[...] = jnp.zeros_like(stack_ref)
    for start, ref in (
        (0, depth_ref), (ROW_SQUEEZE, squeeze_ref), (ROW_EXCITE, excite_ref),
        (ROW_EXCITE_BIAS, excite_bias_ref), (ROW_EXPAND_GAINS, expand_gains_ref),
        (ROW_DEPTH_GAINS, depth_gains_ref),
    ):
        stack_ref[start : start + ref.shape[0], :] = ref[...]
    stack_ref[ROW_PROJECT_GAINS : ROW_PROJECT_GAINS + 2, 0:narrow] = project_gains_ref[...]
    matrix_ref[...] = jnp.concatenate(
        [expand_ref[...], project_ref[...]], axis=0
    ).astype(bf16)


def assemble_kernel(
    index_ref, stack_0, stack_1, stack_2, stack_3, matrix_0, matrix_1, matrix_2, matrix_3,
    stack_ref, project_ref, gains_ref,
):
    channels = stack_0.shape[1]
    narrow = C_IN // 4
    stacks = in_order(index_ref[1], stack_0[...], stack_1[...], stack_2[...], stack_3[...])
    stack_ref[...] = jnp.zeros_like(stack_ref)
    for place in range(4):
        start = place // 2 * PAIR_LANES + place % 2 * channels
        stack_ref[:, start : start + channels] = stacks[place]
        gains_ref[:, place * narrow : (place + 1) * narrow] = stacks[place][
            ROW_PROJECT_GAINS : ROW_PROJECT_GAINS + 2, 0:narrow
        ]
    refs = (matrix_0, matrix_1, matrix_2, matrix_3)
    project_ref[...] = matrix_in_order(index_ref[1], refs, channels, channels)


def kept_sums(keep_own, keep_other, sums_own, sums_other):
    def both(start, stop):
        return keep_own[start:stop, 0:PAIR_LANES] + keep_other[start:stop, 0:PAIR_LANES]

    return (
        both(KEEP_PROJECT, KEEP_PROJECT + C_IN), both(0, 2 * HIDDEN_ROWS),
        sums_own[16 : 16 + TAPS, :] + sums_other[16 : 16 + TAPS, :],
        both(KEEP_BIASES, KEEP_BIASES + 1), both(KEEP_BIASES + 8, KEEP_BIASES + 9)[:, 0:HIDDEN_ROWS],
    )


def input_rows(late_ref):
    return jnp.concatenate(
        [
            late_ref[C_IN : C_IN + LATE_ROWS, group * 128 : group * 128 + C_IN]
            for group in range(4)
        ],
        axis=0,
    )


def expand_sum(late_own, late_other):
    return late_own[0:C_IN, 0:PAIR_LANES] + late_other[0:C_IN, 0:PAIR_LANES]


def both_halves(first, own, other):
    own = own.reshape(POSITIONS, 8, own.shape[-1])
    other = other.reshape(POSITIONS, 8, other.shape[-1])
    return jnp.concatenate(
        [jnp.where(first, own, other), jnp.where(first, other, own)], axis=1
    )


def settle_kernel(
    index_ref, late_own, late_other, keep_own, keep_other, sums_own, sums_other, three_ref, two_ref, one_ref,
    square_ref, packed_ref,
):
    position = index_ref[1]
    narrow = C_IN // 4

    def squared(values):
        return jnp.sum(jnp.sum(values * values, axis=0, keepdims=True), axis=1, keepdims=True)

    project, hidden, kernel, excite_bias, bias = kept_sums(keep_own, keep_other, sums_own, sums_other)
    total = squared(expand_sum(late_own, late_other)) + squared(project) + squared(hidden)
    total = total + squared(kernel) + squared(excite_bias)
    total = total + squared(one_ref[...]) + squared(two_ref[...])
    square_ref[0:8, :] = jnp.broadcast_to(total, (8, 128))
    square_ref[8:16, :] = jnp.broadcast_to(squared(bias) + squared(three_ref[...]), (8, 128))
    whole = both_halves(position % 2 == 0, input_rows(late_own), input_rows(late_other))
    whole = whole.reshape(4 * PACKED_ROWS, C_IN).astype(bf16)
    across = position + 2 - position // 2 * 4
    packed = None
    for group in range(4):
        move = one_hot(
            C_IN,
            C_IN,
            lambda r, c: (r - across * narrow == c - group * narrow)
            & (c >= group * narrow) & (c < (group + 1) * narrow),
        ).astype(bf16)
        part = dot(whole[group * PACKED_ROWS : (group + 1) * PACKED_ROWS], move, contract_plain)
        packed = part if packed is None else packed + part
    packed_ref[0:PACKED_ROWS, :] = packed.astype(bf16)
    rest = jnp.broadcast_to(total, (16, C_IN))
    parts = jnp.zeros((16, C_IN), f32)
    row = lax.broadcasted_iota(jnp.int32, (16, C_IN), 0)
    for at in range(3):
        part = rest.astype(bf16).astype(f32)
        rest = rest - part
        parts = jnp.where(row == at, part, parts)
    packed_ref[PACKED_ROWS : PACKED_ROWS + 16, :] = parts.astype(bf16)


def own_kernel(
    index_ref, late_own, late_other, keep_own, keep_other, sums_own, sums_other, two_ref, one_ref, *refs
):
    params, outs = refs[:30], refs[36:]
    expand_ref, project_ref, lanes_ref, bias_ref, input_ref, output_ref = refs[30:36]
    for entry in range(10):
        shrink = 1.0 - step_rates[entry] * decay_flags[entry] * decay_rate
        for part, scale in enumerate((shrink, beta_first, beta_second)):
            outs[3 * entry + part][...] = scale * params[3 * entry + part][...]
    position = index_ref[1]
    first = position % 2 == 0
    channels = expand_ref.shape[0]
    narrow = C_IN // 4

    def mine(values):
        return jnp.where(first, values[:, 0:channels], values[:, channels : 2 * channels])

    project, hidden, kernel, excite_bias, bias = kept_sums(keep_own, keep_other, sums_own, sums_other)
    bias_ref[...] = bias
    expand_ref[...] = jnp.transpose(mine(expand_sum(late_own, late_other)))
    project_ref[...] = jnp.transpose(mine(project))
    lanes_ref[0:TAPS, :] = mine(kernel)
    lanes_ref[ROW_SQUEEZE : ROW_SQUEEZE + 2 * HIDDEN_ROWS, :] = mine(hidden)
    lanes_ref[ROW_EXCITE_BIAS : ROW_EXCITE_BIAS + 1, :] = mine(excite_bias)
    lanes_ref[ROW_EXPAND_GAINS : ROW_EXPAND_GAINS + 2, :] = mine(one_ref[...])
    lanes_ref[ROW_DEPTH_GAINS : ROW_DEPTH_GAINS + 2, :] = mine(two_ref[...])
    pick = one_hot(C_IN, narrow, lambda r, c: r == c + position * narrow)
    halves = [
        highest(input_rows(ref), pick.astype(f32), contract_plain) for ref in (late_own, late_other)
    ]
    input_ref[...] = both_halves(first, *halves)
    halves = [
        dot(ref[:, PAIR_LANES : PAIR_LANES + C_IN].astype(bf16), pick.astype(bf16), contract_plain)
        for ref in (keep_own, keep_other)
    ]
    output_ref[...] = both_halves(first, *halves).astype(bf16)


def adam_kernel(
    index_ref, square_ref, expand_grad, project_grad, lanes_grad, bias_grad, three_grad,
    input_own, packed_other, cot_ref, *refs,
):
    params, outs = refs[:30], refs[30:]
    narrow = cot_ref.shape[2]
    parts = packed_other[PACKED_ROWS : PACKED_ROWS + 16, :].astype(f32)
    other = (parts[0:1, 0:1] + parts[1:2, 0:1]) + parts[2:3, 0:1]
    total = square_ref[0:1, 0:1] + other + square_ref[8:9, 0:1]
    grad_norm = jnp.sqrt(total)
    factor = clip_limit / jnp.maximum(grad_norm, clip_limit)
    outs[31][...] = grad_norm
    groups = []
    for group in range(4):
        pick = one_hot(C_IN, narrow, lambda r, c: r == c + group * narrow).astype(bf16)
        groups.append(dot(packed_other[0:PACKED_ROWS, :], pick, contract_plain))
    crossed = jnp.concatenate(groups, axis=0).reshape(POSITIONS, 16, narrow)
    outs[0][...] = input_own[...] + crossed + cot_ref[...].astype(f32)
    pick = one_hot(C_IN, narrow, lambda r, c: r == c + index_ref[1] * narrow).astype(f32)
    gradients = (
        expand_grad[...],
        lanes_grad[ROW_EXPAND_GAINS : ROW_EXPAND_GAINS + 2, :],
        lanes_grad[0:TAPS, :],
        lanes_grad[ROW_DEPTH_GAINS : ROW_DEPTH_GAINS + 2, :],
        lanes_grad[ROW_SQUEEZE : ROW_SQUEEZE + params[12].shape[0], :],
        bias_grad[:, 0 : params[15].shape[1]],
        lanes_grad[ROW_EXCITE : ROW_EXCITE + params[18].shape[0], :],
        lanes_grad[ROW_EXCITE_BIAS : ROW_EXCITE_BIAS + 1, :],
        project_grad[...],
        highest(three_grad[0:2, :], pick, contract_plain),
    )
    for entry in range(10):
        gradient = gradients[entry] * factor
        first_new = params[3 * entry + 1][...] + (1.0 - beta_first) * gradient
        second_new = params[3 * entry + 2][...] + (1.0 - beta_second) * gradient * gradient
        first_hat = first_new / (1.0 - beta_first**STEP)
        second_hat = second_new / (1.0 - beta_second**STEP)
        step = first_hat / (jnp.sqrt(second_hat) + adam_epsilon)
        updated = (params[3 * entry][...] - step_rates[entry] * step, first_new, second_new)
        for part in range(3):
            outs[1 + 3 * entry + part][...] = updated[part]


def call(kernel, outs, operands, scratch=(), name=None, keep=True, place=True, after=(), plain=()):
    spaces = [
        pl.BlockSpec(memory_space=pltpu.SMEM)
        if operand.dtype == jnp.int32
        else pl.BlockSpec(memory_space=pltpu.VMEM)
        for operand in operands
    ]
    spaces += [pl.BlockSpec(memory_space=pltpu.VMEM)] * len(plain)
    spaces += [pl.BlockSpec(memory_space=pl.ANY)] * len(after)
    operands = [
        operand
        if operand.dtype == jnp.int32
        else pltpu.with_memory_space_constraint(operand, pltpu.VMEM if place else pltpu.HBM)
        for operand in operands
    ] + [pltpu.with_memory_space_constraint(operand, pltpu.HBM) for operand in (*plain, *after)]
    limit = 4 * 1024 * 1024 + sum(4 * math.prod(shape) for shape, _ in scratch)
    made = pltpu.VMEM if keep else jax.ShapeDtypeStruct
    return pl.pallas_call(
        kernel,
        out_shape=[
            (jax.ShapeDtypeStruct if out[2:] else made)(out[0], out[1]) for out in outs
        ],
        in_specs=spaces,
        out_specs=[pl.BlockSpec(memory_space=pltpu.VMEM)] * len(outs),
        scratch_shapes=[pltpu.VMEM(shape, dtype) for shape, dtype in scratch],
        compiler_params=pltpu.CompilerParams(vmem_limit_bytes=limit),
        name=name,
    )(*operands)


def on_device_paired(*arrays):
    block_input, cotangent = arrays[:2]
    segments = block_input.shape[3]
    if segments != 16:
        return on_device(*arrays)
    params = list(arrays[2:])
    for at in (15, 16, 17, 21, 22, 23):
        params[at] = params[at][None]
    for at in (24, 25, 26):
        params[at] = params[at].T
    (
        expand_weight, expand_gains, depth_weight, depth_gains, squeeze_weight,
        squeeze_bias, excite_weight, excite_bias, project_weight, project_gains,
    ) = params[::3]
    shards = lax.axis_size("dp")
    index = jnp.stack([lax.axis_index("dp"), lax.axis_index("chan")]).astype(jnp.int32)
    total_rows = float(POSITIONS * segments * shards)
    narrow = cotangent.shape[0]
    channels = expand_weight.shape[0]
    rows = POSITIONS * 8
    width = 2 * PAIR_LANES

    def swap(values, mask):
        return lax.ppermute(values, "chan", [(at, at ^ mask) for at in range(4)])

    input_rows = jnp.transpose(block_input, (1, 2, 3, 0)).reshape(POSITIONS, segments, C_IN)
    cot_rows = jnp.transpose(cotangent, (1, 2, 3, 0)).reshape(POSITIONS, segments, narrow)
    (copies,) = call(
        copies_kernel,
        [((shards, SENT_ROWS, 128), bf16)],
        [index, input_rows, cot_rows],
        name="copies",
        keep=False,
        place=False,
    )
    x = lax.all_to_all(copies, "dp", 0, 0)
    stack, matrix = call(
        pack_kernel,
        [((STACK_ROWS, channels), f32), ((2 * channels, C_IN), bf16)],
        [
            expand_weight, project_weight, depth_weight, squeeze_weight, excite_weight, excite_bias,
            expand_gains, depth_gains, project_gains,
        ],
        name="pack",
        keep=False,
        place=False,
    )
    stack_far, matrix_far = swap(stack, 2), swap(matrix, 2)
    pieces = [
        stack, swap(stack, 1), stack_far, swap(stack_far, 1),
        matrix, swap(matrix, 1), matrix_far, swap(matrix_far, 1),
    ]
    stack_all, project_all, gains_all = call(
        assemble_kernel,
        [((STACK_ROWS, width), f32), ((width, C_IN), bf16), ((2, C_IN), f32)],
        [index, *pieces],
        name="assemble",
        keep=False,
    )
    expanded, sums_one, expand_all, kept, sent = call(
        first_kernel,
        [
            ((shards, rows, width), f32),
            ((16, width), f32),
            ((width, C_IN), bf16),
            ((shards, PACKED_ROWS // 2, C_IN), bf16),
            ((shards, PACKED_ROWS // 2, C_IN), bf16),
        ],
        [index, *pieces[4:], x],
        name="first",
        after=[gains_all],
    )
    (cot,) = call(
        cot_kernel,
        [((shards, rows, C_IN), bf16)],
        [index, kept, swap(sent, 1), swap(kept, 2), swap(sent, 3)],
        name="cot",
    )
    bias_row = jnp.pad(squeeze_bias, ((0, 0), (0, HIDDEN_ROWS - squeeze_bias.shape[1])))

    depth, sums, norm_one = call(
        functools.partial(expand_kernel, total_rows),
        [((shards, rows, width), f32), ((16, width), f32), ((32, width), f32)],
        [expanded, sums_one, swap(sums_one, 1), stack_all],
        [((KS * PRODUCTS, 8, width), f32)],
        name="expand",
    )
    projected, scaled, sums, gate, before, pooled, norm_two, active = call(
        functools.partial(squeeze_kernel, total_rows),
        [
            ((shards, rows, C_IN), f32),
            ((shards, rows, width), bf16),
            ((32, C_IN), f32),
            ((shards * 8, width), f32),
            ((shards * 8, HIDDEN_ROWS), f32),
            ((shards * 8, width), f32),
            ((32, width), f32),
            ((shards, rows, width), f32),
        ],
        [depth, sums, swap(sums, 1), stack_all, project_all, cot, bias_row],
        name="squeeze",
    )
    two, sums, lanes_grad, three_grad = call(
        functools.partial(gate_back_kernel, total_rows),
        [
            ((shards, rows, PAIR_LANES), f32),
            ((16, PAIR_LANES), f32),
            ((KEEP_ROWS, PAIR_LANES + 128), f32),
            ((2, C_IN), f32),
        ],
        [
            index, projected, cot, sums, swap(sums, 1), gains_all, depth, norm_two, stack_all,
            project_all, gate, before, pooled, scaled, active, x,
        ],
        [
            ((shards, rows, C_IN), bf16),
            ((shards, rows, width), f32),
            ((shards * 8, width), f32),
            ((shards * 8, PAIR_LANES), f32),
        ],
        name="gate_back",
    )
    lanes_other = swap(lanes_grad, 1)
    one, sums, two_grad = call(
        functools.partial(depth_back_kernel, total_rows),
        [
            ((shards, rows, PAIR_LANES), f32),
            ((48, PAIR_LANES), f32),
            ((2, PAIR_LANES), f32),
        ],
        [
            index, sums, swap(sums, 1), two, depth, expanded, stack_all, norm_one, norm_two,
        ],
        [
            ((KS * PRODUCTS, 8, PAIR_LANES), f32),
            ((KS * PRODUCTS, 8, PAIR_LANES), f32),
            ((24, PAIR_LANES), f32),
        ],
        name="depth_back",
    )
    sums_other = swap(sums, 1)
    late, one_grad = call(
        functools.partial(expand_back_kernel, total_rows),
        [((C_IN + LATE_ROWS, 512), f32), ((2, PAIR_LANES), f32)],
        [
            index, sums, sums_other, one, expanded, x, expand_all, stack_all, norm_one,
            lanes_other,
        ],
        [((shards, rows, PAIR_LANES), bf16)],
        name="expand_back",
    )
    late_pair = [late, swap(late, 1)]
    keep_pair = [lanes_grad, lanes_other, sums, sums_other]
    square, packed = call(
        settle_kernel,
        [((16, 128), f32), ((PACKED_ROWS + 16, C_IN), bf16)],
        [index, *late_pair, *keep_pair, three_grad, two_grad, one_grad],
        name="settle",
    )
    expand_own, project_own, lanes_own, bias_own, input_own, block_output, *scaled_params = call(
        own_kernel,
        [
            ((channels, C_IN), f32),
            ((channels, C_IN), f32),
            ((STACK_ROWS, channels), f32),
            ((1, HIDDEN_ROWS), f32),
            ((POSITIONS, segments, narrow), f32),
            ((POSITIONS, segments, narrow), bf16, False),
            *[(value.shape, f32) for value in params],
        ],
        [index, *late_pair, *keep_pair, two_grad, one_grad],
        name="own",
        plain=params,
    )
    updated = call(
        adam_kernel,
        [((POSITIONS, segments, narrow), f32)]
        + [(value.shape, f32) for value in params]
        + [((1, 1), f32)],
        [
            index, square, expand_own, project_own, lanes_own, bias_own, three_grad,
            input_own, swap(packed, 2), cot_rows, *scaled_params,
        ],
        name="adam",
        keep=False,
    )
    results = [block_output] + list(updated)
    for at in (0, 1):
        results[at] = jnp.transpose(results[at].reshape(HT, WD, segments, narrow), (3, 0, 1, 2))
    for at in (17, 18, 19, 23, 24, 25):
        results[at] = results[at][0]
    for at in (26, 27, 28):
        results[at] = results[at].T
    results[32] = results[32][0, 0]
    return tuple(results)


def solution(mesh):
    body = on_device_paired if paired_fits(mesh) else on_device
    return jax.shard_map(
        body,
        mesh=mesh,
        in_specs=(
            P(None, None, None, "dp"),
            P("chan", None, None, "dp"),
            P("chan", None),
            P("chan", None),
            P("chan", None),
            P(None, "chan"),
            P(None, "chan"),
            P(None, "chan"),
            P(None, "chan"),
            P(None, "chan"),
            P(None, "chan"),
            P(None, "chan"),
            P(None, "chan"),
            P(None, "chan"),
            P(None, "chan"),
            P(None, "chan"),
            P(None, "chan"),
            P(),
            P(),
            P(),
            P(None, "chan"),
            P(None, "chan"),
            P(None, "chan"),
            P("chan"),
            P("chan"),
            P("chan"),
            P(None, "chan"),
            P(None, "chan"),
            P(None, "chan"),
            P(None, "chan"),
            P(None, "chan"),
            P(None, "chan"),
        ),
        out_specs=(
            P("chan", None, None, "dp"),
            P("chan", None, None, "dp"),
            P("chan", None),
            P("chan", None),
            P("chan", None),
            P(None, "chan"),
            P(None, "chan"),
            P(None, "chan"),
            P(None, "chan"),
            P(None, "chan"),
            P(None, "chan"),
            P(None, "chan"),
            P(None, "chan"),
            P(None, "chan"),
            P(None, "chan"),
            P(None, "chan"),
            P(None, "chan"),
            P(),
            P(),
            P(),
            P(None, "chan"),
            P(None, "chan"),
            P(None, "chan"),
            P("chan"),
            P("chan"),
            P("chan"),
            P(None, "chan"),
            P(None, "chan"),
            P(None, "chan"),
            P(None, "chan"),
            P(None, "chan"),
            P(None, "chan"),
            P(),
        ),
        check_vma=False,
    )
```

```python
import functools
import math

import jax
import jax.numpy as jnp
from jax import lax
from jax.experimental import pallas as pl
from jax.experimental.pallas import tpu as pltpu
from jax.sharding import PartitionSpec as P

C_IN = 112
KS = 5
HT = 6
WD = 4
STEP = 10


norm_epsilon = 1e-05
beta_first = 0.9
beta_second = 0.999
adam_epsilon = 1e-08
decay_rate = 0.01
clip_limit = 1.0
step_rates = (0.3, 0.6, 0.6, 0.6, 0.12, 0.6, 0.6, 0.6, 0.12, 0.6)
decay_flags = (1.0, 0.0, 1.0, 0.0, 1.0, 0.0, 1.0, 0.0, 1.0, 0.0)
contract_rows = (((0,), (0,)), ((), ()))
contract_cols = (((1,), (1,)), ((), ()))
contract_plain = (((1,), (0,)), ((), ()))


def swish(values):
    return values * jax.nn.sigmoid(values)


def swish_slope(values):
    logistic = jax.nn.sigmoid(values)
    return logistic * (1.0 + values * (1.0 - logistic))


def highest(left, right, numbers):
    return lax.dot_general(
        left, right, numbers, precision=lax.Precision.HIGHEST, preferred_element_type=jnp.float32
    )


def depthwise(activity, kernel):
    half = KS // 2
    padded = jnp.pad(activity, ((0, 0), (half, half), (half, half), (0, 0)))
    result = jnp.zeros_like(activity)
    for row_shift in range(KS):
        for col_shift in range(KS):
            window = padded[:, row_shift : row_shift + HT, col_shift : col_shift + WD, :]
            result = result + kernel[row_shift * KS + col_shift][:, None, None, None] * window
    return result


def depthwise_back(grad_field, activity, kernel):
    half = KS // 2
    padded = jnp.pad(activity, ((0, 0), (half, half), (half, half), (0, 0)))
    grad_padded = jnp.pad(grad_field, ((0, 0), (half, half), (half, half), (0, 0)))
    activity_grad = jnp.zeros_like(activity)
    kernel_rows = []
    for row_shift in range(KS):
        for col_shift in range(KS):
            window = padded[:, row_shift : row_shift + HT, col_shift : col_shift + WD, :]
            kernel_rows.append(jnp.sum(grad_field * window, axis=(1, 2, 3)))
            back_window = grad_padded[
                :,
                2 * half - row_shift : 2 * half - row_shift + HT,
                2 * half - col_shift : 2 * half - col_shift + WD,
                :,
            ]
            activity_grad = (
                activity_grad
                + kernel[row_shift * KS + col_shift][:, None, None, None] * back_window
            )
    return (activity_grad, jnp.stack(kernel_rows))


def adam_step(weight, first_moment, second, gradient, step_rate, decay_flag):
    first_new = beta_first * first_moment + (1.0 - beta_first) * gradient
    second_new = beta_second * second + (1.0 - beta_second) * gradient * gradient
    first_hat = first_new / (1.0 - beta_first**STEP)
    second_hat = second_new / (1.0 - beta_second**STEP)
    weight_new = weight - step_rate * (
        first_hat / (jnp.sqrt(second_hat) + adam_epsilon) + decay_flag * decay_rate * weight
    )
    return (weight_new, first_new, second_new)


def on_device(
    block_input,
    cotangent,
    expand_weight,
    expand_weight_first,
    expand_weight_second,
    expand_gains,
    expand_gains_first,
    expand_gains_second,
    depth_weight,
    depth_weight_first,
    depth_weight_second,
    depth_gains,
    depth_gains_first,
    depth_gains_second,
    squeeze_weight,
    squeeze_weight_first,
    squeeze_weight_second,
    squeeze_bias,
    squeeze_bias_first,
    squeeze_bias_second,
    excite_weight,
    excite_weight_first,
    excite_weight_second,
    excite_bias,
    excite_bias_first,
    excite_bias_second,
    project_weight,
    project_weight_first,
    project_weight_second,
    project_gains,
    project_gains_first,
    project_gains_second,
):
    shards = lax.axis_size("chan")
    position = lax.axis_index("chan")
    segments = block_input.shape[3]
    batch_rows = HT * WD * segments * lax.axis_size("dp")
    narrow = cotangent.shape[0]
    local_channels = expand_weight.shape[0]
    flattened = block_input.reshape(C_IN, -1)
    expand_low = expand_weight.astype(jnp.bfloat16)
    expanded = jnp.dot(expand_low, flattened, preferred_element_type=jnp.float32)
    one_sums, one_squares = lax.psum(
        (jnp.sum(expanded, axis=1), jnp.sum(expanded * expanded, axis=1)), "dp"
    )
    one_average = one_sums / batch_rows
    one_spread = lax.rsqrt(one_squares / batch_rows - one_average * one_average + norm_epsilon)
    one_normal = (expanded - one_average[:, None]) * one_spread[:, None]
    one_before = one_normal * expand_gains[0][:, None] + expand_gains[1][:, None]
    active_one = swish(one_before).reshape(local_channels, HT, WD, segments)
    depth_out = depthwise(active_one, depth_weight).reshape(local_channels, -1)
    two_sums, two_squares = lax.psum(
        (jnp.sum(depth_out, axis=1), jnp.sum(depth_out * depth_out, axis=1)), "dp"
    )
    two_average = two_sums / batch_rows
    two_spread = lax.rsqrt(two_squares / batch_rows - two_average * two_average + norm_epsilon)
    two_normal = (depth_out - two_average[:, None]) * two_spread[:, None]
    two_before = two_normal * depth_gains[0][:, None] + depth_gains[1][:, None]
    active_two = swish(two_before).reshape(local_channels, HT, WD, segments)
    pooled = jnp.mean(active_two, axis=(1, 2))
    squeeze_part = highest(squeeze_weight, pooled, contract_plain)
    squeeze_pre = lax.psum(squeeze_part, "chan") + squeeze_bias[:, None]
    hidden = swish(squeeze_pre)
    gating = jax.nn.sigmoid(highest(excite_weight, hidden, contract_rows) + excite_bias[:, None])
    scaled = (
        (active_two * gating[:, None, None, :]).astype(jnp.bfloat16).reshape(local_channels, -1)
    )
    project_low = project_weight.astype(jnp.bfloat16)
    projected = lax.psum_scatter(
        jnp.dot(project_low, scaled, preferred_element_type=jnp.float32),
        "chan",
        scatter_dimension=0,
        tiled=True,
    )
    three_sums, three_squares = lax.psum(
        (jnp.sum(projected, axis=1), jnp.sum(projected * projected, axis=1)), "dp"
    )
    three_average = three_sums / batch_rows
    three_spread = lax.rsqrt(
        three_squares / batch_rows - three_average * three_average + norm_epsilon
    )
    three_normal = (projected - three_average[:, None]) * three_spread[:, None]
    three_after = three_normal * project_gains[0][:, None] + project_gains[1][:, None]
    own_input = lax.dynamic_slice_in_dim(flattened, position * narrow, narrow, 0).astype(
        jnp.float32
    )
    block_output = (own_input + three_after).astype(jnp.bfloat16).reshape(narrow, HT, WD, segments)
    upstream = cotangent.astype(jnp.float32).reshape(narrow, -1)
    three_beta, three_gamma = lax.psum(
        (jnp.sum(upstream, axis=1), jnp.sum(upstream * three_normal, axis=1)), "dp"
    )
    project_gains_grad = jnp.stack([three_gamma, three_beta])
    three_delta = (project_gains[0] * three_spread)[:, None] * (
        upstream
        - (three_beta / batch_rows)[:, None]
        - three_normal * (three_gamma / batch_rows)[:, None]
    )
    delta_whole = lax.all_gather(three_delta.astype(jnp.bfloat16), "chan", axis=0, tiled=True)
    scaled_grad = lax.dot_general(
        project_low, delta_whole, contract_rows, preferred_element_type=jnp.float32
    )
    project_weight_grad = lax.dot_general(
        delta_whole, scaled, contract_cols, preferred_element_type=jnp.float32
    )
    scaled_four = scaled_grad.reshape(local_channels, HT, WD, segments)
    gating_grad = jnp.sum(scaled_four * active_two, axis=(1, 2))
    excite_delta = gating_grad * gating * (1.0 - gating)
    excite_bias_grad = jnp.sum(excite_delta, axis=1)
    excite_weight_grad = highest(hidden, excite_delta, contract_cols)
    hidden_part = highest(excite_weight, excite_delta, contract_plain)
    hidden_grad = lax.psum(hidden_part, "chan")
    squeeze_delta = hidden_grad * swish_slope(squeeze_pre)
    squeeze_bias_grad = jnp.sum(squeeze_delta, axis=1)
    squeeze_weight_grad = highest(squeeze_delta, pooled, contract_cols)
    pooled_grad = highest(squeeze_weight, squeeze_delta, contract_rows)
    active_grad = scaled_four * gating[:, None, None, :] + pooled_grad[:, None, None, :] / (HT * WD)
    two_delta = active_grad.reshape(local_channels, -1) * swish_slope(two_before)
    two_gamma, two_beta = lax.psum(
        (jnp.sum(two_delta * two_normal, axis=1), jnp.sum(two_delta, axis=1)), "dp"
    )
    depth_gains_grad = jnp.stack([two_gamma, two_beta])
    depth_grad = (depth_gains[0] * two_spread)[:, None] * (
        two_delta
        - (two_beta / batch_rows)[:, None]
        - two_normal * (two_gamma / batch_rows)[:, None]
    )
    active_one_grad, depth_weight_grad = depthwise_back(
        depth_grad.reshape(local_channels, HT, WD, segments), active_one, depth_weight
    )
    one_delta = active_one_grad.reshape(local_channels, -1) * swish_slope(one_before)
    one_gamma, one_beta = lax.psum(
        (jnp.sum(one_delta * one_normal, axis=1), jnp.sum(one_delta, axis=1)), "dp"
    )
    expand_gains_grad = jnp.stack([one_gamma, one_beta])
    expand_delta = (
        (expand_gains[0] * one_spread)[:, None]
        * (
            one_delta
            - (one_beta / batch_rows)[:, None]
            - one_normal * (one_gamma / batch_rows)[:, None]
        )
    ).astype(jnp.bfloat16)
    expand_weight_grad = lax.dot_general(
        expand_delta, flattened, contract_cols, preferred_element_type=jnp.float32
    )
    input_part = lax.psum_scatter(
        lax.dot_general(
            expand_low, expand_delta, contract_rows, preferred_element_type=jnp.float32
        ).astype(jnp.bfloat16),
        "chan",
        scatter_dimension=0,
        tiled=True,
    ).astype(jnp.float32)
    input_grad = (input_part + upstream).reshape(narrow, HT, WD, segments)
    partials = (
        expand_weight_grad,
        depth_weight_grad,
        squeeze_weight_grad,
        excite_weight_grad,
        excite_bias_grad,
        project_weight_grad,
        squeeze_bias_grad,
    )
    gains_square = (
        jnp.sum(expand_gains_grad * expand_gains_grad)
        + jnp.sum(depth_gains_grad * depth_gains_grad)
        + jnp.sum(project_gains_grad * project_gains_grad)
    )
    summed = lax.psum(
        (partials[0], partials[1], partials[2], partials[3], partials[4], partials[5], partials[6]),
        "dp",
    )
    local_square = gains_square + jnp.sum(summed[6] * summed[6]) / shards
    for member in summed[:6]:
        local_square = local_square + jnp.sum(member * member)
    total_square = lax.psum(local_square, "chan")
    grad_norm = jnp.sqrt(total_square)
    factor = clip_limit / jnp.maximum(grad_norm, clip_limit)
    weights = (
        expand_weight,
        expand_gains,
        depth_weight,
        depth_gains,
        squeeze_weight,
        squeeze_bias,
        excite_weight,
        excite_bias,
        project_weight,
        project_gains,
    )
    firsts = (
        expand_weight_first,
        expand_gains_first,
        depth_weight_first,
        depth_gains_first,
        squeeze_weight_first,
        squeeze_bias_first,
        excite_weight_first,
        excite_bias_first,
        project_weight_first,
        project_gains_first,
    )
    seconds = (
        expand_weight_second,
        expand_gains_second,
        depth_weight_second,
        depth_gains_second,
        squeeze_weight_second,
        squeeze_bias_second,
        excite_weight_second,
        excite_bias_second,
        project_weight_second,
        project_gains_second,
    )
    gradients = (
        summed[0],
        expand_gains_grad,
        summed[1],
        depth_gains_grad,
        summed[2],
        summed[6],
        summed[3],
        summed[4],
        summed[5],
        project_gains_grad,
    )
    updated = [
        adam_step(
            weights[entry],
            firsts[entry],
            seconds[entry],
            gradients[entry] * factor,
            step_rates[entry],
            decay_flags[entry],
        )
        for entry in range(10)
    ]
    return (
        block_output,
        input_grad,
        updated[0][0],
        updated[0][1],
        updated[0][2],
        updated[1][0],
        updated[1][1],
        updated[1][2],
        updated[2][0],
        updated[2][1],
        updated[2][2],
        updated[3][0],
        updated[3][1],
        updated[3][2],
        updated[4][0],
        updated[4][1],
        updated[4][2],
        updated[5][0],
        updated[5][1],
        updated[5][2],
        updated[6][0],
        updated[6][1],
        updated[6][2],
        updated[7][0],
        updated[7][1],
        updated[7][2],
        updated[8][0],
        updated[8][1],
        updated[8][2],
        updated[9][0],
        updated[9][1],
        updated[9][2],
        grad_norm,
    )


POSITIONS = HT * WD
HALF_KS = KS // 2
PAIR_LANES = 384
HIDDEN_ROWS = 32
TAPS = KS * KS
ROW_SQUEEZE = 32
ROW_EXCITE = 64
ROW_EXCITE_BIAS = 96
ROW_EXPAND_GAINS = 97
ROW_DEPTH_GAINS = 99
ROW_PROJECT_GAINS = 101
STACK_ROWS = 104
KEEP_BIASES = 64
KEEP_PROJECT = 80
KEEP_ROWS = 192
LATE_ROWS = 48
PACKED_ROWS = 96
BLOCK_ROWS = POSITIONS * 8
SENT_ROWS = 256
TAIL_ROWS = BLOCK_ROWS + PACKED_ROWS - SENT_ROWS
TAIL_LANES = 128 - C_IN
PAIRED_ROWS_LIMIT = 3072
contract_lanes = (((1,), (1,)), ((), ()))
f32 = jnp.float32
bf16 = jnp.bfloat16


def paired_fits(mesh):
    return mesh.shape["chan"] == 4 and mesh.shape["dp"] * POSITIONS * 8 <= PAIRED_ROWS_LIMIT


def dot(left, right, numbers):
    return lax.dot_general(left, right, numbers, preferred_element_type=f32)


def split_dot(left, right, numbers):
    left_high, right_high = left.astype(bf16), right.astype(bf16)
    left_low = (left - left_high.astype(f32)).astype(bf16)
    right_low = (right - right_high.astype(f32)).astype(bf16)
    mixed = dot(left_high, right_low, numbers) + dot(left_low, right_high, numbers)
    return dot(left_high, right_high, numbers) + mixed


def rows_sum(values):
    return jnp.broadcast_to(jnp.sum(values, axis=0, keepdims=True), (8, values.shape[1]))


def lane_tile(index, start=0):
    if isinstance(start, int):
        return slice(start + index * 128, start + index * 128 + 128)
    return pl.ds(pl.multiple_of(start + index * 128, 128), 128)


def swish_of_half(half):
    return half * jnp.tanh(half) + half


def slope_of_half(half):
    bent = jnp.tanh(half)
    up = 1.0 + bent
    return 0.5 * up * (1.0 + half * (1.0 - bent))


PRODUCTS = 9
FILTER_SIGNS = (
    ((2, 1),),
    ((3, 1), (2, -1)),
    ((1, 1), (2, -1)),
    ((4, 1), (2, -1)),
    ((2, 1), (3, -1), (4, -1)),
    ((2, 1), (3, 1), (1, -1), (4, -1)),
    ((0, 1), (2, -1)),
    ((2, 1), (1, 1), (3, -1), (0, -1)),
    ((2, 1), (1, -1), (0, -1)),
)


def signed(terms):
    total = None
    for value, sign in terms:
        if total is None:
            total = value if sign > 0 else -value
        else:
            total = total + value if sign > 0 else total - value
    return total


def product_filters(taps, out_ref):
    for i in range(KS):
        for at, signs in enumerate(FILTER_SIGNS):
            value = signed([(taps(i, column), sign) for column, sign in signs])
            out_ref[i * PRODUCTS + at] = jnp.broadcast_to(value, out_ref.shape[1:])


def product_inputs(field):
    rows = []
    for row in range(HT):
        x0, x1, x2, x3 = field[row * WD : row * WD + WD]
        even, odd = x0 + x2, x1 + x3
        rows.append((even + odd, odd, even, x2 + x3, x3, x2, x0 + x1, x1, x0))
    return list(zip(*rows))


def product_targets(inputs):
    both, odd, even, right, x3, x2, left, x1, x0 = inputs
    return (both, even, odd, left, x0, x1, right, x2, x3)


def rows_of(row):
    return [(i, row + i - HALF_KS) for i in range(KS) if 0 <= row + i - HALF_KS < HT]


def product_sum(filters, inputs):
    sums = []
    for at in range(PRODUCTS):
        weights = [filters(i * PRODUCTS + at) for i in range(KS)]
        found = []
        for row in range(HT):
            value = None
            for i, source in rows_of(row):
                term = weights[i] * inputs[at][source]
                value = term if value is None else value + term
            found.append(value)
        sums.append(found)
    return sums


def product_outputs(sums, row):
    q = [found[row] for found in sums]
    near_0, near_1 = q[0] + q[1], q[0] + q[2]
    return (
        near_0 + (q[3] + q[4]), near_1 + (q[3] + q[5]), near_0 + (q[6] + q[7]), near_1 + (q[6] + q[8])
    )


def in_order(position, own, near, far, cross):
    first = position % 2 == 0
    front = position // 2 == 0
    low, high = jnp.where(first, own, near), jnp.where(first, near, own)
    far_low, far_high = jnp.where(first, far, cross), jnp.where(first, cross, far)
    return (
        jnp.where(front, low, far_low), jnp.where(front, high, far_high),
        jnp.where(front, far_low, low), jnp.where(front, far_high, high),
    )


def matrix_in_order(position, refs, start, channels):
    parts = in_order(position, *[ref[start : start + channels, :].astype(f32) for ref in refs])
    gap = jnp.zeros((PAIR_LANES - 2 * channels, C_IN), f32)
    return jnp.concatenate([*parts[0:2], gap, *parts[2:4], gap], axis=0).astype(bf16)


def first_kernel(
    index_ref, matrix_0, matrix_1, matrix_2, matrix_3, x_ref, _after_ref,
    expanded_ref, sums_ref, we_ref, keep_ref, send_ref,
):
    blocks = x_ref.shape[0]
    width = we_ref.shape[0]
    refs = (matrix_0, matrix_1, matrix_2, matrix_3)
    we_ref[...] = matrix_in_order(index_ref[1], refs, 0, matrix_0.shape[0] // 2)
    tail = None
    for piece in range(C_IN // TAIL_LANES):
        rows = x_ref[:, piece * TAIL_ROWS : (piece + 1) * TAIL_ROWS, :].reshape(-1, 128)
        move = one_hot(
            128, C_IN, lambda r, c: (r - C_IN == c - piece * TAIL_LANES) & (r >= C_IN)
        ).astype(bf16)
        part = dot(rows, move, contract_plain)
        tail = part if tail is None else tail + part
    packed = jnp.concatenate(
        [
            x_ref[:, BLOCK_ROWS:SENT_ROWS, 0:C_IN].astype(f32),
            tail.reshape(blocks, TAIL_ROWS, C_IN),
        ],
        axis=1,
    )
    packed = packed.reshape(blocks * PACKED_ROWS // 16, 2, 8, C_IN)
    first = index_ref[1] % 2 == 0
    for ref, at in ((keep_ref, 0), (send_ref, 1)):
        half = jnp.where(first, packed[:, at], packed[:, 1 - at])
        ref[...] = half.reshape(blocks, PACKED_ROWS // 2, C_IN).astype(bf16)
    for lanes in (slice(at, at + 256) for at in range(0, width, 256)):
        total = jnp.zeros((8, 256), f32)
        square = jnp.zeros((8, 256), f32)
        for block in range(blocks):
            value = dot(x_ref[block, 0:BLOCK_ROWS, 0:C_IN], we_ref[lanes, :], contract_lanes)
            expanded_ref[block, :, lanes] = value
            shaped = value.reshape(POSITIONS, 8, 256)
            total = total + jnp.sum(shaped, axis=0)
            square = square + jnp.sum(shaped * shaped, axis=0)
        sums_ref[0:8, lanes] = total
        sums_ref[8:16, lanes] = square


def norm_factors(total_rows, sums_own, sums_other, gain, shift, norm_ref):
    average = rows_sum(sums_own[0:8] + sums_other[0:8]) / total_rows
    squares = rows_sum(sums_own[8:16] + sums_other[8:16]) / total_rows
    spread = lax.rsqrt(squares - average * average + norm_epsilon)
    gain = gain * spread
    norm_ref[0:8, :] = 0.5 * gain
    norm_ref[8:16, :] = 0.5 * (shift - average * gain)
    norm_ref[16:24, :] = average
    norm_ref[24:32, :] = spread


def expand_kernel(
    total_rows, expanded_ref, sums_own, sums_other, stack_ref, depth_ref, sums_ref, norm_ref, taps_scr
):
    blocks, _, width = expanded_ref.shape
    norm_factors(
        total_rows, sums_own, sums_other, stack_ref[ROW_EXPAND_GAINS : ROW_EXPAND_GAINS + 1, :],
        stack_ref[ROW_EXPAND_GAINS + 1 : ROW_EXPAND_GAINS + 2, :], norm_ref,
    )
    product_filters(lambda i, j: stack_ref[i * KS + j : i * KS + j + 1, :], taps_scr)
    sums_ref[...] = jnp.zeros_like(sums_ref)

    def one_block(block, carry):
        for tile in range(width // 128):
            lanes = lane_tile(tile)
            gain_half = norm_ref[0:8, lanes]
            shift_half = norm_ref[8:16, lanes]
            active = [
                swish_of_half(expanded_ref[block, 8 * at : 8 * at + 8, lanes] * gain_half + shift_half)
                for at in range(POSITIONS)
            ]
            total = jnp.zeros((8, 128), f32)
            square = jnp.zeros((8, 128), f32)
            sums = product_sum(lambda at: taps_scr[at, :, lanes], product_inputs(active))
            for row in range(HT):
                for col, value in enumerate(product_outputs(sums, row)):
                    at = row * WD + col
                    depth_ref[block, 8 * at : 8 * at + 8, lanes] = value
                    total = total + value
                    square = square + value * value
            sums_ref[0:8, lanes] += total
            sums_ref[8:16, lanes] += square
        return carry

    lax.fori_loop(0, blocks, one_block, 0)


def squeeze_kernel(
    total_rows, depth_ref, sums_own, sums_other, stack_ref, wp_ref, cot_ref, bias_ref,
    projected_ref, scaled_ref, sums_ref, gate_ref, before_ref, pooled_ref, norm_ref, active_ref,
):
    blocks, _, width = depth_ref.shape
    norm_factors(
        total_rows, sums_own, sums_other, stack_ref[ROW_DEPTH_GAINS : ROW_DEPTH_GAINS + 1, :],
        stack_ref[ROW_DEPTH_GAINS + 1 : ROW_DEPTH_GAINS + 2, :], norm_ref,
    )

    def pool_block(block):
        for tile in range(width // 128):
            lanes = lane_tile(tile)
            gain_half = norm_ref[0:8, lanes]
            shift_half = norm_ref[8:16, lanes]
            total = jnp.zeros((8, 128), f32)
            for at in range(POSITIONS):
                value = swish_of_half(
                    depth_ref[block, 8 * at : 8 * at + 8, lanes] * gain_half + shift_half
                )
                active_ref[block, 8 * at : 8 * at + 8, lanes] = value
                total = total + value
            pooled_ref[slice(8 * block, 8 * block + 8), lanes] = total / POSITIONS

    for block in range(blocks):
        pool_block(block)
    squeeze = stack_ref[ROW_SQUEEZE : ROW_SQUEEZE + HIDDEN_ROWS, :]
    excite = stack_ref[ROW_EXCITE : ROW_EXCITE + HIDDEN_ROWS, :]
    before = split_dot(pooled_ref[...], squeeze, contract_lanes) + bias_ref[...]
    before_ref[...] = before
    hidden = swish_of_half(0.5 * before)
    raised = split_dot(hidden, excite, contract_plain)
    raised = raised + stack_ref[ROW_EXCITE_BIAS : ROW_EXCITE_BIAS + 1, :]
    gate_ref[...] = 0.5 + 0.5 * jnp.tanh(0.5 * raised)
    totals = [jnp.zeros((8, C_IN), f32)] * 4
    for block in range(blocks):
        for tile in range(width // 128):
            lanes = lane_tile(tile)
            gate = gate_ref[8 * block : 8 * block + 8, lanes]
            value = active_ref[block, :, lanes].reshape(POSITIONS, 8, 128) * gate[None]
            scaled_ref[block, :, lanes] = value.reshape(BLOCK_ROWS, 128).astype(bf16)
        projected = dot(scaled_ref[block], wp_ref[...], contract_plain)
        projected_ref[block] = projected
        shaped = projected.reshape(POSITIONS, 8, C_IN)
        upstream = cot_ref[block].astype(f32).reshape(POSITIONS, 8, C_IN)
        terms = (shaped, shaped * shaped, shaped * upstream, upstream)
        totals = [total + jnp.sum(term, axis=0) for total, term in zip(totals, terms)]
    for at in range(4):
        sums_ref[8 * at : 8 * at + 8, :] = totals[at]


def gate_back_kernel(
    total_rows, index_ref, projected_ref, cot_ref, sums_own, sums_other, gains_ref, depth_ref,
    norm_ref, stack_ref, wp_ref, gate_ref, before_ref, pooled_ref, scaled_ref, active_ref, x_ref,
    two_ref, sums_ref, lanes_ref, gains_grad_ref,
    delta_scr, grad_scr, gate_grad_scr, pooled_scr,
):
    blocks = depth_ref.shape[0]
    width = depth_ref.shape[2]
    own = pl.multiple_of(index_ref[1] // 2 * PAIR_LANES, 128)
    own_lanes = pl.ds(own, PAIR_LANES)
    sums = [rows_sum(sums_own[8 * k : 8 * k + 8] + sums_other[8 * k : 8 * k + 8])[0:1] for k in range(4)]
    average = sums[0] / total_rows
    spread = lax.rsqrt(sums[1] / total_rows - average * average + norm_epsilon)
    beta = sums[3]
    gamma = spread * (sums[2] - average * beta)
    gains_grad_ref[0:1, :] = gamma
    gains_grad_ref[1:2, :] = beta
    gain = gains_ref[0:1, :]
    shift = gains_ref[1:2, :]
    mine = index_ref[0]
    output = x_ref[mine, 0:BLOCK_ROWS, 0:C_IN].astype(f32)
    output = output + ((projected_ref[mine] - average) * spread * gain + shift)
    lanes_ref[:, PAIR_LANES : PAIR_LANES + C_IN] = output
    outer = gain * spread

    for block in range(blocks):
        normal = (projected_ref[block] - average) * spread
        delta = outer * (
            cot_ref[block].astype(f32) - beta / total_rows - normal * (gamma / total_rows)
        )
        delta_scr[block] = delta.astype(bf16)
    for block in range(blocks):
        for lanes in (slice(at, at + 256) for at in range(0, width, 256)):
            value = dot(delta_scr[block], wp_ref[lanes, :], contract_lanes)
            grad_scr[block, :, lanes] = value
            value = (value * active_ref[block, :, lanes]).reshape(POSITIONS, 8, 256)
            gate_grad_scr[8 * block : 8 * block + 8, lanes] = jnp.sum(value, axis=0)
    excite = stack_ref[ROW_EXCITE : ROW_EXCITE + HIDDEN_ROWS, :]
    gate = gate_ref[...]
    gate_grad_scr[...] = gate_grad_scr[...] * gate * (1.0 - gate)
    half = 0.5 * before_ref[...]
    hidden = swish_of_half(half)
    squeeze_delta = split_dot(gate_grad_scr[...], excite, contract_lanes) * slope_of_half(half)
    own_delta = gate_grad_scr[:, own_lanes]
    lanes_ref[0:HIDDEN_ROWS, 0:PAIR_LANES] = split_dot(squeeze_delta, pooled_ref[:, own_lanes], contract_rows)
    lanes_ref[HIDDEN_ROWS : 2 * HIDDEN_ROWS, 0:PAIR_LANES] = split_dot(hidden, own_delta, contract_rows)
    lanes_ref[KEEP_BIASES : KEEP_BIASES + 8, 0:PAIR_LANES] = rows_sum(own_delta)
    lanes_ref[KEEP_BIASES + 8 : KEEP_BIASES + 16, 0:PAIR_LANES] = jnp.zeros((8, PAIR_LANES), f32)
    lanes_ref[KEEP_BIASES + 8 : KEEP_BIASES + 16, 0:HIDDEN_ROWS] = rows_sum(squeeze_delta)
    squeeze = stack_ref[ROW_SQUEEZE : ROW_SQUEEZE + HIDDEN_ROWS, own_lanes]
    pooled_scr[...] = split_dot(squeeze_delta, squeeze, contract_plain) / POSITIONS
    sums_ref[...] = jnp.zeros_like(sums_ref)

    def two_block(block):
        rows = slice(8 * block, 8 * block + 8)
        for tile in range(PAIR_LANES // 128):
            lanes = lane_tile(tile)
            whole = lane_tile(tile, own)
            gain_half = norm_ref[0:8, whole]
            shift_half = norm_ref[8:16, whole]
            average = norm_ref[16:24, whole]
            gate = 0.5 * gate_ref[rows, whole]
            pooled_grad = 0.5 * pooled_scr[rows, lanes]
            total = jnp.zeros((8, 128), f32)
            product = jnp.zeros((8, 128), f32)
            for at in range(POSITIONS):
                spot = slice(8 * at, 8 * at + 8)
                depth = depth_ref[block, spot, whole]
                bent = jnp.tanh(depth * gain_half + shift_half)
                slope = (1.0 + bent) + active_ref[block, spot, whole] * (1.0 - bent)
                value = (grad_scr[block, spot, whole] * gate + pooled_grad) * slope
                two_ref[block, spot, lanes] = value
                total = total + value
                product = product + value * (depth - average)
            sums_ref[0:8, lanes] += total
            sums_ref[8:16, lanes] += product

    for block in range(blocks):
        two_block(block)
    rows = blocks * POSITIONS * 8
    lanes_ref[KEEP_PROJECT : KEEP_PROJECT + C_IN, 0:PAIR_LANES] = dot(
        delta_scr[...].reshape(rows, C_IN), scaled_ref[:, :, own_lanes].reshape(rows, PAIR_LANES), contract_rows
    )


def depth_back_kernel(
    total_rows, index_ref, sums_own, sums_other, two_ref, depth_ref, expanded_ref, stack_ref,
    norm_one_ref, norm_two_ref,
    one_ref, sums_ref, gains_grad_ref, taps_scr, kernel_scr, factors_scr,
):
    blocks = depth_ref.shape[0]
    own = pl.multiple_of(index_ref[1] // 2 * PAIR_LANES, 128)
    own_lanes = pl.ds(own, PAIR_LANES)
    spread = norm_two_ref[24:32, own_lanes]
    average = norm_two_ref[16:24, own_lanes]
    beta = rows_sum(sums_own[0:8] + sums_other[0:8])
    gamma = rows_sum(sums_own[8:16] + sums_other[8:16]) * spread
    gains_grad_ref[0:1, :] = gamma[0:1]
    gains_grad_ref[1:2, :] = beta[0:1]
    outer = stack_ref[ROW_DEPTH_GAINS : ROW_DEPTH_GAINS + 1, own_lanes] * spread
    slope = outer * spread * gamma / total_rows
    factors_scr[0:8, :] = outer
    factors_scr[8:16, :] = slope
    factors_scr[16:24, :] = outer * (beta / total_rows) - slope * average
    product_filters(
        lambda i, j: 0.5 * stack_ref[TAPS - 1 - i * KS - j : TAPS - i * KS - j, own_lanes], taps_scr
    )
    sums_ref[...] = jnp.zeros_like(sums_ref)
    kernel_scr[...] = jnp.zeros_like(kernel_scr)

    def one_block(block, carry):
        for tile in range(PAIR_LANES // 128):
            lanes = lane_tile(tile)
            whole = lane_tile(tile, own)
            gain_half = norm_one_ref[0:8, whole]
            shift_half = norm_one_ref[8:16, whole]
            average_one = norm_one_ref[16:24, whole]
            outer = factors_scr[0:8, lanes]
            slope = factors_scr[8:16, lanes]
            level = factors_scr[16:24, lanes]
            grads = []
            active = []
            bents = []
            for at in range(POSITIONS):
                spot = slice(8 * at, 8 * at + 8)
                grads.append(
                    outer * two_ref[block, spot, lanes]
                    - level
                    - slope * depth_ref[block, spot, whole]
                )
                half = expanded_ref[block, spot, whole] * gain_half + shift_half
                bents.append(jnp.tanh(half))
                active.append(half * bents[at] + half)
            sources = product_inputs(active)
            inputs = product_inputs(grads)
            targets = product_targets(inputs)
            for at in range(PRODUCTS):
                for i in range(KS):
                    value = None
                    for row in range(HT):
                        if 0 <= row + i - HALF_KS < HT:
                            term = targets[at][row] * sources[at][row + i - HALF_KS]
                            value = term if value is None else value + term
                    kernel_scr[i * PRODUCTS + at, :, lanes] += value
            sums = product_sum(lambda at: taps_scr[at, :, lanes], inputs)
            total = jnp.zeros((8, 128), f32)
            product = jnp.zeros((8, 128), f32)
            for row in range(HT):
                for col, value in enumerate(product_outputs(sums, row)):
                    at = row * WD + col
                    spot = slice(8 * at, 8 * at + 8)
                    expanded = expanded_ref[block, spot, whole]
                    value = value * ((1.0 + bents[at]) + active[at] * (1.0 - bents[at]))
                    one_ref[block, spot, lanes] = value
                    total = total + value
                    product = product + value * (expanded - average_one)
            sums_ref[0:8, lanes] += total
            sums_ref[8:16, lanes] += product
        return carry

    lax.fori_loop(0, blocks, one_block, 0)
    for i in range(KS):
        for j in range(KS):
            terms = [
                (jnp.sum(kernel_scr[i * PRODUCTS + at], axis=0, keepdims=True), sign)
                for at, signs in enumerate(FILTER_SIGNS)
                for column, sign in signs
                if column == j
            ]
            row = 16 + i * KS + j
            sums_ref[row : row + 1, :] = signed(terms)


def expand_back_kernel(
    total_rows, index_ref, sums_own, sums_other, one_ref, expanded_ref, x_ref, we_ref, stack_ref, norm_ref,
    _lanes_ref,
    late_ref, gains_grad_ref, delta_scr,
):
    blocks = x_ref.shape[0]
    own = pl.multiple_of(index_ref[1] // 2 * PAIR_LANES, 128)
    own_lanes = pl.ds(own, PAIR_LANES)
    spread = norm_ref[24:32, own_lanes]
    average = norm_ref[16:17, own_lanes]
    beta = rows_sum(sums_own[0:8] + sums_other[0:8])
    gamma = rows_sum(sums_own[8:16] + sums_other[8:16]) * spread
    gains_grad_ref[0:1, :] = gamma[0:1]
    gains_grad_ref[1:2, :] = beta[0:1]
    outer = stack_ref[ROW_EXPAND_GAINS : ROW_EXPAND_GAINS + 1, own_lanes] * spread[0:1]
    slope = outer * spread[0:1] * gamma[0:1] / total_rows
    level = outer * (beta[0:1] / total_rows)
    own_weights = we_ref[own_lanes, :]

    for block in range(blocks):
        centred = expanded_ref[block, :, own_lanes] - average
        delta = outer * one_ref[block] - level - slope * centred
        delta_scr[block] = delta.astype(bf16)
    rows = blocks * POSITIONS * 8
    late_ref[0:C_IN, 0:PAIR_LANES] = dot(
        x_ref[:, 0:BLOCK_ROWS, 0:C_IN].reshape(rows, C_IN), delta_scr[...].reshape(rows, PAIR_LANES), contract_rows
    )
    part = dot(delta_scr[index_ref[0]], own_weights, contract_plain)
    for group in range(4):
        late_ref[C_IN : C_IN + LATE_ROWS, group * 128 : group * 128 + C_IN] = part[
            group * LATE_ROWS : (group + 1) * LATE_ROWS
        ]


def one_hot(rows, columns, matches):
    return matches(
        lax.broadcasted_iota(jnp.int32, (rows, columns), 0),
        lax.broadcasted_iota(jnp.int32, (rows, columns), 1),
    )


def copies_kernel(index_ref, rows_ref, cot_ref, copies_ref):
    whole = rows_ref[...].astype(f32)
    half = jnp.where(index_ref[1] % 2 == 0, whole[:, 0:8, :], whole[:, 8:16, :])
    half = half.reshape(BLOCK_ROWS, C_IN)
    narrow = cot_ref.shape[2]
    rows = cot_ref[...].reshape(4 * PACKED_ROWS, narrow)
    packed = None
    for group in range(4):
        place = one_hot(narrow, C_IN, lambda r, c: c == r + group * narrow).astype(bf16)
        part = dot(rows[group * PACKED_ROWS : (group + 1) * PACKED_ROWS], place, contract_plain)
        packed = part if packed is None else packed + part
    value = jnp.concatenate([half, packed], axis=0).astype(bf16)
    widen = one_hot(C_IN, 128, lambda r, c: r == c).astype(bf16)
    dense = dot(value[0:SENT_ROWS], widen, contract_plain)
    parts = []
    for piece in range(SENT_ROWS // TAIL_ROWS):
        move = one_hot(
            C_IN, 128, lambda r, c: (c - C_IN == r - piece * TAIL_LANES) & (c >= C_IN)
        ).astype(bf16)
        parts.append(dot(value[SENT_ROWS:], move, contract_plain))
    dense = (dense + jnp.concatenate(parts, axis=0)).astype(bf16)
    for at in range(copies_ref.shape[0]):
        copies_ref[at] = dense


def cot_kernel(index_ref, own_ref, near_ref, far_ref, cross_ref, cot_ref):
    position = index_ref[1]
    near = position + 1 - position % 2 * 2
    blocks = cot_ref.shape[0]
    narrow = C_IN // 4
    rows = blocks * PACKED_ROWS // 2
    pieces = (
        (own_ref, position), (near_ref, near), (far_ref, (position + 2) % 4),
        (cross_ref, (near + 2) % 4),
    )
    for group in range(4):
        total = None
        for ref, place in pieces:
            move = one_hot(
                C_IN,
                C_IN,
                lambda r, c: (c - place * narrow == r - group * narrow)
                & (r >= group * narrow) & (r < (group + 1) * narrow),
            ).astype(bf16)
            part = dot(ref[...].reshape(rows, C_IN), move, contract_plain)
            total = part if total is None else total + part
        half = total.reshape(blocks, PACKED_ROWS // 2, C_IN).astype(bf16)
        start = group * (PACKED_ROWS // 2)
        cot_ref[:, start : start + PACKED_ROWS // 2, :] = half


def pack_kernel(
    expand_ref, project_ref, depth_ref, squeeze_ref, excite_ref, excite_bias_ref, expand_gains_ref,
    depth_gains_ref, project_gains_ref, stack_ref, matrix_ref,
):
    channels = expand_ref.shape[0]
    narrow = project_gains_ref.shape[1]
    stack_ref[...] = jnp.zeros_like(stack_ref)
    for start, ref in (
        (0, depth_ref), (ROW_SQUEEZE, squeeze_ref), (ROW_EXCITE, excite_ref),
        (ROW_EXCITE_BIAS, excite_bias_ref), (ROW_EXPAND_GAINS, expand_gains_ref),
        (ROW_DEPTH_GAINS, depth_gains_ref),
    ):
        stack_ref[start : start + ref.shape[0], :] = ref[...]
    stack_ref[ROW_PROJECT_GAINS : ROW_PROJECT_GAINS + 2, 0:narrow] = project_gains_ref[...]
    matrix_ref[...] = jnp.concatenate(
        [expand_ref[...], project_ref[...]], axis=0
    ).astype(bf16)


def assemble_kernel(
    index_ref, stack_0, stack_1, stack_2, stack_3, matrix_0, matrix_1, matrix_2, matrix_3,
    stack_ref, project_ref, gains_ref,
):
    channels = stack_0.shape[1]
    narrow = C_IN // 4
    stacks = in_order(index_ref[1], stack_0[...], stack_1[...], stack_2[...], stack_3[...])
    stack_ref[...] = jnp.zeros_like(stack_ref)
    for place in range(4):
        start = place // 2 * PAIR_LANES + place % 2 * channels
        stack_ref[:, start : start + channels] = stacks[place]
        gains_ref[:, place * narrow : (place + 1) * narrow] = stacks[place][
            ROW_PROJECT_GAINS : ROW_PROJECT_GAINS + 2, 0:narrow
        ]
    refs = (matrix_0, matrix_1, matrix_2, matrix_3)
    project_ref[...] = matrix_in_order(index_ref[1], refs, channels, channels)


def squared(values):
    return jnp.sum(jnp.sum(values * values, axis=0, keepdims=True), axis=1, keepdims=True)


def own_block(position, values, channels):
    return jnp.where(
        position % 2 == 0, values[:, 0:channels], values[:, channels : 2 * channels]
    )


def early_kernel(
    index_ref, keep_own, keep_other, project_ref, lanes_ref, bias_ref, output_ref, square_ref
):
    position = index_ref[1]
    channels = project_ref.shape[0]
    narrow = output_ref.shape[2]

    def both(start, stop):
        return keep_own[start:stop, 0:PAIR_LANES] + keep_other[start:stop, 0:PAIR_LANES]

    project = both(KEEP_PROJECT, KEEP_PROJECT + C_IN)
    hidden = both(0, 2 * HIDDEN_ROWS)
    excite_bias = both(KEEP_BIASES, KEEP_BIASES + 1)
    bias = both(KEEP_BIASES + 8, KEEP_BIASES + 9)[:, 0:HIDDEN_ROWS]
    total = squared(project) + squared(hidden) + squared(excite_bias)
    square_ref[0:8, :] = jnp.broadcast_to(total, (8, 128))
    square_ref[8:16, :] = jnp.broadcast_to(squared(bias), (8, 128))
    bias_ref[...] = bias
    project_ref[...] = jnp.transpose(own_block(position, project, channels))
    lanes_ref[0 : 2 * HIDDEN_ROWS, :] = own_block(position, hidden, channels)
    lanes_ref[2 * HIDDEN_ROWS : 2 * HIDDEN_ROWS + 1, :] = own_block(position, excite_bias, channels)
    pick = one_hot(C_IN, narrow, lambda r, c: r == c + position * narrow).astype(bf16)
    halves = [
        dot(ref[:, PAIR_LANES : PAIR_LANES + C_IN].astype(bf16), pick, contract_plain)
        for ref in (keep_own, keep_other)
    ]
    output_ref[...] = both_halves(position % 2 == 0, *halves).astype(bf16)


def input_rows(late_ref):
    return jnp.concatenate(
        [
            late_ref[C_IN : C_IN + LATE_ROWS, group * 128 : group * 128 + C_IN]
            for group in range(4)
        ],
        axis=0,
    )


def expand_sum(late_own, late_other):
    return late_own[0:C_IN, 0:PAIR_LANES] + late_other[0:C_IN, 0:PAIR_LANES]


def both_halves(first, own, other):
    own = own.reshape(POSITIONS, 8, own.shape[-1])
    other = other.reshape(POSITIONS, 8, other.shape[-1])
    return jnp.concatenate(
        [jnp.where(first, own, other), jnp.where(first, other, own)], axis=1
    )


def settle_kernel(
    index_ref, late_own, late_other, early_ref, sums_own, sums_other, three_ref, two_ref, one_ref,
    square_ref, packed_ref,
):
    position = index_ref[1]
    narrow = C_IN // 4

    kernel = sums_own[16 : 16 + TAPS, :] + sums_other[16 : 16 + TAPS, :]
    total = early_ref[0:1, 0:1] + squared(expand_sum(late_own, late_other)) + squared(kernel)
    total = total + squared(one_ref[...]) + squared(two_ref[...])
    square_ref[0:8, :] = jnp.broadcast_to(total, (8, 128))
    square_ref[8:16, :] = jnp.broadcast_to(early_ref[8:9, 0:1] + squared(three_ref[...]), (8, 128))
    whole = both_halves(position % 2 == 0, input_rows(late_own), input_rows(late_other))
    whole = whole.reshape(4 * PACKED_ROWS, C_IN).astype(bf16)
    across = position + 2 - position // 2 * 4
    packed = None
    for group in range(4):
        move = one_hot(
            C_IN,
            C_IN,
            lambda r, c: (r - across * narrow == c - group * narrow)
            & (c >= group * narrow) & (c < (group + 1) * narrow),
        ).astype(bf16)
        part = dot(whole[group * PACKED_ROWS : (group + 1) * PACKED_ROWS], move, contract_plain)
        packed = part if packed is None else packed + part
    packed_ref[0:PACKED_ROWS, :] = packed.astype(bf16)
    rest = jnp.broadcast_to(total, (16, C_IN))
    parts = jnp.zeros((16, C_IN), f32)
    row = lax.broadcasted_iota(jnp.int32, (16, C_IN), 0)
    for at in range(3):
        part = rest.astype(bf16).astype(f32)
        rest = rest - part
        parts = jnp.where(row == at, part, parts)
    packed_ref[PACKED_ROWS : PACKED_ROWS + 16, :] = parts.astype(bf16)


def own_kernel(
    index_ref, late_own, late_other, sums_own, sums_other, two_ref, one_ref, *refs
):
    params, outs = refs[:30], refs[33:]
    expand_ref, lanes_ref, input_ref = refs[30:33]
    for entry in range(10):
        shrink = 1.0 - step_rates[entry] * decay_flags[entry] * decay_rate
        for part, scale in enumerate((shrink, beta_first, beta_second)):
            outs[3 * entry + part][...] = scale * params[3 * entry + part][...]
    position = index_ref[1]
    first = position % 2 == 0
    channels = expand_ref.shape[0]
    narrow = C_IN // 4

    def mine(values):
        return own_block(position, values, channels)

    expand_ref[...] = jnp.transpose(mine(expand_sum(late_own, late_other)))
    lanes_ref[0:TAPS, :] = mine(sums_own[16 : 16 + TAPS, :] + sums_other[16 : 16 + TAPS, :])
    lanes_ref[32:34, :] = mine(one_ref[...])
    lanes_ref[34:36, :] = mine(two_ref[...])
    pick = one_hot(C_IN, narrow, lambda r, c: r == c + position * narrow).astype(f32)
    halves = [highest(input_rows(ref), pick, contract_plain) for ref in (late_own, late_other)]
    input_ref[...] = both_halves(first, *halves)


def adam_kernel(
    index_ref, square_ref, expand_grad, project_grad, lanes_grad, early_grad, bias_grad, three_grad,
    input_own, packed_other, cot_ref, *refs,
):
    params, outs = refs[:30], refs[30:]
    narrow = cot_ref.shape[2]
    parts = packed_other[PACKED_ROWS : PACKED_ROWS + 16, :].astype(f32)
    other = (parts[0:1, 0:1] + parts[1:2, 0:1]) + parts[2:3, 0:1]
    total = square_ref[0:1, 0:1] + other + square_ref[8:9, 0:1]
    grad_norm = jnp.sqrt(total)
    factor = clip_limit / jnp.maximum(grad_norm, clip_limit)
    outs[31][...] = grad_norm
    groups = []
    for group in range(4):
        pick = one_hot(C_IN, narrow, lambda r, c: r == c + group * narrow).astype(bf16)
        groups.append(dot(packed_other[0:PACKED_ROWS, :], pick, contract_plain))
    crossed = jnp.concatenate(groups, axis=0).reshape(POSITIONS, 16, narrow)
    outs[0][...] = input_own[...] + crossed + cot_ref[...].astype(f32)
    pick = one_hot(C_IN, narrow, lambda r, c: r == c + index_ref[1] * narrow).astype(f32)
    gradients = (
        expand_grad[...],
        lanes_grad[32:34, :],
        lanes_grad[0:TAPS, :],
        lanes_grad[34:36, :],
        early_grad[0 : params[12].shape[0], :],
        bias_grad[:, 0 : params[15].shape[1]],
        early_grad[HIDDEN_ROWS : HIDDEN_ROWS + params[18].shape[0], :],
        early_grad[2 * HIDDEN_ROWS : 2 * HIDDEN_ROWS + 1, :],
        project_grad[...],
        highest(three_grad[0:2, :], pick, contract_plain),
    )
    for entry in range(10):
        gradient = gradients[entry] * factor
        first_new = params[3 * entry + 1][...] + (1.0 - beta_first) * gradient
        second_new = params[3 * entry + 2][...] + (1.0 - beta_second) * gradient * gradient
        first_hat = first_new / (1.0 - beta_first**STEP)
        second_hat = second_new / (1.0 - beta_second**STEP)
        step = first_hat / (jnp.sqrt(second_hat) + adam_epsilon)
        updated = (params[3 * entry][...] - step_rates[entry] * step, first_new, second_new)
        for part in range(3):
            outs[1 + 3 * entry + part][...] = updated[part]


def call(kernel, outs, operands, scratch=(), name=None, keep=True, place=True, after=(), plain=()):
    spaces = [
        pl.BlockSpec(memory_space=pltpu.SMEM)
        if operand.dtype == jnp.int32
        else pl.BlockSpec(memory_space=pltpu.VMEM)
        for operand in operands
    ]
    spaces += [pl.BlockSpec(memory_space=pltpu.VMEM)] * len(plain)
    spaces += [pl.BlockSpec(memory_space=pl.ANY)] * len(after)
    operands = [
        operand
        if operand.dtype == jnp.int32
        else pltpu.with_memory_space_constraint(operand, pltpu.VMEM if place else pltpu.HBM)
        for operand in operands
    ] + [pltpu.with_memory_space_constraint(operand, pltpu.HBM) for operand in (*plain, *after)]
    limit = 4 * 1024 * 1024 + sum(4 * math.prod(shape) for shape, _ in scratch)
    made = pltpu.VMEM if keep else jax.ShapeDtypeStruct
    return pl.pallas_call(
        kernel,
        out_shape=[
            (jax.ShapeDtypeStruct if out[2:] else made)(out[0], out[1]) for out in outs
        ],
        in_specs=spaces,
        out_specs=[pl.BlockSpec(memory_space=pltpu.VMEM)] * len(outs),
        scratch_shapes=[pltpu.VMEM(shape, dtype) for shape, dtype in scratch],
        compiler_params=pltpu.CompilerParams(vmem_limit_bytes=limit),
        name=name,
    )(*operands)


def on_device_paired(*arrays):
    block_input, cotangent = arrays[:2]
    segments = block_input.shape[3]
    if segments != 16:
        return on_device(*arrays)
    params = list(arrays[2:])
    for at in (15, 16, 17, 21, 22, 23):
        params[at] = params[at][None]
    for at in (24, 25, 26):
        params[at] = params[at].T
    (
        expand_weight, expand_gains, depth_weight, depth_gains, squeeze_weight,
        squeeze_bias, excite_weight, excite_bias, project_weight, project_gains,
    ) = params[::3]
    shards = lax.axis_size("dp")
    index = jnp.stack([lax.axis_index("dp"), lax.axis_index("chan")]).astype(jnp.int32)
    total_rows = float(POSITIONS * segments * shards)
    narrow = cotangent.shape[0]
    channels = expand_weight.shape[0]
    rows = POSITIONS * 8
    width = 2 * PAIR_LANES

    def swap(values, mask):
        return lax.ppermute(values, "chan", [(at, at ^ mask) for at in range(4)])

    input_rows = jnp.transpose(block_input, (1, 2, 3, 0)).reshape(POSITIONS, segments, C_IN)
    cot_rows = jnp.transpose(cotangent, (1, 2, 3, 0)).reshape(POSITIONS, segments, narrow)
    (copies,) = call(
        copies_kernel,
        [((shards, SENT_ROWS, 128), bf16)],
        [index, input_rows, cot_rows],
        name="copies",
        keep=False,
        place=False,
    )
    x = lax.all_to_all(copies, "dp", 0, 0)
    stack, matrix = call(
        pack_kernel,
        [((STACK_ROWS, channels), f32), ((2 * channels, C_IN), bf16)],
        [
            expand_weight, project_weight, depth_weight, squeeze_weight, excite_weight, excite_bias,
            expand_gains, depth_gains, project_gains,
        ],
        name="pack",
        keep=False,
        place=False,
    )
    stack_far, matrix_far = swap(stack, 2), swap(matrix, 2)
    pieces = [
        stack, swap(stack, 1), stack_far, swap(stack_far, 1),
        matrix, swap(matrix, 1), matrix_far, swap(matrix_far, 1),
    ]
    stack_all, project_all, gains_all = call(
        assemble_kernel,
        [((STACK_ROWS, width), f32), ((width, C_IN), bf16), ((2, C_IN), f32)],
        [index, *pieces],
        name="assemble",
        keep=False,
    )
    expanded, sums_one, expand_all, kept, sent = call(
        first_kernel,
        [
            ((shards, rows, width), f32),
            ((16, width), f32),
            ((width, C_IN), bf16),
            ((shards, PACKED_ROWS // 2, C_IN), bf16),
            ((shards, PACKED_ROWS // 2, C_IN), bf16),
        ],
        [index, *pieces[4:], x],
        name="first",
        after=[gains_all],
    )
    (cot,) = call(
        cot_kernel,
        [((shards, rows, C_IN), bf16)],
        [index, kept, swap(sent, 1), swap(kept, 2), swap(sent, 3)],
        name="cot",
    )
    bias_row = jnp.pad(squeeze_bias, ((0, 0), (0, HIDDEN_ROWS - squeeze_bias.shape[1])))

    depth, sums, norm_one = call(
        functools.partial(expand_kernel, total_rows),
        [((shards, rows, width), f32), ((16, width), f32), ((32, width), f32)],
        [expanded, sums_one, swap(sums_one, 1), stack_all],
        [((KS * PRODUCTS, 8, width), f32)],
        name="expand",
    )
    projected, scaled, sums, gate, before, pooled, norm_two, active = call(
        functools.partial(squeeze_kernel, total_rows),
        [
            ((shards, rows, C_IN), f32),
            ((shards, rows, width), bf16),
            ((32, C_IN), f32),
            ((shards * 8, width), f32),
            ((shards * 8, HIDDEN_ROWS), f32),
            ((shards * 8, width), f32),
            ((32, width), f32),
            ((shards, rows, width), f32),
        ],
        [depth, sums, swap(sums, 1), stack_all, project_all, cot, bias_row],
        name="squeeze",
    )
    two, sums, lanes_grad, three_grad = call(
        functools.partial(gate_back_kernel, total_rows),
        [
            ((shards, rows, PAIR_LANES), f32),
            ((16, PAIR_LANES), f32),
            ((KEEP_ROWS, PAIR_LANES + 128), f32),
            ((2, C_IN), f32),
        ],
        [
            index, projected, cot, sums, swap(sums, 1), gains_all, depth, norm_two, stack_all,
            project_all, gate, before, pooled, scaled, active, x,
        ],
        [
            ((shards, rows, C_IN), bf16),
            ((shards, rows, width), f32),
            ((shards * 8, width), f32),
            ((shards * 8, PAIR_LANES), f32),
        ],
        name="gate_back",
    )
    two_other, lanes_late = lax.optimization_barrier((swap(sums, 1), lanes_grad))
    lanes_other = swap(lanes_late, 1)
    one, sums, two_grad = call(
        functools.partial(depth_back_kernel, total_rows),
        [
            ((shards, rows, PAIR_LANES), f32),
            ((48, PAIR_LANES), f32),
            ((2, PAIR_LANES), f32),
        ],
        [
            index, sums, two_other, two, depth, expanded, stack_all, norm_one, norm_two,
        ],
        [
            ((KS * PRODUCTS, 8, PAIR_LANES), f32),
            ((KS * PRODUCTS, 8, PAIR_LANES), f32),
            ((24, PAIR_LANES), f32),
        ],
        name="depth_back",
    )
    sums_other = swap(sums, 1)
    late, one_grad = call(
        functools.partial(expand_back_kernel, total_rows),
        [((C_IN + LATE_ROWS, 512), f32), ((2, PAIR_LANES), f32)],
        [
            index, sums, sums_other, one, expanded, x, expand_all, stack_all, norm_one,
            lanes_other,
        ],
        [((shards, rows, PAIR_LANES), bf16)],
        name="expand_back",
    )
    late_pair = [late, swap(late, 1)]
    kernel_pair = [sums, sums_other]
    project_own, lanes_early, bias_own, block_output, square_early = call(
        early_kernel,
        [
            ((channels, C_IN), f32),
            ((2 * HIDDEN_ROWS + 8, channels), f32),
            ((1, HIDDEN_ROWS), f32),
            ((POSITIONS, segments, narrow), bf16, False),
            ((16, 128), f32),
        ],
        [index, lanes_late, lanes_other],
        name="early",
    )
    square, packed = call(
        settle_kernel,
        [((16, 128), f32), ((PACKED_ROWS + 16, C_IN), bf16)],
        [index, *late_pair, square_early, *kernel_pair, three_grad, two_grad, one_grad],
        name="settle",
    )
    expand_own, lanes_own, input_own, *scaled_params = call(
        own_kernel,
        [
            ((channels, C_IN), f32),
            ((40, channels), f32),
            ((POSITIONS, segments, narrow), f32),
            *[(value.shape, f32) for value in params],
        ],
        [index, *late_pair, *kernel_pair, two_grad, one_grad],
        name="own",
        plain=params,
    )
    updated = call(
        adam_kernel,
        [((POSITIONS, segments, narrow), f32)]
        + [(value.shape, f32) for value in params]
        + [((1, 1), f32)],
        [
            index, square, expand_own, project_own, lanes_own, lanes_early, bias_own, three_grad,
            input_own, swap(packed, 2), cot_rows, *scaled_params,
        ],
        name="adam",
        keep=False,
    )
    results = [block_output] + list(updated)
    for at in (0, 1):
        results[at] = jnp.transpose(results[at].reshape(HT, WD, segments, narrow), (3, 0, 1, 2))
    for at in (17, 18, 19, 23, 24, 25):
        results[at] = results[at][0]
    for at in (26, 27, 28):
        results[at] = results[at].T
    results[32] = results[32][0, 0]
    return tuple(results)


def solution(mesh):
    body = on_device_paired if paired_fits(mesh) else on_device
    return jax.shard_map(
        body,
        mesh=mesh,
        in_specs=(
            P(None, None, None, "dp"),
            P("chan", None, None, "dp"),
            P("chan", None),
            P("chan", None),
            P("chan", None),
            P(None, "chan"),
            P(None, "chan"),
            P(None, "chan"),
            P(None, "chan"),
            P(None, "chan"),
            P(None, "chan"),
            P(None, "chan"),
            P(None, "chan"),
            P(None, "chan"),
            P(None, "chan"),
            P(None, "chan"),
            P(None, "chan"),
            P(),
            P(),
            P(),
            P(None, "chan"),
            P(None, "chan"),
            P(None, "chan"),
            P("chan"),
            P("chan"),
            P("chan"),
            P(None, "chan"),
            P(None, "chan"),
            P(None, "chan"),
            P(None, "chan"),
            P(None, "chan"),
            P(None, "chan"),
        ),
        out_specs=(
            P("chan", None, None, "dp"),
            P("chan", None, None, "dp"),
            P("chan", None),
            P("chan", None),
            P("chan", None),
            P(None, "chan"),
            P(None, "chan"),
            P(None, "chan"),
            P(None, "chan"),
            P(None, "chan"),
            P(None, "chan"),
            P(None, "chan"),
            P(None, "chan"),
            P(None, "chan"),
            P(None, "chan"),
            P(None, "chan"),
            P(None, "chan"),
            P(),
            P(),
            P(),
            P(None, "chan"),
            P(None, "chan"),
            P(None, "chan"),
            P("chan"),
            P("chan"),
            P("chan"),
            P(None, "chan"),
            P(None, "chan"),
            P(None, "chan"),
            P(None, "chan"),
            P(None, "chan"),
            P(None, "chan"),
            P(),
        ),
        check_vma=False,
    )
```
